32 devices in a mesh: grp: 8 (over z, core), exp: 4 (over y, x).
Axes of the slice: x: 2, y: 2, z: 4, core: 2. Of those that a mesh axis runs over, the one named last changes fastest.
Arguments:
- hidden: bfloat16 [8, 16, 7168], P('grp', 'exp'), may hold values from -6 to 6
- norm_gain: float32 [7168], replicated, may hold values from 0.1 to 1.9
- route: int32 [8, 16, 1], P('grp', 'exp'), may hold values from 0 to 1; in each aligned block of 4 rows (0 to 3, 4 to 7, ..., all dimensions but the last counted through in order) at most 3 rows name the same one
- route_weight: float32 [8, 16], P('grp', 'exp'), may hold values from 0.2 to 1
- resident: bfloat16 [2, 2048, 7168], P(None, 'exp'), may hold values from -0.0625 to 0.0625
- sectioned: bfloat16 [8, 512, 7168], P('grp', 'exp'), may hold values from -0.1875 to 0.1875
- owner: int32 [8], replicated, may hold values from 0 to 7, each once
Outputs:
- moe_out: bfloat16 [8, 16, 7168], P('grp', 'exp')
The draws below stay inside these ranges and needn't reach their ends.
Inputs may be any that keep to these rules, and one draw needn't show every extreme that they name: `route`: each row names one of the 2 experts. Among the 4 rows of one device at most 3 name the same expert, and in every draw some device has exactly 3 rows naming one expert. Every group number appears exactly once, so the 4 buckets have distinct owner groups.
All inputs are finite; a program needn't handle non-finite values.
Results may differ from the reference program's by a relative error of at most 0.0071.
Values may be sent and summed in bfloat16 or wider, within the bound.
No kernel may reach another device: no remote copies, remote signals or barrier semaphores. Data moves between devices by JAX's collectives and lax.ppermute only.
A program may use at most 64 MiB of HBM per device.

```python
import math
import jax
import jax.numpy as jnp
import numpy as np
from jax import lax

D = 7168
FF_WIN = 1024
E_WIN = 2
BUCKETS = 4
ROWS_DEV = 4
CAP = 3
ROWS = 16
UNITS = 512
FB = 128
N_GRP = 8
N_EXP = 4


def shard_levels(own_key, shape, pieces, smallest, largest):
    loudness, own = 1.0, jax.random.fold_in(own_key, 6)
    for position, parts in pieces:
        steps = jnp.exp(jax.random.uniform(jax.random.fold_in(own, position), (parts,), jnp.float32, smallest / len(pieces), largest / len(pieces)))
        loudness = loudness * jnp.repeat(steps, shape[position] // parts).reshape([-1 if axis == position else 1 for axis in range(len(shape))])
    return loudness


def shared_out(stream_key, own, number, rows, amount, top, bound, skew):
    sequence = jax.random.permutation(stream_key, amount)
    packed, ordinary = shares(amount, rows * top, bound, skew, True), shares(amount, rows * top, bound, skew, False)
    places = jnp.arange(amount)

    def named(lengths, rotation):
        used = int((lengths > 0).sum())
        fixed = max(1, used // 4)
        passed = fixed + (places - fixed + rotation * (used - fixed)) % max(1, amount - fixed)
        return jnp.zeros((amount,), jnp.int32).at[sequence[jnp.where(places < fixed, places, passed)]].set(jnp.asarray(lengths, jnp.int32))

    lengths = jnp.where(number % 4 == 0, named(packed, number // 4), named(ordinary, number - number // 4 - 1))
    mixed = jax.random.permutation(jax.random.fold_in(own, 3), amount)
    source_of, sink = mixed[0:amount // 2 * 2:2], mixed[1:amount // 2 * 2:2]
    margin = jnp.minimum(lengths[source_of] - 1, bound - lengths[sink]) // 2
    margin = jnp.where((source_of == sequence[0]) | (sink == sequence[0]) | (lengths[sink] == 0), 0, jnp.maximum(margin, 0))
    passed = jax.random.randint(jax.random.fold_in(own, 4), (amount // 2,), 0, 1 << 20) % (margin + 1)
    lengths = lengths.at[source_of].add(-passed).at[sink].add(passed)
    members = jnp.searchsorted(jnp.cumsum(lengths), jnp.arange(rows * top), side="right").astype(jnp.int32)
    listing = members.reshape(top, rows).T
    listing = listing[jax.random.permutation(jax.random.fold_in(own, 1), rows)]
    rotation = jax.random.randint(jax.random.fold_in(own, 2), (rows, 1), 0, top)
    return jnp.take_along_axis(listing, (jnp.arange(top)[None, :] + rotation) % top, axis=1)


def shares(amount, total, bound, skew, full):
    loads = [(1 << 20) // math.isqrt(rank ** skew) + 1 for rank in range(1, amount + 1)]
    largest = bound if full else min(bound, max(-(-total // amount), total * loads[0] // sum(loads)))
    least = 1 if total - largest >= amount - 1 else 0
    counts, surplus = [largest] + [least] * (amount - 1), total - largest - least * (amount - 1)
    while surplus > 0:
        candidates = [i for i in range(1, amount) if counts[i] < largest] or [i for i in range(1, amount) if counts[i] < bound]
        whole, budget = sum([loads[i] for i in candidates]), surplus
        for i in candidates:
            extra = min(bound - counts[i], max(1, budget * loads[i] // whole), surplus)
            counts[i] = counts[i] + extra
            surplus = surplus - extra
    return np.array(counts)


def normal_values(key, dims, scale, bound, cuts=(), held_as=jnp.bfloat16):
    values = jax.random.normal(key, dims, jnp.float32) * scale
    if len(cuts) > 0:
        values = shard_levels(key, dims, cuts, -0.22, 0.18) * values
    return jnp.clip(values, min=-bound, max=bound).astype(held_as)


def setup_inputs(seed: int = 0) -> dict:
    streams_of = jax.random.split(jax.random.key(seed), 8)
    hidden = normal_values(streams_of[0], (N_GRP, ROWS, D), 1.0, 6.0, ((0, 8), (1, 4)))
    norm_gain = jnp.clip(1.0 + 0.18 * jax.random.normal(streams_of[1], (D,), jnp.float32), 0.1, 1.9)
    route_keys = jax.random.split(jax.random.fold_in(streams_of[2], 1), N_GRP * ROWS // ROWS_DEV)
    route_turns = jax.random.permutation(jax.random.fold_in(streams_of[2], 3), N_GRP * ROWS // ROWS_DEV)
    route = jax.vmap(lambda own, number: shared_out(jax.random.fold_in(streams_of[2], 2), own, number, ROWS_DEV, E_WIN, 1, CAP, 0))(route_keys, route_turns).reshape((N_GRP, ROWS, 1))
    route_weight = jnp.clip(0.2 + 0.8 * jax.random.uniform(streams_of[3], (N_GRP, ROWS), jnp.float32) ** shard_levels(streams_of[3], (N_GRP, ROWS), ((0, 8), (1, 4)), -0.2, 0.2), 0.2, 1.0)
    resident = normal_values(streams_of[4], (2, N_EXP * BUCKETS * FB, D), D ** -0.5, 0.0625, ((1, 4),))
    sectioned = normal_values(streams_of[5], (N_GRP, UNITS, D), FF_WIN ** -0.5, 0.1875, ((0, 8), (1, 4)))
    owner = jax.random.permutation(streams_of[6], N_GRP).astype(jnp.int32)
    return dict(hidden=hidden, norm_gain=norm_gain, route=route, route_weight=route_weight, resident=resident, sectioned=sectioned, owner=owner)


epsilon = 1e-06

def reference(hidden, norm_gain, route, route_weight, resident, sectioned, owner):
    live = sectioned[owner[:BUCKETS]]
    down_blocks = live.reshape(BUCKETS, N_EXP, FB, D)
    down_blocks = jnp.transpose(down_blocks, (1, 0, 2, 3)).reshape(N_EXP, BUCKETS * FB, D)
    gate_blocks = jnp.transpose(resident.reshape(2, N_EXP, BUCKETS * FB, D), (1, 0, 2, 3))
    row_data = hidden.reshape(-1, D).astype(jnp.float32)
    scale = lax.rsqrt(lax.optimization_barrier(jnp.mean(row_data * row_data, axis=1, keepdims=True)) + epsilon)
    normed = (row_data * scale * norm_gain[None, :]).astype(jnp.bfloat16)
    expert_ids = route.reshape(-1)
    shards = N_EXP // E_WIN

    def accumulate(running, inputs):
        gate_up, down_rows, device = inputs
        gate_part = lax.dot_general(normed, gate_up[0], (((1,), (1,)), ((), ())), preferred_element_type=jnp.float32)
        up_part = lax.dot_general(normed, gate_up[1], (((1,), (1,)), ((), ())), preferred_element_type=jnp.float32)
        activation = (jax.nn.silu(gate_part) * up_part).astype(jnp.bfloat16)
        partial_value = jnp.dot(activation, down_rows, preferred_element_type=jnp.float32).astype(jnp.bfloat16)
        partial_value = lax.optimization_barrier(partial_value).astype(jnp.float32)
        chosen = (expert_ids == device // shards)[:, None]
        return (running + jnp.where(chosen, partial_value, jnp.zeros_like(partial_value)), None)
    start = jnp.zeros((normed.shape[0], D), jnp.float32)
    running, _ = lax.scan(accumulate, start, (gate_blocks, down_blocks, jnp.arange(N_EXP, dtype=jnp.int32)))
    result = (running * route_weight.reshape(-1, 1)).astype(jnp.bfloat16)
    return result.reshape(N_GRP, -1, D)
```

```python
import jax
import jax.numpy as jnp
from jax import lax
from jax.sharding import PartitionSpec as P

E_WIN = 2
BUCKETS = 4
CAP = 3
PAIR = 2


epsilon = 1e-06


def from_root(value, axis, source):
    kept = jnp.where(lax.axis_index(axis) == source, value, 0).astype(value.dtype)
    return lax.psum(kept, axis)


def activate(slot_rows, gate_up):
    gate_part = lax.dot_general(
        slot_rows, gate_up[0], (((1,), (1,)), ((), ())), preferred_element_type=jnp.float32
    )
    up_part = lax.dot_general(
        slot_rows, gate_up[1], (((1,), (1,)), ((), ())), preferred_element_type=jnp.float32
    )
    return (jax.nn.silu(gate_part) * up_part).astype(jnp.bfloat16)


def normalize(rows, norm_gain):
    row_data = rows.astype(jnp.float32)
    scale = lax.rsqrt(jnp.mean(row_data * row_data, axis=1, keepdims=True) + epsilon)
    return (row_data * scale * norm_gain[None, :]).astype(jnp.bfloat16)


def move_weights(hidden, norm_gain, route, route_weight, resident, sectioned, owner):
    normed = normalize(hidden[0], norm_gain)
    row_count, width = normed.shape
    devices = lax.axis_size("exp")
    shards = devices // E_WIN
    expert_ids = route[0, :, 0]
    onehot = (expert_ids[:, None] == jnp.arange(E_WIN, dtype=jnp.int32)[None, :]).astype(jnp.int32)
    position = jnp.cumsum(onehot, axis=0) - onehot
    slot_index = jnp.sum(position * onehot, axis=1)
    placing = onehot[:, :, None] * (
        slot_index[:, None, None] == jnp.arange(CAP, dtype=jnp.int32)[None, None, :]
    ).astype(jnp.int32)
    placing = placing.reshape(row_count, E_WIN * CAP)
    packed = jnp.dot(
        placing.astype(jnp.bfloat16).T, normed, preferred_element_type=jnp.float32
    ).astype(jnp.bfloat16)
    packed = packed.reshape(E_WIN, 1, CAP, width)
    outgoing = jnp.broadcast_to(packed, (E_WIN, shards, CAP, width)).reshape(devices, CAP, width)
    piece_rows = sectioned.shape[1]
    arrived = lax.all_to_all(outgoing, "exp", split_axis=0, concat_axis=0, tiled=True)
    flat_slots = arrived.reshape(-1, width)
    activation = activate(flat_slots, resident)
    running_sum = jnp.zeros((flat_slots.shape[0], width), jnp.float32)
    for bucket in range(BUCKETS):
        weight_piece = from_root(sectioned[0], "grp", owner[bucket])
        act_piece = activation[:, bucket * piece_rows : (bucket + 1) * piece_rows]
        running_sum = running_sum + jnp.dot(
            act_piece, weight_piece, preferred_element_type=jnp.float32
        )
    partials = running_sum.astype(jnp.bfloat16).reshape(arrived.shape)
    returned = lax.all_to_all(partials, "exp", split_axis=0, concat_axis=0, tiled=True)
    summed = jnp.sum(returned.astype(jnp.float32).reshape(E_WIN, shards, CAP, width), axis=1)
    summed = summed.reshape(E_WIN * CAP, width)
    combined = jnp.dot(placing.astype(jnp.float32), summed, precision=lax.Precision.HIGHEST)
    result = (combined * route_weight[0][:, None]).astype(jnp.bfloat16)
    return result.reshape(1, row_count, width)


def swap(value, axis, bits):
    size = lax.axis_size(axis)
    return lax.ppermute(value, axis, [(i, i ^ bits) for i in range(size)])


def move_rows(hidden, norm_gain, route, route_weight, resident, sectioned, owner):
    rows = hidden[0]
    row_count, width = rows.shape
    devices = lax.axis_size("exp")
    chips = lax.axis_size("grp") // PAIR
    shards = devices // E_WIN
    me, group = lax.axis_index("exp"), lax.axis_index("grp")
    piece = sectioned.shape[1]
    own_piece = sectioned[0]
    other_piece = swap(own_piece, "grp", 1)
    arrived = []
    for bits in range(devices):
        expert = (me ^ bits) // shards
        kept = jnp.where(route[0] == expert, rows, 0).astype(rows.dtype)
        arrived.append(swap(kept, "exp", bits) if bits else kept)
    normed = normalize(jnp.concatenate(arrived, axis=0), norm_gain)
    activation = activate(normed, resident)
    along = [activation] + [swap(activation, "grp", PAIR * hop) for hop in range(1, chips)]
    acts = jnp.stack(along).reshape(chips, devices, row_count, BUCKETS, piece)
    acts = jnp.transpose(acts, (1, 0, 2, 3, 4)).reshape(-1, BUCKETS, piece)
    partial = 0.0
    for held_by, weights in ((group, own_piece), (group ^ 1, other_piece)):
        mine = (owner[:BUCKETS] == held_by)[None, :, None]
        picked = jnp.sum(jnp.where(mine, acts, 0).astype(jnp.float32), axis=1).astype(jnp.bfloat16)
        partial = partial + jnp.dot(picked, weights, preferred_element_type=jnp.float32)
    partial = partial.astype(jnp.bfloat16).reshape(devices, chips * row_count, width)
    total = partial[0].astype(jnp.float32)
    for bits in range(1, devices):
        total = total + swap(partial[bits], "exp", bits).astype(jnp.float32)
    total = total.astype(jnp.bfloat16).reshape(chips, row_count, width)
    combined = total[0].astype(jnp.float32)
    for hop in range(1, chips):
        combined = combined + swap(total[hop], "grp", PAIR * hop).astype(jnp.float32)
    result = (combined * route_weight[0][:, None]).astype(jnp.bfloat16)
    return result.reshape(1, row_count, width)


def per_device(hidden, norm_gain, route, route_weight, resident, sectioned, owner):
    weight_rows = BUCKETS * sectioned.shape[1]
    partial_rows = lax.axis_size("exp") * lax.axis_size("grp") // PAIR * hidden.shape[1]
    plan = move_rows if partial_rows < weight_rows else move_weights
    return plan(hidden, norm_gain, route, route_weight, resident, sectioned, owner)


def solution(mesh):
    in_specs = (
        P("grp", "exp", None),
        P(),
        P("grp", "exp", None),
        P("grp", "exp"),
        P(None, "exp", None),
        P("grp", "exp", None),
        P(),
    )
    out_specs = P("grp", "exp", None)
    return jax.shard_map(
        per_device, mesh=mesh, in_specs=in_specs, out_specs=out_specs, check_vma=False
    )
```

```python
import functools

import jax
import jax.numpy as jnp
from jax import lax
from jax.experimental import pallas as pl
from jax.experimental.pallas import tpu as pltpu
from jax.sharding import PartitionSpec as P

E_WIN = 2
BUCKETS = 4
CAP = 3
PAIR = 2


epsilon = 1e-06


def from_root(value, axis, source):
    kept = jnp.where(lax.axis_index(axis) == source, value, 0).astype(value.dtype)
    return lax.psum(kept, axis)


def activate(slot_rows, gate_up):
    gate_part = lax.dot_general(
        slot_rows, gate_up[0], (((1,), (1,)), ((), ())), preferred_element_type=jnp.float32
    )
    up_part = lax.dot_general(
        slot_rows, gate_up[1], (((1,), (1,)), ((), ())), preferred_element_type=jnp.float32
    )
    return (jax.nn.silu(gate_part) * up_part).astype(jnp.bfloat16)


def normalize(rows, norm_gain):
    row_data = rows.astype(jnp.float32)
    scale = lax.rsqrt(jnp.mean(row_data * row_data, axis=1, keepdims=True) + epsilon)
    return (row_data * scale * norm_gain[None, :]).astype(jnp.bfloat16)


def move_weights(hidden, norm_gain, route, route_weight, resident, sectioned, owner):
    normed = normalize(hidden[0], norm_gain)
    row_count, width = normed.shape
    devices = lax.axis_size("exp")
    shards = devices // E_WIN
    expert_ids = route[0, :, 0]
    onehot = (expert_ids[:, None] == jnp.arange(E_WIN, dtype=jnp.int32)[None, :]).astype(jnp.int32)
    position = jnp.cumsum(onehot, axis=0) - onehot
    slot_index = jnp.sum(position * onehot, axis=1)
    placing = onehot[:, :, None] * (
        slot_index[:, None, None] == jnp.arange(CAP, dtype=jnp.int32)[None, None, :]
    ).astype(jnp.int32)
    placing = placing.reshape(row_count, E_WIN * CAP)
    packed = jnp.dot(
        placing.astype(jnp.bfloat16).T, normed, preferred_element_type=jnp.float32
    ).astype(jnp.bfloat16)
    packed = packed.reshape(E_WIN, 1, CAP, width)
    outgoing = jnp.broadcast_to(packed, (E_WIN, shards, CAP, width)).reshape(devices, CAP, width)
    piece_rows = sectioned.shape[1]
    arrived = lax.all_to_all(outgoing, "exp", split_axis=0, concat_axis=0, tiled=True)
    flat_slots = arrived.reshape(-1, width)
    activation = activate(flat_slots, resident)
    running_sum = jnp.zeros((flat_slots.shape[0], width), jnp.float32)
    for bucket in range(BUCKETS):
        weight_piece = from_root(sectioned[0], "grp", owner[bucket])
        act_piece = activation[:, bucket * piece_rows : (bucket + 1) * piece_rows]
        running_sum = running_sum + jnp.dot(
            act_piece, weight_piece, preferred_element_type=jnp.float32
        )
    partials = running_sum.astype(jnp.bfloat16).reshape(arrived.shape)
    returned = lax.all_to_all(partials, "exp", split_axis=0, concat_axis=0, tiled=True)
    summed = jnp.sum(returned.astype(jnp.float32).reshape(E_WIN, shards, CAP, width), axis=1)
    summed = summed.reshape(E_WIN * CAP, width)
    combined = jnp.dot(placing.astype(jnp.float32), summed, precision=lax.Precision.HIGHEST)
    result = (combined * route_weight[0][:, None]).astype(jnp.bfloat16)
    return result.reshape(1, row_count, width)


def swap(value, axis, bits):
    size = lax.axis_size(axis)
    return lax.ppermute(value, axis, [(i, i ^ bits) for i in range(size)])


NT = (((1,), (1,)), ((), ()))
VMEM = pl.BlockSpec(memory_space=pltpu.VMEM)
SMEM = pl.BlockSpec(memory_space=pltpu.SMEM)
ANY = pl.BlockSpec(memory_space=pl.ANY)


def pack_body(chips, shards, gain_ref, *refs):
    rows, routes, blocks, line = refs[:chips], refs[chips : 2 * chips], refs[2 * chips : -1], refs[-1]
    row_count, width = rows[0].shape
    half = width // 2
    block = 2 * CAP * chips
    height = E_WIN * block
    mine = lax.axis_index("exp") // shards
    at = lax.broadcasted_iota(jnp.int32, (height, row_count), 0)
    at_expert, at_slot = at // block, (at % block) // (2 * chips)
    at_half, at_chip = (at % (2 * chips)) // chips, at % chips
    total = jnp.zeros((height, half), jnp.float32)
    for chip in range(chips):
        line[...] = jnp.full(line.shape, -1, jnp.int32)
        line[0:1, 0:row_count] = routes[chip][...]
        named = line[...]
        position = jnp.zeros(named.shape, jnp.int32)
        for back in range(1, row_count):
            position = position + (named == pltpu.roll(named, back, 1)).astype(jnp.int32)
        named, position = named[0:1, 0:row_count], position[0:1, 0:row_count]
        wanted = (at_chip == chip) & (at_slot == position) & ((mine ^ at_expert) == named)
        for part in range(2):
            placing = jnp.where(wanted & (at_half == part), 1.0, 0.0).astype(jnp.bfloat16)
            total = total + jnp.dot(
                placing,
                rows[chip][:, part * half : (part + 1) * half],
                preferred_element_type=jnp.float32,
            )
    squares = jnp.broadcast_to(jnp.sum(total * total, axis=1, keepdims=True), (height, 128))
    first = (lax.broadcasted_iota(jnp.int32, (height, 128), 0) % (2 * chips)) < chips
    partner = jnp.where(first, pltpu.roll(squares, height - chips, 0), pltpu.roll(squares, chips, 0))
    scale = lax.rsqrt((squares + partner) * (1.0 / width) + epsilon)[:, 0:1]
    upper = (lax.broadcasted_iota(jnp.int32, (height, half), 0) % (2 * chips)) < chips
    gain = jnp.where(upper, gain_ref[:, :half], gain_ref[:, half:])
    normed = total * scale * gain
    for expert in range(E_WIN):
        blocks[expert][...] = normed[expert * block : (expert + 1) * block].astype(jnp.bfloat16)


def fetch_body(piece, owner_ref, resident, own, other, after, both, down, held, sems):
    group = lax.axis_index("grp")
    copies = []
    for which, holder in enumerate((group, group ^ 1)):
        bucket, has = jnp.int32(0), jnp.int32(0)
        for index in range(BUCKETS):
            hit = owner_ref[index] == holder
            bucket, has = jnp.where(hit, index, bucket), jnp.where(hit, 1, has)
        here = pl.ds(which * piece, piece)
        for part in range(2):
            copies.append(
                pltpu.make_async_copy(
                    resident.at[part, pl.ds(pl.multiple_of(bucket * piece, piece), piece)],
                    both.at[part, here],
                    sems.at[3 * which + part],
                )
            )
        copies.append(
            pltpu.make_async_copy((own, other)[which], down.at[here], sems.at[3 * which + 2])
        )
        held[here, :] = jnp.broadcast_to(has.astype(jnp.float32), (piece, held.shape[1]))
    for copy in copies:
        copy.start()
    for copy in copies:
        copy.wait()


def expert_body(devices, chips, lanes, both, down, held, *refs):
    blocks, partials, stacked = refs[:devices], refs[devices : 2 * devices], refs[-1]
    block, half = blocks[0].shape
    used = devices * block
    for index in range(devices):
        stacked[index * block : (index + 1) * block, :] = blocks[index][...]
    if lanes > used:
        stacked[used:, :] = jnp.zeros((lanes - used, half), jnp.bfloat16)
    sums = []
    for part in range(2):
        upper = lax.dot_general(
            both[part, :, :half], stacked[...], NT, preferred_element_type=jnp.float32
        )
        lower = lax.dot_general(
            both[part, :, half:], stacked[...], NT, preferred_element_type=jnp.float32
        )
        sums.append(upper + pltpu.roll(lower, lanes - chips, 1))
    column = lax.broadcasted_iota(jnp.int32, sums[0].shape, 1)
    valid = ((column % (2 * chips)) < chips) & (column < used)
    act = sums[0] * jax.nn.sigmoid(sums[0]) * sums[1]
    act = jnp.where(valid & (held[...] > 0.5), act, 0.0)
    above = act.T.astype(jnp.bfloat16)[:used]
    below = pltpu.roll(act, chips, 1).T.astype(jnp.bfloat16)[:used]
    step = half // 7 if half % (7 * 128) == 0 else half
    for start in range(0, half, step):
        out = jnp.dot(above, down[:, start : start + step], preferred_element_type=jnp.float32)
        out = out + jnp.dot(
            below, down[:, half + start : half + start + step], preferred_element_type=jnp.float32
        )
        for index in range(devices):
            partials[index][:, start : start + step] = out[
                index * block : (index + 1) * block
            ].astype(jnp.bfloat16)


def combine_body(devices, chips, shards, placing, *refs):
    blocks, outs = refs[:devices], refs[devices:]
    half = blocks[0].shape[1]
    row_count = outs[0].shape[0]
    for part in range(2):
        total = 0.0
        for index in range(devices):
            total = total + jnp.dot(
                placing[2 * (index // shards) + part],
                blocks[index][...],
                preferred_element_type=jnp.float32,
            )
        for chip in range(chips):
            outs[chip][:, part * half : (part + 1) * half] = total[
                chip * row_count : (chip + 1) * row_count
            ].astype(outs[chip].dtype)


def move_rows(hidden, norm_gain, route, route_weight, resident, sectioned, owner):
    rows = hidden[0]
    row_count, width = rows.shape
    devices = lax.axis_size("exp")
    chips = lax.axis_size("grp") // PAIR
    shards = devices // E_WIN
    half, block = width // 2, 2 * CAP * chips
    piece = sectioned.shape[1]
    mine = lax.axis_index("exp") // shards
    routes = [route[0].reshape(1, row_count)]
    gathered = [rows]
    for hop in range(1, chips):
        gathered.append(swap(rows, "grp", PAIR * hop))
    for hop in range(1, chips):
        routes.append(swap(routes[0], "grp", PAIR * hop))
    other_piece = swap(sectioned[0], "grp", 1)
    half_block = jax.ShapeDtypeStruct((block, half), jnp.bfloat16)
    packed = pl.pallas_call(
        functools.partial(pack_body, chips, shards),
        out_shape=[half_block] * E_WIN,
        in_specs=[VMEM] * (1 + 2 * chips),
        out_specs=[VMEM] * E_WIN,
        scratch_shapes=[pltpu.VMEM((8, 128), jnp.int32)],
        name="pack",
    )(norm_gain.reshape(1, width), *gathered, *routes)
    blocks = [packed[bits // shards] for bits in range(devices)]
    blocks = [blocks[0]] + [swap(blocks[bits], "exp", bits) for bits in range(1, devices)]
    both, down, held = pl.pallas_call(
        functools.partial(fetch_body, piece),
        out_shape=[
            jax.ShapeDtypeStruct((2, PAIR * piece, width), jnp.bfloat16),
            jax.ShapeDtypeStruct((PAIR * piece, width), jnp.bfloat16),
            jax.ShapeDtypeStruct((PAIR * piece, 128), jnp.float32),
        ],
        in_specs=[SMEM, ANY, ANY, ANY, ANY],
        out_specs=[VMEM] * 3,
        scratch_shapes=[pltpu.SemaphoreType.DMA((3 * PAIR,))],
        name="fetch",
    )(owner, resident, sectioned[0], other_piece, packed[0])
    named = jnp.concatenate(routes, axis=0)
    seen = [
        sum([(named[:, r] == named[:, b]).astype(jnp.int32) for b in range(r)], jnp.zeros((chips,), jnp.int32))
        for r in range(row_count)
    ]
    position = jnp.stack(seen, axis=1)
    chip_of = jnp.arange(chips, dtype=jnp.int32)[:, None]
    column = jnp.arange(block, dtype=jnp.int32)[None, None, :]
    placing = []
    for expert in range(E_WIN):
        for part in range(2):
            target = (position * 2 + part) * chips + chip_of
            chosen = (named == (mine ^ expert))[:, :, None] & (column == target[:, :, None])
            placing.append(chosen.astype(jnp.bfloat16).reshape(chips * row_count, block))
    placing = jnp.stack(placing)
    lanes = -(-devices * block // 128) * 128
    partials = pl.pallas_call(
        functools.partial(expert_body, devices, chips, lanes),
        out_shape=[half_block] * devices,
        in_specs=[VMEM] * (3 + devices),
        out_specs=[VMEM] * devices,
        scratch_shapes=[pltpu.VMEM((lanes, half), jnp.bfloat16)],
        name="expert",
    )(both, down, held, *blocks)
    returned = [partials[0]] + [swap(partials[bits], "exp", bits) for bits in range(1, devices)]
    home = jax.ShapeDtypeStruct((row_count, width), jnp.bfloat16)
    sums = pl.pallas_call(
        functools.partial(combine_body, devices, chips, shards),
        out_shape=[home] * chips,
        in_specs=[VMEM] * (1 + devices),
        out_specs=[VMEM] * chips,
        name="combine",
    )(placing, *returned)
    combined = sums[0].astype(jnp.float32)
    for hop in range(1, chips):
        combined = combined + swap(sums[hop], "grp", PAIR * hop).astype(jnp.float32)
    result = (combined * route_weight[0][:, None]).astype(jnp.bfloat16)
    return result.reshape(1, row_count, width)


def per_device(hidden, norm_gain, route, route_weight, resident, sectioned, owner):
    weight_rows = BUCKETS * sectioned.shape[1]
    partial_rows = lax.axis_size("exp") * lax.axis_size("grp") // PAIR * hidden.shape[1]
    plan = move_rows if partial_rows < weight_rows else move_weights
    return plan(hidden, norm_gain, route, route_weight, resident, sectioned, owner)


def solution(mesh):
    in_specs = (
        P("grp", "exp", None),
        P(),
        P("grp", "exp", None),
        P("grp", "exp"),
        P(None, "exp", None),
        P("grp", "exp", None),
        P(),
    )
    out_specs = P("grp", "exp", None)
    return jax.shard_map(
        per_device, mesh=mesh, in_specs=in_specs, out_specs=out_specs, check_vma=False
    )
```

```python
import functools

import jax
import jax.numpy as jnp
from jax import lax
from jax.experimental import pallas as pl
from jax.experimental.pallas import tpu as pltpu
from jax.sharding import PartitionSpec as P

E_WIN = 2
BUCKETS = 4
CAP = 3
PAIR = 2


epsilon = 1e-06


def from_root(value, axis, source):
    kept = jnp.where(lax.axis_index(axis) == source, value, 0).astype(value.dtype)
    return lax.psum(kept, axis)


def activate(slot_rows, gate_up):
    gate_part = lax.dot_general(
        slot_rows, gate_up[0], (((1,), (1,)), ((), ())), preferred_element_type=jnp.float32
    )
    up_part = lax.dot_general(
        slot_rows, gate_up[1], (((1,), (1,)), ((), ())), preferred_element_type=jnp.float32
    )
    return (jax.nn.silu(gate_part) * up_part).astype(jnp.bfloat16)


def normalize(rows, norm_gain):
    row_data = rows.astype(jnp.float32)
    scale = lax.rsqrt(jnp.mean(row_data * row_data, axis=1, keepdims=True) + epsilon)
    return (row_data * scale * norm_gain[None, :]).astype(jnp.bfloat16)


def move_weights(hidden, norm_gain, route, route_weight, resident, sectioned, owner):
    normed = normalize(hidden[0], norm_gain)
    row_count, width = normed.shape
    devices = lax.axis_size("exp")
    shards = devices // E_WIN
    expert_ids = route[0, :, 0]
    onehot = (expert_ids[:, None] == jnp.arange(E_WIN, dtype=jnp.int32)[None, :]).astype(jnp.int32)
    position = jnp.cumsum(onehot, axis=0) - onehot
    slot_index = jnp.sum(position * onehot, axis=1)
    placing = onehot[:, :, None] * (
        slot_index[:, None, None] == jnp.arange(CAP, dtype=jnp.int32)[None, None, :]
    ).astype(jnp.int32)
    placing = placing.reshape(row_count, E_WIN * CAP)
    packed = jnp.dot(
        placing.astype(jnp.bfloat16).T, normed, preferred_element_type=jnp.float32
    ).astype(jnp.bfloat16)
    packed = packed.reshape(E_WIN, 1, CAP, width)
    outgoing = jnp.broadcast_to(packed, (E_WIN, shards, CAP, width)).reshape(devices, CAP, width)
    piece_rows = sectioned.shape[1]
    arrived = lax.all_to_all(outgoing, "exp", split_axis=0, concat_axis=0, tiled=True)
    flat_slots = arrived.reshape(-1, width)
    activation = activate(flat_slots, resident)
    running_sum = jnp.zeros((flat_slots.shape[0], width), jnp.float32)
    for bucket in range(BUCKETS):
        weight_piece = from_root(sectioned[0], "grp", owner[bucket])
        act_piece = activation[:, bucket * piece_rows : (bucket + 1) * piece_rows]
        running_sum = running_sum + jnp.dot(
            act_piece, weight_piece, preferred_element_type=jnp.float32
        )
    partials = running_sum.astype(jnp.bfloat16).reshape(arrived.shape)
    returned = lax.all_to_all(partials, "exp", split_axis=0, concat_axis=0, tiled=True)
    summed = jnp.sum(returned.astype(jnp.float32).reshape(E_WIN, shards, CAP, width), axis=1)
    summed = summed.reshape(E_WIN * CAP, width)
    combined = jnp.dot(placing.astype(jnp.float32), summed, precision=lax.Precision.HIGHEST)
    result = (combined * route_weight[0][:, None]).astype(jnp.bfloat16)
    return result.reshape(1, row_count, width)


def swap(value, axis, bits):
    size = lax.axis_size(axis)
    return lax.ppermute(value, axis, [(i, i ^ bits) for i in range(size)])


NT = (((1,), (1,)), ((), ()))
VMEM = pl.BlockSpec(memory_space=pltpu.VMEM)
SMEM = pl.BlockSpec(memory_space=pltpu.SMEM)
ANY = pl.BlockSpec(memory_space=pl.ANY)
HBM = pl.BlockSpec(memory_space=pltpu.HBM)
CODE = 128
MIB = 1 << 20


def held(*values):
    return [pltpu.with_memory_space_constraint(value, pltpu.VMEM) for value in values]


def limit(mib):
    return pltpu.CompilerParams(vmem_limit_bytes=mib * MIB)


def prepare_body(route_ref, rows_ref, gain_ref, out_ref):
    row_count, width = rows_ref.shape
    rows = rows_ref[...].astype(jnp.float32)
    scale = lax.rsqrt(jnp.sum(rows * rows, axis=1, keepdims=True) * (1.0 / width) + epsilon)
    out_ref[:, :width] = (rows * scale * gain_ref[...]).astype(jnp.bfloat16)
    named = [route_ref[row] for row in range(row_count)]
    at = lax.broadcasted_iota(jnp.int32, (row_count, CODE), 0)
    code = jnp.zeros((row_count, CODE), jnp.int32)
    for row in range(row_count):
        slot = jnp.int32(0)
        for before in range(row):
            slot = slot + jnp.where(named[before] == named[row], 1, 0)
        code = jnp.where(at == row, named[row] * row_count + slot, code)
    out_ref[:, width:] = code.astype(jnp.float32).astype(jnp.bfloat16)


def pack_body(chips, shards, *refs):
    rows, blocks = refs[:chips], refs[chips:]
    row_count, half = rows[0].shape[0], (rows[0].shape[1] - CODE) // 2
    block = 2 * CAP * chips
    height = E_WIN * block
    mine = lax.axis_index("exp") // shards
    at = lax.broadcasted_iota(jnp.int32, (height, CODE), 0)
    at_slot, at_part, at_chip = (at % block) // (2 * chips), (at % (2 * chips)) // chips, at % chips
    wanted = ((mine ^ (at // block)) * row_count + at_slot).astype(jnp.float32)
    diagonal = lax.broadcasted_iota(jnp.int32, (row_count, CODE), 0) == lax.broadcasted_iota(
        jnp.int32, (row_count, CODE), 1
    )
    total = jnp.zeros((height, half), jnp.float32)
    for chip in range(chips):
        code = rows[chip][:, 2 * half :].astype(jnp.float32)
        code = jnp.sum(jnp.where(diagonal, code, 0.0), axis=0, keepdims=True)
        for part in range(2):
            chosen = (wanted == code) & (at_chip == chip) & (at_part == part)
            placing = jnp.where(chosen, 1.0, 0.0).astype(jnp.bfloat16)[:, :row_count]
            total = total + jnp.dot(
                placing,
                rows[chip][:, part * half : (part + 1) * half],
                preferred_element_type=jnp.float32,
            )
    for expert in range(E_WIN):
        blocks[expert][...] = total[expert * block : (expert + 1) * block].astype(jnp.bfloat16)


def fetch_body(piece, owner_ref, resident, own, other, after, both, down, has_ref, sems):
    group = lax.axis_index("grp")
    copies = []
    for which, holder in enumerate((group, group ^ 1)):
        bucket, has = jnp.int32(0), jnp.int32(0)
        for index in range(BUCKETS):
            hit = owner_ref[index] == holder
            bucket, has = jnp.where(hit, index, bucket), jnp.where(hit, 1, has)
        here = pl.ds(which * piece, piece)
        for part in range(2):
            copies.append(
                pltpu.make_async_copy(
                    resident.at[part, pl.ds(pl.multiple_of(bucket * piece, piece), piece)],
                    both.at[part, here],
                    sems.at[3 * which + part],
                )
            )
        copies.append(
            pltpu.make_async_copy((own, other)[which], down.at[here], sems.at[3 * which + 2])
        )
        has_ref[here, :] = jnp.broadcast_to(has.astype(jnp.float32), (piece, has_ref.shape[1]))
    for copy in copies:
        copy.start()
    for copy in copies:
        copy.wait()


def expert_body(devices, chips, lanes, both, down, has_ref, *refs):
    blocks, partials, stacked = refs[:devices], refs[devices : 2 * devices], refs[-1]
    block, half = blocks[0].shape
    used = devices * block
    for index in range(devices):
        stacked[index * block : (index + 1) * block, :] = blocks[index][...]
    if lanes > used:
        stacked[used:, :] = jnp.zeros((lanes - used, half), jnp.bfloat16)
    sums = []
    for part in range(2):
        upper = lax.dot_general(
            both[part, :, :half], stacked[...], NT, preferred_element_type=jnp.float32
        )
        lower = lax.dot_general(
            both[part, :, half:], stacked[...], NT, preferred_element_type=jnp.float32
        )
        sums.append(upper + pltpu.roll(lower, lanes - chips, 1))
    column = lax.broadcasted_iota(jnp.int32, sums[0].shape, 1)
    valid = ((column % (2 * chips)) < chips) & (column < used)
    act = sums[0] * jax.nn.sigmoid(sums[0]) * sums[1]
    act = jnp.where(valid & (has_ref[...] > 0.5), act, 0.0)
    above = act.T.astype(jnp.bfloat16)[:used]
    below = pltpu.roll(act, chips, 1).T.astype(jnp.bfloat16)[:used]
    step = half // 7 if half % (7 * 128) == 0 else half
    for start in range(0, half, step):
        out = jnp.dot(above, down[:, start : start + step], preferred_element_type=jnp.float32)
        out = out + jnp.dot(
            below, down[:, half + start : half + start + step], preferred_element_type=jnp.float32
        )
        for index in range(devices):
            partials[index][:, start : start + step] = out[
                index * block : (index + 1) * block
            ].astype(jnp.bfloat16)


def combine_body(devices, chips, shards, *refs):
    rows, blocks = refs[:chips], refs[chips : chips + devices]
    outs, codes = refs[chips + devices : -1], refs[-1]
    block, half = blocks[0].shape
    row_count = outs[0].shape[0]
    mine = lax.axis_index("exp") // shards
    for chip in range(chips):
        codes[chip * row_count : (chip + 1) * row_count, :] = rows[chip][:, 2 * half :].astype(
            jnp.float32
        )
    code = codes[...]
    home = lax.broadcasted_iota(jnp.int32, code.shape, 0) // row_count
    at = lax.broadcasted_iota(jnp.int32, code.shape, 1)
    at_slot, at_part, at_chip = at // (2 * chips), (at % (2 * chips)) // chips, at % chips
    placing = []
    for expert in range(E_WIN):
        wanted = ((mine ^ expert) * row_count + at_slot).astype(jnp.float32)
        chosen = (wanted == code) & (at_chip == home) & (at < block)
        placing.append(
            [
                jnp.where(chosen & (at_part == part), 1.0, 0.0).astype(jnp.bfloat16)[:, :block]
                for part in range(2)
            ]
        )
    for part in range(2):
        total = 0.0
        for index in range(devices):
            total = total + jnp.dot(
                placing[index // shards][part],
                blocks[index][...],
                preferred_element_type=jnp.float32,
            )
        for chip in range(chips):
            outs[chip][:, part * half : (part + 1) * half] = total[
                chip * row_count : (chip + 1) * row_count
            ].astype(outs[chip].dtype)


def move_rows(hidden, norm_gain, route, route_weight, resident, sectioned, owner):
    rows = hidden[0]
    row_count, width = rows.shape
    devices = lax.axis_size("exp")
    chips = lax.axis_size("grp") // PAIR
    shards = devices // E_WIN
    half, block = width // 2, 2 * CAP * chips
    piece = sectioned.shape[1]
    payload = pl.pallas_call(
        prepare_body,
        out_shape=pltpu.VMEM((row_count, width + CODE), jnp.bfloat16),
        in_specs=[SMEM, VMEM, VMEM],
        out_specs=VMEM,
        compiler_params=limit(4),
        name="prepare",
    )(route.reshape(row_count), rows, norm_gain.reshape(1, width))
    gathered = [payload] + [swap(payload, "grp", PAIR * hop) for hop in range(1, chips)]
    own_piece, payload = lax.optimization_barrier((sectioned[0], payload))
    other_piece = swap(own_piece, "grp", 1)
    half_block = pltpu.VMEM((block, half), jnp.bfloat16)
    packed = pl.pallas_call(
        functools.partial(pack_body, chips, shards),
        out_shape=[half_block] * E_WIN,
        in_specs=[VMEM] * chips,
        out_specs=[VMEM] * E_WIN,
        compiler_params=limit(8),
        name="pack",
    )(*held(*gathered))
    blocks = [packed[bits // shards] for bits in range(devices)]
    blocks = [blocks[0]] + [swap(blocks[bits], "exp", bits) for bits in range(1, devices)]
    both, down, has = pl.pallas_call(
        functools.partial(fetch_body, piece),
        out_shape=[
            pltpu.VMEM((2, PAIR * piece, width), jnp.bfloat16),
            pltpu.VMEM((PAIR * piece, width), jnp.bfloat16),
            pltpu.VMEM((PAIR * piece, 128), jnp.float32),
        ],
        in_specs=[SMEM, HBM, HBM, ANY, ANY],
        out_specs=[VMEM] * 3,
        scratch_shapes=[pltpu.SemaphoreType.DMA((3 * PAIR,))],
        compiler_params=limit(2),
        name="fetch",
    )(owner, resident, sectioned[0], other_piece, packed[0])
    lanes = -(-devices * block // 128) * 128
    partials = pl.pallas_call(
        functools.partial(expert_body, devices, chips, lanes),
        out_shape=[half_block] * devices,
        in_specs=[VMEM] * (3 + devices),
        out_specs=[VMEM] * devices,
        scratch_shapes=[pltpu.VMEM((lanes, half), jnp.bfloat16)],
        compiler_params=limit(12),
        name="expert",
    )(*held(both, down, has, *blocks))
    returned = [partials[0]] + [swap(partials[bits], "exp", bits) for bits in range(1, devices)]
    home = pltpu.VMEM((row_count, width), jnp.bfloat16)
    sums = pl.pallas_call(
        functools.partial(combine_body, devices, chips, shards),
        out_shape=[home] * chips,
        in_specs=[VMEM] * (chips + devices),
        out_specs=[VMEM] * chips,
        scratch_shapes=[pltpu.VMEM((chips * row_count, CODE), jnp.float32)],
        compiler_params=limit(8),
        name="combine",
    )(*held(*gathered, *returned))
    combined = sums[0].astype(jnp.float32)
    for hop in range(1, chips):
        combined = combined + swap(sums[hop], "grp", PAIR * hop).astype(jnp.float32)
    result = (combined * route_weight[0][:, None]).astype(jnp.bfloat16)
    return result.reshape(1, row_count, width)


def per_device(hidden, norm_gain, route, route_weight, resident, sectioned, owner):
    weight_rows = BUCKETS * sectioned.shape[1]
    partial_rows = lax.axis_size("exp") * lax.axis_size("grp") // PAIR * hidden.shape[1]
    plan = move_rows if partial_rows < weight_rows else move_weights
    return plan(hidden, norm_gain, route, route_weight, resident, sectioned, owner)


def solution(mesh):
    in_specs = (
        P("grp", "exp", None),
        P(),
        P("grp", "exp", None),
        P("grp", "exp"),
        P(None, "exp", None),
        P("grp", "exp", None),
        P(),
    )
    out_specs = P("grp", "exp", None)
    return jax.shard_map(
        per_device, mesh=mesh, in_specs=in_specs, out_specs=out_specs, check_vma=False
    )
```

```python
import functools

import jax
import jax.numpy as jnp
from jax import lax
from jax.experimental import pallas as pl
from jax.experimental.pallas import tpu as pltpu
from jax.sharding import PartitionSpec as P


E_WIN = 2
BUCKETS = 4
CAP = 3
PAIR = 2


epsilon = 1e-06


def from_root(value, axis, source):
    kept = jnp.where(lax.axis_index(axis) == source, value, 0).astype(value.dtype)
    return lax.psum(kept, axis)


def activate(slot_rows, gate_up):
    gate_part = lax.dot_general(
        slot_rows, gate_up[0], (((1,), (1,)), ((), ())), preferred_element_type=jnp.float32
    )
    up_part = lax.dot_general(
        slot_rows, gate_up[1], (((1,), (1,)), ((), ())), preferred_element_type=jnp.float32
    )
    return (jax.nn.silu(gate_part) * up_part).astype(jnp.bfloat16)


def normalize(rows, norm_gain):
    row_data = rows.astype(jnp.float32)
    scale = lax.rsqrt(jnp.mean(row_data * row_data, axis=1, keepdims=True) + epsilon)
    return (row_data * scale * norm_gain[None, :]).astype(jnp.bfloat16)


def move_weights(hidden, norm_gain, route, route_weight, resident, sectioned, owner):
    normed = normalize(hidden[0], norm_gain)
    row_count, width = normed.shape
    devices = lax.axis_size("exp")
    shards = devices // E_WIN
    expert_ids = route[0, :, 0]
    onehot = (expert_ids[:, None] == jnp.arange(E_WIN, dtype=jnp.int32)[None, :]).astype(jnp.int32)
    position = jnp.cumsum(onehot, axis=0) - onehot
    slot_index = jnp.sum(position * onehot, axis=1)
    placing = onehot[:, :, None] * (
        slot_index[:, None, None] == jnp.arange(CAP, dtype=jnp.int32)[None, None, :]
    ).astype(jnp.int32)
    placing = placing.reshape(row_count, E_WIN * CAP)
    packed = jnp.dot(
        placing.astype(jnp.bfloat16).T, normed, preferred_element_type=jnp.float32
    ).astype(jnp.bfloat16)
    packed = packed.reshape(E_WIN, 1, CAP, width)
    outgoing = jnp.broadcast_to(packed, (E_WIN, shards, CAP, width)).reshape(devices, CAP, width)
    piece_rows = sectioned.shape[1]
    arrived = lax.all_to_all(outgoing, "exp", split_axis=0, concat_axis=0, tiled=True)
    flat_slots = arrived.reshape(-1, width)
    activation = activate(flat_slots, resident)
    running_sum = jnp.zeros((flat_slots.shape[0], width), jnp.float32)
    for bucket in range(BUCKETS):
        weight_piece = from_root(sectioned[0], "grp", owner[bucket])
        act_piece = activation[:, bucket * piece_rows : (bucket + 1) * piece_rows]
        running_sum = running_sum + jnp.dot(
            act_piece, weight_piece, preferred_element_type=jnp.float32
        )
    partials = running_sum.astype(jnp.bfloat16).reshape(arrived.shape)
    returned = lax.all_to_all(partials, "exp", split_axis=0, concat_axis=0, tiled=True)
    summed = jnp.sum(returned.astype(jnp.float32).reshape(E_WIN, shards, CAP, width), axis=1)
    summed = summed.reshape(E_WIN * CAP, width)
    combined = jnp.dot(placing.astype(jnp.float32), summed, precision=lax.Precision.HIGHEST)
    result = (combined * route_weight[0][:, None]).astype(jnp.bfloat16)
    return result.reshape(1, row_count, width)


def swap(value, axis, bits):
    size = lax.axis_size(axis)
    return lax.ppermute(value, axis, [(i, i ^ bits) for i in range(size)])


NT = (((1,), (1,)), ((), ()))
VMEM = pl.BlockSpec(memory_space=pltpu.VMEM)
ANY = pl.BlockSpec(memory_space=pl.ANY)
HBM = pl.BlockSpec(memory_space=pltpu.HBM)
CODE = 128
MIB = 1 << 20


def held(*values):
    return [pltpu.with_memory_space_constraint(value, pltpu.VMEM) for value in values]


def in_hbm(*values):
    return [pltpu.with_memory_space_constraint(value, pltpu.HBM) for value in values]


def limit(mib):
    return pltpu.CompilerParams(vmem_limit_bytes=mib * MIB)


def prepare_body(route_hbm, rows_hbm, gain_hbm, out_ref, route_ref, rows_ref, gain_ref, sems):
    copies = [
        pltpu.make_async_copy(source, target, sems.at[index])
        for index, (source, target) in enumerate(
            ((rows_hbm, rows_ref), (gain_hbm, gain_ref), (route_hbm, route_ref))
        )
    ]
    for copy in copies:
        copy.start()
    for copy in copies:
        copy.wait()
    row_count, width = rows_ref.shape
    rows = rows_ref[...].astype(jnp.float32)
    scale = lax.rsqrt(jnp.sum(rows * rows, axis=1, keepdims=True) * (1.0 / width) + epsilon)
    out_ref[:, :width] = (rows * scale * gain_ref[...]).astype(jnp.bfloat16)
    named = [route_ref[0, row] for row in range(row_count)]
    at = lax.broadcasted_iota(jnp.int32, (row_count, CODE), 0)
    code = jnp.zeros((row_count, CODE), jnp.int32)
    for row in range(row_count):
        slot = jnp.int32(0)
        for before in range(row):
            slot = slot + jnp.where(named[before] == named[row], 1, 0)
        code = jnp.where(at == row, named[row] * row_count + slot, code)
    out_ref[:, width:] = code.astype(jnp.float32).astype(jnp.bfloat16)


def pack_body(chips, shards, *refs):
    rows, blocks = refs[:chips], refs[chips:]
    row_count, half = rows[0].shape[0], (rows[0].shape[1] - CODE) // 2
    block = 2 * CAP * chips
    height = E_WIN * block
    mine = lax.axis_index("exp") // shards
    at = lax.broadcasted_iota(jnp.int32, (height, CODE), 0)
    at_slot, at_part, at_chip = (at % block) // (2 * chips), (at % (2 * chips)) // chips, at % chips
    wanted = ((mine ^ (at // block)) * row_count + at_slot).astype(jnp.float32)
    diagonal = lax.broadcasted_iota(jnp.int32, (row_count, CODE), 0) == lax.broadcasted_iota(
        jnp.int32, (row_count, CODE), 1
    )
    total = jnp.zeros((height, half), jnp.float32)
    for chip in range(chips):
        code = rows[chip][:, 2 * half :].astype(jnp.float32)
        code = jnp.sum(jnp.where(diagonal, code, 0.0), axis=0, keepdims=True)
        for part in range(2):
            chosen = (wanted == code) & (at_chip == chip) & (at_part == part)
            placing = jnp.where(chosen, 1.0, 0.0).astype(jnp.bfloat16)[:, :row_count]
            total = total + jnp.dot(
                placing,
                rows[chip][:, part * half : (part + 1) * half],
                preferred_element_type=jnp.float32,
            )
    for expert in range(E_WIN):
        blocks[expert][...] = total[expert * block : (expert + 1) * block].astype(jnp.bfloat16)


def fetch_body(piece, owner, resident, after, both, has_ref, owner_ref, sems):
    owner_copy = pltpu.make_async_copy(owner, owner_ref, sems.at[2 * PAIR])
    owner_copy.start()
    owner_copy.wait()
    group = lax.axis_index("grp")
    copies = []
    for which, holder in enumerate((group, group ^ 1)):
        bucket, has = jnp.int32(0), jnp.int32(0)
        for index in range(BUCKETS):
            hit = owner_ref[0, index] == holder
            bucket, has = jnp.where(hit, index, bucket), jnp.where(hit, 1, has)
        here = pl.ds(which * piece, piece)
        for part in range(2):
            copies.append(
                pltpu.make_async_copy(
                    resident.at[part, pl.ds(pl.multiple_of(bucket * piece, piece), piece)],
                    both.at[part, here],
                    sems.at[2 * which + part],
                )
            )
        has_ref[here, :] = jnp.broadcast_to(has.astype(jnp.float32), (piece, has_ref.shape[1]))
    for copy in copies:
        copy.start()
    for copy in copies:
        copy.wait()


def expert_body(devices, chips, lanes, own, other, both, has_ref, *refs):
    blocks, partials = refs[:devices], refs[devices : 2 * devices]
    stacked, down, sems = refs[2 * devices :]
    piece = own.shape[0]
    copies = [
        pltpu.make_async_copy(source, down.at[pl.ds(index * piece, piece)], sems.at[index])
        for index, source in enumerate((own, other))
    ]
    for copy in copies:
        copy.start()
    block, half = blocks[0].shape
    used = devices * block
    for index in range(devices):
        stacked[index * block : (index + 1) * block, :] = blocks[index][...]
    if lanes > used:
        stacked[used:, :] = jnp.zeros((lanes - used, half), jnp.bfloat16)
    sums = []
    for part in range(2):
        upper = lax.dot_general(
            both[part, :, :half], stacked[...], NT, preferred_element_type=jnp.float32
        )
        lower = lax.dot_general(
            both[part, :, half:], stacked[...], NT, preferred_element_type=jnp.float32
        )
        sums.append(upper + pltpu.roll(lower, lanes - chips, 1))
    column = lax.broadcasted_iota(jnp.int32, sums[0].shape, 1)
    valid = ((column % (2 * chips)) < chips) & (column < used)
    act = sums[0] * jax.nn.sigmoid(sums[0]) * sums[1]
    act = jnp.where(valid & (has_ref[...] > 0.5), act, 0.0)
    above = act.T.astype(jnp.bfloat16)[:used]
    below = pltpu.roll(act, chips, 1).T.astype(jnp.bfloat16)[:used]
    for copy in copies:
        copy.wait()
    step = half // 7 if half % (7 * 128) == 0 else half
    for start in range(0, half, step):
        out = jnp.dot(above, down[:, start : start + step], preferred_element_type=jnp.float32)
        out = out + jnp.dot(
            below, down[:, half + start : half + start + step], preferred_element_type=jnp.float32
        )
        for index in range(devices):
            partials[index][:, start : start + step] = out[
                index * block : (index + 1) * block
            ].astype(jnp.bfloat16)


def combine_body(devices, chips, shards, *refs):
    rows, blocks = refs[:chips], refs[chips : chips + devices]
    outs, codes = refs[chips + devices : -1], refs[-1]
    block, half = blocks[0].shape
    row_count = outs[0].shape[0]
    mine = lax.axis_index("exp") // shards
    for chip in range(chips):
        codes[chip * row_count : (chip + 1) * row_count, :] = rows[chip][:, 2 * half :].astype(
            jnp.float32
        )
    code = codes[...]
    home = lax.broadcasted_iota(jnp.int32, code.shape, 0) // row_count
    at = lax.broadcasted_iota(jnp.int32, code.shape, 1)
    at_slot, at_part, at_chip = at // (2 * chips), (at % (2 * chips)) // chips, at % chips
    placing = []
    for expert in range(E_WIN):
        wanted = ((mine ^ expert) * row_count + at_slot).astype(jnp.float32)
        chosen = (wanted == code) & (at_chip == home) & (at < block)
        placing.append(
            [
                jnp.where(chosen & (at_part == part), 1.0, 0.0).astype(jnp.bfloat16)[:, :block]
                for part in range(2)
            ]
        )
    for part in range(2):
        total = 0.0
        for index in range(devices):
            total = total + jnp.dot(
                placing[index // shards][part],
                blocks[index][...],
                preferred_element_type=jnp.float32,
            )
        for chip in range(chips):
            outs[chip][:, part * half : (part + 1) * half] = total[
                chip * row_count : (chip + 1) * row_count
            ].astype(outs[chip].dtype)


def move_rows(hidden, norm_gain, route, route_weight, resident, sectioned, owner):
    rows = hidden[0]
    row_count, width = rows.shape
    devices = lax.axis_size("exp")
    chips = lax.axis_size("grp") // PAIR
    shards = devices // E_WIN
    half, block = width // 2, 2 * CAP * chips
    piece = sectioned.shape[1]
    payload = pl.pallas_call(
        prepare_body,
        out_shape=pltpu.VMEM((row_count, width + CODE), jnp.bfloat16),
        in_specs=[HBM] * 3,
        out_specs=VMEM,
        scratch_shapes=[
            pltpu.SMEM((1, row_count), jnp.int32),
            pltpu.VMEM((row_count, width), jnp.bfloat16),
            pltpu.VMEM((1, width), jnp.float32),
            pltpu.SemaphoreType.DMA((3,)),
        ],
        compiler_params=limit(4),
        name="prepare",
    )(*in_hbm(route.reshape(1, row_count), rows, norm_gain.reshape(1, width)))
    gathered = [payload]
    for hop in range(1, chips):
        gathered.append(swap(payload, "grp", PAIR * hop))
    other_piece = swap(sectioned[0], "grp", 1)
    half_block = pltpu.VMEM((block, half), jnp.bfloat16)
    packed = pl.pallas_call(
        functools.partial(pack_body, chips, shards),
        out_shape=[half_block] * E_WIN,
        in_specs=[VMEM] * chips,
        out_specs=[VMEM] * E_WIN,
        compiler_params=limit(8),
        name="pack",
    )(*held(*gathered))
    blocks = [packed[bits // shards] for bits in range(devices)]
    blocks = [blocks[0]] + [swap(blocks[bits], "exp", bits) for bits in range(1, devices)]
    both, has = pl.pallas_call(
        functools.partial(fetch_body, piece),
        out_shape=[
            pltpu.VMEM((2, PAIR * piece, width), jnp.bfloat16),
            pltpu.VMEM((PAIR * piece, 128), jnp.float32),
        ],
        in_specs=[HBM, HBM, ANY],
        out_specs=[VMEM] * 2,
        scratch_shapes=[
            pltpu.SMEM((1, owner.shape[0]), jnp.int32),
            pltpu.SemaphoreType.DMA((2 * PAIR + 1,)),
        ],
        compiler_params=limit(2),
        name="fetch",
    )(*in_hbm(owner.reshape(1, -1), resident), *held(packed[0]))
    lanes = -(-devices * block // 128) * 128
    partials = pl.pallas_call(
        functools.partial(expert_body, devices, chips, lanes),
        out_shape=[half_block] * devices,
        in_specs=[HBM, ANY] + [VMEM] * (2 + devices),
        out_specs=[VMEM] * devices,
        scratch_shapes=[
            pltpu.VMEM((lanes, half), jnp.bfloat16),
            pltpu.VMEM((PAIR * piece, width), jnp.bfloat16),
            pltpu.SemaphoreType.DMA((PAIR,)),
        ],
        compiler_params=limit(16),
        name="expert",
    )(*in_hbm(sectioned[0]), *held(other_piece, both, has, *blocks))
    returned = [partials[0]] + [swap(partials[bits], "exp", bits) for bits in range(1, devices)]
    home = pltpu.VMEM((row_count, width), jnp.bfloat16)
    sums = pl.pallas_call(
        functools.partial(combine_body, devices, chips, shards),
        out_shape=[home] * chips,
        in_specs=[VMEM] * (chips + devices),
        out_specs=[VMEM] * chips,
        scratch_shapes=[pltpu.VMEM((chips * row_count, CODE), jnp.float32)],
        compiler_params=limit(8),
        name="combine",
    )(*held(*gathered, *returned))
    combined = sums[0].astype(jnp.float32)
    for hop in range(1, chips):
        combined = combined + swap(sums[hop], "grp", PAIR * hop).astype(jnp.float32)
    result = (combined * route_weight[0][:, None]).astype(jnp.bfloat16)
    return result.reshape(1, row_count, width)


def per_device(hidden, norm_gain, route, route_weight, resident, sectioned, owner):
    weight_rows = BUCKETS * sectioned.shape[1]
    partial_rows = lax.axis_size("exp") * lax.axis_size("grp") // PAIR * hidden.shape[1]
    plan = move_rows if partial_rows < weight_rows else move_weights
    return plan(hidden, norm_gain, route, route_weight, resident, sectioned, owner)


def solution(mesh):
    in_specs = (
        P("grp", "exp", None),
        P(),
        P("grp", "exp", None),
        P("grp", "exp"),
        P(None, "exp", None),
        P("grp", "exp", None),
        P(),
    )
    out_specs = P("grp", "exp", None)
    return jax.shard_map(
        per_device, mesh=mesh, in_specs=in_specs, out_specs=out_specs, check_vma=False
    )
```

```python
import functools

import jax
import jax.numpy as jnp
from jax import lax
from jax.experimental import pallas as pl
from jax.experimental.pallas import tpu as pltpu
from jax.sharding import PartitionSpec as P


E_WIN = 2
BUCKETS = 4
CAP = 3
PAIR = 2


epsilon = 1e-06


def from_root(value, axis, source):
    kept = jnp.where(lax.axis_index(axis) == source, value, 0).astype(value.dtype)
    return lax.psum(kept, axis)


def activate(slot_rows, gate_up):
    gate_part = lax.dot_general(
        slot_rows, gate_up[0], (((1,), (1,)), ((), ())), preferred_element_type=jnp.float32
    )
    up_part = lax.dot_general(
        slot_rows, gate_up[1], (((1,), (1,)), ((), ())), preferred_element_type=jnp.float32
    )
    return (jax.nn.silu(gate_part) * up_part).astype(jnp.bfloat16)


def normalize(rows, norm_gain):
    row_data = rows.astype(jnp.float32)
    scale = lax.rsqrt(jnp.mean(row_data * row_data, axis=1, keepdims=True) + epsilon)
    return (row_data * scale * norm_gain[None, :]).astype(jnp.bfloat16)


def move_weights(hidden, norm_gain, route, route_weight, resident, sectioned, owner):
    normed = normalize(hidden[0], norm_gain)
    row_count, width = normed.shape
    devices = lax.axis_size("exp")
    shards = devices // E_WIN
    expert_ids = route[0, :, 0]
    onehot = (expert_ids[:, None] == jnp.arange(E_WIN, dtype=jnp.int32)[None, :]).astype(jnp.int32)
    position = jnp.cumsum(onehot, axis=0) - onehot
    slot_index = jnp.sum(position * onehot, axis=1)
    placing = onehot[:, :, None] * (
        slot_index[:, None, None] == jnp.arange(CAP, dtype=jnp.int32)[None, None, :]
    ).astype(jnp.int32)
    placing = placing.reshape(row_count, E_WIN * CAP)
    packed = jnp.dot(
        placing.astype(jnp.bfloat16).T, normed, preferred_element_type=jnp.float32
    ).astype(jnp.bfloat16)
    packed = packed.reshape(E_WIN, 1, CAP, width)
    outgoing = jnp.broadcast_to(packed, (E_WIN, shards, CAP, width)).reshape(devices, CAP, width)
    piece_rows = sectioned.shape[1]
    arrived = lax.all_to_all(outgoing, "exp", split_axis=0, concat_axis=0, tiled=True)
    flat_slots = arrived.reshape(-1, width)
    activation = activate(flat_slots, resident)
    running_sum = jnp.zeros((flat_slots.shape[0], width), jnp.float32)
    for bucket in range(BUCKETS):
        weight_piece = from_root(sectioned[0], "grp", owner[bucket])
        act_piece = activation[:, bucket * piece_rows : (bucket + 1) * piece_rows]
        running_sum = running_sum + jnp.dot(
            act_piece, weight_piece, preferred_element_type=jnp.float32
        )
    partials = running_sum.astype(jnp.bfloat16).reshape(arrived.shape)
    returned = lax.all_to_all(partials, "exp", split_axis=0, concat_axis=0, tiled=True)
    summed = jnp.sum(returned.astype(jnp.float32).reshape(E_WIN, shards, CAP, width), axis=1)
    summed = summed.reshape(E_WIN * CAP, width)
    combined = jnp.dot(placing.astype(jnp.float32), summed, precision=lax.Precision.HIGHEST)
    result = (combined * route_weight[0][:, None]).astype(jnp.bfloat16)
    return result.reshape(1, row_count, width)


def swap(value, axis, bits):
    size = lax.axis_size(axis)
    return lax.ppermute(value, axis, [(i, i ^ bits) for i in range(size)])


NT = (((1,), (1,)), ((), ()))
VMEM = pl.BlockSpec(memory_space=pltpu.VMEM)
ANY = pl.BlockSpec(memory_space=pl.ANY)
HBM = pl.BlockSpec(memory_space=pltpu.HBM)
CODE = 128
MIB = 1 << 20


def held(*values):
    return [pltpu.with_memory_space_constraint(value, pltpu.VMEM) for value in values]


def in_hbm(*values):
    return [pltpu.with_memory_space_constraint(value, pltpu.HBM) for value in values]


def limit(mib):
    return pltpu.CompilerParams(vmem_limit_bytes=mib * MIB)


def prepare_body(shards, route_hbm, rows_hbm, gain_hbm, *refs):
    blocks, code_ref = refs[:E_WIN], refs[E_WIN]
    route_ref, rows_ref, gain_ref, sems = refs[E_WIN + 1 :]
    copies = [
        pltpu.make_async_copy(source, target, sems.at[index])
        for index, (source, target) in enumerate(
            ((rows_hbm, rows_ref), (gain_hbm, gain_ref), (route_hbm, route_ref))
        )
    ]
    for copy in copies:
        copy.start()
    for copy in copies:
        copy.wait()
    row_count, width = rows_ref.shape
    rows = rows_ref[...].astype(jnp.float32)
    scale = lax.rsqrt(jnp.sum(rows * rows, axis=1, keepdims=True) * (1.0 / width) + epsilon)
    normed = (rows * scale * gain_ref[...]).astype(jnp.bfloat16)
    named = [route_ref[0, row] for row in range(row_count)]
    at = lax.broadcasted_iota(jnp.int32, code_ref.shape, 1)
    code = jnp.full(code_ref.shape, -1, jnp.int32)
    for row in range(row_count):
        slot = jnp.int32(0)
        for before in range(row):
            slot = slot + jnp.where(named[before] == named[row], 1, 0)
        code = jnp.where(at == row, named[row] * row_count + slot, code)
    code_ref[...] = code.astype(jnp.float32)
    mine = lax.axis_index("exp") // shards
    height = E_WIN * row_count
    row = lax.broadcasted_iota(jnp.int32, (height, CODE), 0)
    wanted = (mine ^ (row // row_count)) * row_count + row % row_count
    placing = jnp.where(wanted == code[0:1], 1.0, 0.0).astype(jnp.bfloat16)[:, :row_count]
    packed = jnp.dot(placing, normed, preferred_element_type=jnp.float32)
    for expert in range(E_WIN):
        blocks[expert][...] = packed[expert * row_count : (expert + 1) * row_count].astype(
            jnp.bfloat16
        )


def ahead_body(owner, resident, after, early, flags, owner_ref, sems):
    early_copy = pltpu.make_async_copy(resident.at[:, pl.ds(0, early.shape[1])], early, sems.at[0])
    early_copy.start()
    owner_copy = pltpu.make_async_copy(owner, owner_ref, sems.at[1])
    owner_copy.start()
    owner_copy.wait()
    group = lax.axis_index("grp")
    row = lax.broadcasted_iota(jnp.int32, flags.shape, 0)
    values = jnp.zeros(flags.shape, jnp.float32)
    for which in range(PAIR):
        for bucket in range(BUCKETS):
            hit = jnp.where(owner_ref[0, bucket] == (group ^ which), 1.0, 0.0)
            values = jnp.where(row == which * BUCKETS + bucket, hit, values)
    flags[...] = values
    early_copy.wait()


def activate_body(devices, resident, early, code_ref, *refs):
    blocks, out = refs[:devices], refs[devices]
    late, stacked, sem = refs[devices + 1 :]
    first = early.shape[1]
    late_copy = pltpu.make_async_copy(
        resident.at[:, pl.ds(first, late.shape[1])], late, sem.at[0]
    )
    late_copy.start()
    row_count = blocks[0].shape[0]
    for index in range(devices):
        stacked[index * row_count : (index + 1) * row_count, :] = blocks[index][...].astype(
            jnp.float32
        )
    rows = stacked[...].astype(jnp.bfloat16)

    def hidden_units(weights):
        gate = lax.dot_general(weights[0], rows, NT, preferred_element_type=jnp.float32)
        up = lax.dot_general(weights[1], rows, NT, preferred_element_type=jnp.float32)
        return (gate * jax.nn.sigmoid(gate) * up).T

    out[:, :first] = hidden_units(early).astype(jnp.bfloat16)
    late_copy.wait()
    out[:, first:] = hidden_units(late).astype(jnp.bfloat16)
    head = out[:, :CODE]
    spare = lax.broadcasted_iota(jnp.int32, head.shape, 0) == CAP
    out[:, :CODE] = jnp.where(spare, code_ref[0:1, :], head.astype(jnp.float32)).astype(
        jnp.bfloat16
    )


def hold_body(own, other, after, down, sems):
    piece = own.shape[0]
    copies = [
        pltpu.make_async_copy(source, down.at[pl.ds(index * piece, piece)], sems.at[index])
        for index, source in enumerate((own, other))
    ]
    for copy in copies:
        copy.start()
    for copy in copies:
        copy.wait()


def down_body(devices, chips, down, flags, *refs):
    acts, partials = refs[:chips], refs[chips:]
    block, half = partials[0].shape
    used = devices * block
    rows, units = acts[0].shape
    row_count, piece = rows // devices, units // BUCKETS
    row = lax.broadcasted_iota(jnp.int32, (2 * used, rows), 0)
    column = lax.broadcasted_iota(jnp.int32, (2 * used, rows), 1)
    lower, within = row // used, row % used
    home, spot = within // block, within % block
    slot, part, chip_at = spot // (2 * chips), (spot % (2 * chips)) // chips, spot % chips
    matches = (part == lower) & (home == column // row_count) & (slot == column % row_count)
    placed = jnp.zeros((2 * used, PAIR * piece), jnp.float32)
    for chip in range(chips):
        picked = []
        for which in range(PAIR):
            chosen = jnp.zeros((rows, piece), jnp.float32)
            for bucket in range(BUCKETS):
                flag = flags[which * BUCKETS + bucket : which * BUCKETS + bucket + 1, 0:piece]
                piece_of = acts[chip][:, bucket * piece : (bucket + 1) * piece].astype(jnp.float32)
                chosen = jnp.where(flag > 0.5, piece_of, chosen)
            picked.append(chosen.astype(jnp.bfloat16))
        placing = jnp.where(matches & (chip_at == chip), 1.0, 0.0).astype(jnp.bfloat16)
        placed = placed + jnp.dot(
            placing, jnp.concatenate(picked, axis=1), preferred_element_type=jnp.float32
        )
    placed = placed.astype(jnp.bfloat16)
    above, below = placed[:used], placed[used:]
    step = half // 7 if half % (7 * 128) == 0 else half
    for start in range(0, half, step):
        out = jnp.dot(above, down[:, start : start + step], preferred_element_type=jnp.float32)
        out = out + jnp.dot(
            below, down[:, half + start : half + start + step], preferred_element_type=jnp.float32
        )
        for index in range(devices):
            partials[index][:, start : start + step] = out[
                index * block : (index + 1) * block
            ].astype(jnp.bfloat16)


def combine_body(devices, chips, shards, *refs):
    acts, blocks = refs[:chips], refs[chips : chips + devices]
    outs, codes = refs[chips + devices : -1], refs[-1]
    block, half = blocks[0].shape
    row_count = outs[0].shape[0]
    mine = lax.axis_index("exp") // shards
    diagonal = lax.broadcasted_iota(jnp.int32, (row_count, CODE), 0) == lax.broadcasted_iota(
        jnp.int32, (row_count, CODE), 1
    )
    for chip in range(chips):
        line = acts[chip][:, :CODE].astype(jnp.float32)[CAP : CAP + 1, :]
        mark = jnp.sum(jnp.where(diagonal, line, 0.0), axis=1, keepdims=True)
        codes[chip * row_count : (chip + 1) * row_count, :] = jnp.broadcast_to(
            mark, (row_count, CODE)
        )
    code = codes[...]
    home = lax.broadcasted_iota(jnp.int32, code.shape, 0) // row_count
    at = lax.broadcasted_iota(jnp.int32, code.shape, 1)
    at_slot, at_part, at_chip = at // (2 * chips), (at % (2 * chips)) // chips, at % chips
    placing = []
    for expert in range(E_WIN):
        wanted = ((mine ^ expert) * row_count + at_slot).astype(jnp.float32)
        chosen = (wanted == code) & (at_chip == home) & (at < block)
        placing.append(
            [
                jnp.where(chosen & (at_part == part), 1.0, 0.0).astype(jnp.bfloat16)[:, :block]
                for part in range(2)
            ]
        )
    for part in range(2):
        total = 0.0
        for index in range(devices):
            total = total + jnp.dot(
                placing[index // shards][part],
                blocks[index][...],
                preferred_element_type=jnp.float32,
            )
        for chip in range(chips):
            outs[chip][:, part * half : (part + 1) * half] = total[
                chip * row_count : (chip + 1) * row_count
            ].astype(outs[chip].dtype)


def exchange(values, axis, unit):
    moved = [values[0]]
    for bits in range(1, len(values)):
        moved.append(swap(values[bits], axis, bits * unit))
    return moved


def move_rows(hidden, norm_gain, route, route_weight, resident, sectioned, owner):
    rows, own_piece = hidden[0], sectioned[0]
    row_count, width = rows.shape
    devices = lax.axis_size("exp")
    chips = lax.axis_size("grp") // PAIR
    shards = devices // E_WIN
    half, block = width // 2, 2 * CAP * chips
    piece, units = own_piece.shape[0], resident.shape[1]
    early_units = units * 5 // 8
    row_block = pltpu.VMEM((row_count, width), jnp.bfloat16)
    *packed, code = pl.pallas_call(
        functools.partial(prepare_body, shards),
        out_shape=[row_block] * E_WIN + [pltpu.VMEM((8, CODE), jnp.float32)],
        in_specs=[HBM] * 3,
        out_specs=[VMEM] * (E_WIN + 1),
        scratch_shapes=[
            pltpu.SMEM((1, row_count), jnp.int32),
            pltpu.VMEM((row_count, width), jnp.bfloat16),
            pltpu.VMEM((1, width), jnp.float32),
            pltpu.SemaphoreType.DMA((3,)),
        ],
        compiler_params=limit(4),
        name="prepare",
    )(*in_hbm(route.reshape(1, row_count), rows, norm_gain.reshape(1, width)))
    arrived = exchange([packed[bits // shards] for bits in range(devices)], "exp", 1)
    other_piece = swap(own_piece, "grp", 1)
    early, flags = pl.pallas_call(
        ahead_body,
        out_shape=[
            pltpu.VMEM((2, early_units, width), jnp.bfloat16),
            pltpu.VMEM((8, CODE), jnp.float32),
        ],
        in_specs=[HBM, HBM, ANY],
        out_specs=[VMEM] * 2,
        scratch_shapes=[
            pltpu.SMEM((1, owner.shape[0]), jnp.int32),
            pltpu.SemaphoreType.DMA((2,)),
        ],
        compiler_params=limit(2),
        name="ahead",
    )(*in_hbm(owner.reshape(1, -1), resident), *held(code))
    act = pl.pallas_call(
        functools.partial(activate_body, devices),
        out_shape=pltpu.VMEM((devices * row_count, units), jnp.bfloat16),
        in_specs=[HBM] + [VMEM] * (2 + devices),
        out_specs=VMEM,
        scratch_shapes=[
            pltpu.VMEM((2, units - early_units, width), jnp.bfloat16),
            pltpu.VMEM((devices * row_count, width), jnp.float32),
            pltpu.SemaphoreType.DMA((1,)),
        ],
        compiler_params=limit(16),
        name="activate",
    )(*in_hbm(resident), *held(early, code, *arrived))
    acts = exchange([act] * chips, "grp", PAIR)
    down = pl.pallas_call(
        hold_body,
        out_shape=pltpu.VMEM((PAIR * piece, width), jnp.bfloat16),
        in_specs=[HBM, ANY, ANY],
        out_specs=VMEM,
        scratch_shapes=[pltpu.SemaphoreType.DMA((PAIR,))],
        compiler_params=limit(2),
        name="hold",
    )(*in_hbm(own_piece), *held(other_piece, act))
    half_block = pltpu.VMEM((block, half), jnp.bfloat16)
    partials = pl.pallas_call(
        functools.partial(down_body, devices, chips),
        out_shape=[half_block] * devices,
        in_specs=[VMEM] * (2 + chips),
        out_specs=[VMEM] * devices,
        compiler_params=limit(12),
        name="down",
    )(*held(down, flags, *acts))
    returned = exchange(partials, "exp", 1)
    sums = pl.pallas_call(
        functools.partial(combine_body, devices, chips, shards),
        out_shape=[row_block] * chips,
        in_specs=[VMEM] * (chips + devices),
        out_specs=[VMEM] * chips,
        scratch_shapes=[pltpu.VMEM((chips * row_count, CODE), jnp.float32)],
        compiler_params=limit(8),
        name="combine",
    )(*held(*acts, *returned))
    combined = 0.0
    for share in exchange(sums, "grp", PAIR):
        combined = combined + share.astype(jnp.float32)
    result = (combined * route_weight[0][:, None]).astype(jnp.bfloat16)
    return result.reshape(1, row_count, width)


def per_device(hidden, norm_gain, route, route_weight, resident, sectioned, owner):
    weight_rows = BUCKETS * sectioned.shape[1]
    partial_rows = lax.axis_size("exp") * lax.axis_size("grp") // PAIR * hidden.shape[1]
    plan = move_rows if partial_rows < weight_rows else move_weights
    return plan(hidden, norm_gain, route, route_weight, resident, sectioned, owner)


def solution(mesh):
    in_specs = (
        P("grp", "exp", None),
        P(),
        P("grp", "exp", None),
        P("grp", "exp"),
        P(None, "exp", None),
        P("grp", "exp", None),
        P(),
    )
    out_specs = P("grp", "exp", None)
    return jax.shard_map(
        per_device, mesh=mesh, in_specs=in_specs, out_specs=out_specs, check_vma=False
    )
```

```python
import functools

import jax
import jax.numpy as jnp
from jax import lax
from jax.experimental import pallas as pl
from jax.experimental.pallas import tpu as pltpu
from jax.sharding import PartitionSpec as P


E_WIN = 2
BUCKETS = 4
CAP = 3
PAIR = 2


epsilon = 1e-06


def from_root(value, axis, source):
    kept = jnp.where(lax.axis_index(axis) == source, value, 0).astype(value.dtype)
    return lax.psum(kept, axis)


def activate(slot_rows, gate_up):
    gate_part = lax.dot_general(
        slot_rows, gate_up[0], (((1,), (1,)), ((), ())), preferred_element_type=jnp.float32
    )
    up_part = lax.dot_general(
        slot_rows, gate_up[1], (((1,), (1,)), ((), ())), preferred_element_type=jnp.float32
    )
    return (jax.nn.silu(gate_part) * up_part).astype(jnp.bfloat16)


def normalize(rows, norm_gain):
    row_data = rows.astype(jnp.float32)
    scale = lax.rsqrt(jnp.mean(row_data * row_data, axis=1, keepdims=True) + epsilon)
    return (row_data * scale * norm_gain[None, :]).astype(jnp.bfloat16)


def move_weights(hidden, norm_gain, route, route_weight, resident, sectioned, owner):
    normed = normalize(hidden[0], norm_gain)
    row_count, width = normed.shape
    devices = lax.axis_size("exp")
    shards = devices // E_WIN
    expert_ids = route[0, :, 0]
    onehot = (expert_ids[:, None] == jnp.arange(E_WIN, dtype=jnp.int32)[None, :]).astype(jnp.int32)
    position = jnp.cumsum(onehot, axis=0) - onehot
    slot_index = jnp.sum(position * onehot, axis=1)
    placing = onehot[:, :, None] * (
        slot_index[:, None, None] == jnp.arange(CAP, dtype=jnp.int32)[None, None, :]
    ).astype(jnp.int32)
    placing = placing.reshape(row_count, E_WIN * CAP)
    packed = jnp.dot(
        placing.astype(jnp.bfloat16).T, normed, preferred_element_type=jnp.float32
    ).astype(jnp.bfloat16)
    packed = packed.reshape(E_WIN, 1, CAP, width)
    outgoing = jnp.broadcast_to(packed, (E_WIN, shards, CAP, width)).reshape(devices, CAP, width)
    piece_rows = sectioned.shape[1]
    arrived = lax.all_to_all(outgoing, "exp", split_axis=0, concat_axis=0, tiled=True)
    flat_slots = arrived.reshape(-1, width)
    activation = activate(flat_slots, resident)
    running_sum = jnp.zeros((flat_slots.shape[0], width), jnp.float32)
    for bucket in range(BUCKETS):
        weight_piece = from_root(sectioned[0], "grp", owner[bucket])
        act_piece = activation[:, bucket * piece_rows : (bucket + 1) * piece_rows]
        running_sum = running_sum + jnp.dot(
            act_piece, weight_piece, preferred_element_type=jnp.float32
        )
    partials = running_sum.astype(jnp.bfloat16).reshape(arrived.shape)
    returned = lax.all_to_all(partials, "exp", split_axis=0, concat_axis=0, tiled=True)
    summed = jnp.sum(returned.astype(jnp.float32).reshape(E_WIN, shards, CAP, width), axis=1)
    summed = summed.reshape(E_WIN * CAP, width)
    combined = jnp.dot(placing.astype(jnp.float32), summed, precision=lax.Precision.HIGHEST)
    result = (combined * route_weight[0][:, None]).astype(jnp.bfloat16)
    return result.reshape(1, row_count, width)


def swap(value, axis, bits):
    size = lax.axis_size(axis)
    return lax.ppermute(value, axis, [(i, i ^ bits) for i in range(size)])


NT = (((1,), (1,)), ((), ()))
VMEM = pl.BlockSpec(memory_space=pltpu.VMEM)
ANY = pl.BlockSpec(memory_space=pl.ANY)
HBM = pl.BlockSpec(memory_space=pltpu.HBM)
CODE = 128
MIB = 1 << 20


def held(*values):
    return [pltpu.with_memory_space_constraint(value, pltpu.VMEM) for value in values]


def in_hbm(*values):
    return [pltpu.with_memory_space_constraint(value, pltpu.HBM) for value in values]


def limit(mib):
    return pltpu.CompilerParams(vmem_limit_bytes=mib * MIB)


def prepare_body(shards, route_hbm, rows_hbm, gain_hbm, *refs):
    blocks, code_ref = refs[:E_WIN], refs[E_WIN]
    route_ref, rows_ref, gain_ref, sems = refs[E_WIN + 1 :]
    copies = [
        pltpu.make_async_copy(source, target, sems.at[index])
        for index, (source, target) in enumerate(
            ((rows_hbm, rows_ref), (gain_hbm, gain_ref), (route_hbm, route_ref))
        )
    ]
    for copy in copies:
        copy.start()
    for copy in copies:
        copy.wait()
    row_count, width = rows_ref.shape
    rows = rows_ref[...].astype(jnp.float32)
    scale = lax.rsqrt(jnp.sum(rows * rows, axis=1, keepdims=True) * (1.0 / width) + epsilon)
    normed = (rows * scale * gain_ref[...]).astype(jnp.bfloat16)
    named = [route_ref[0, row] for row in range(row_count)]
    at = lax.broadcasted_iota(jnp.int32, code_ref.shape, 1)
    code = jnp.full(code_ref.shape, -1, jnp.int32)
    for row in range(row_count):
        slot = jnp.int32(0)
        for before in range(row):
            slot = slot + jnp.where(named[before] == named[row], 1, 0)
        code = jnp.where(at == row, named[row] * row_count + slot, code)
    code_ref[...] = code.astype(jnp.float32)
    mine = lax.axis_index("exp") // shards
    height = E_WIN * row_count
    row = lax.broadcasted_iota(jnp.int32, (height, CODE), 0)
    wanted = (mine ^ (row // row_count)) * row_count + row % row_count
    placing = jnp.where(wanted == code[0:1], 1.0, 0.0).astype(jnp.bfloat16)[:, :row_count]
    packed = jnp.dot(placing, normed, preferred_element_type=jnp.float32)
    for expert in range(E_WIN):
        blocks[expert][...] = packed[expert * row_count : (expert + 1) * row_count].astype(
            jnp.bfloat16
        )


def flag_body(owner, after, flags, owner_ref, sems):
    owner_copy = pltpu.make_async_copy(owner, owner_ref, sems.at[0])
    owner_copy.start()
    owner_copy.wait()
    group = lax.axis_index("grp")
    row = lax.broadcasted_iota(jnp.int32, flags.shape, 0)
    values = jnp.zeros(flags.shape, jnp.float32)
    for which in range(PAIR):
        for bucket in range(BUCKETS):
            hit = jnp.where(owner_ref[0, bucket] == (group ^ which), 1.0, 0.0)
            values = jnp.where(row == which * BUCKETS + bucket, hit, values)
    flags[...] = values


def activate_body(devices, weights, code_ref, *refs):
    blocks, out, stacked = refs[:devices], refs[devices], refs[devices + 1]
    row_count = blocks[0].shape[0]
    for index in range(devices):
        stacked[index * row_count : (index + 1) * row_count, :] = blocks[index][...].astype(
            jnp.float32
        )
    rows = stacked[...].astype(jnp.bfloat16)
    gate = lax.dot_general(weights[0], rows, NT, preferred_element_type=jnp.float32)
    up = lax.dot_general(weights[1], rows, NT, preferred_element_type=jnp.float32)
    act = (gate * jax.nn.sigmoid(gate) * up).T
    spare = lax.broadcasted_iota(jnp.int32, (act.shape[0], CODE), 0) == CAP
    out[:, :CODE] = jnp.where(spare, code_ref[0:1, :], act[:, :CODE]).astype(jnp.bfloat16)
    out[:, CODE:] = act[:, CODE:].astype(jnp.bfloat16)


def hold_body(own, other, after, down, sems):
    piece = own.shape[0]
    copies = [
        pltpu.make_async_copy(source, down.at[pl.ds(index * piece, piece)], sems.at[index])
        for index, source in enumerate((own, other))
    ]
    for copy in copies:
        copy.start()
    for copy in copies:
        copy.wait()


def down_body(devices, chips, down, flags, *refs):
    acts, partials = refs[:chips], refs[chips:]
    block, half = partials[0].shape
    used = devices * block
    rows, units = acts[0].shape
    row_count, piece = rows // devices, units // BUCKETS
    row = lax.broadcasted_iota(jnp.int32, (2 * used, rows), 0)
    column = lax.broadcasted_iota(jnp.int32, (2 * used, rows), 1)
    lower, within = row // used, row % used
    home, spot = within // block, within % block
    slot, part, chip_at = spot // (2 * chips), (spot % (2 * chips)) // chips, spot % chips
    matches = (part == lower) & (home == column // row_count) & (slot == column % row_count)
    placed = jnp.zeros((2 * used, PAIR * piece), jnp.float32)
    for chip in range(chips):
        picked = []
        for which in range(PAIR):
            chosen = jnp.zeros((rows, piece), jnp.float32)
            for bucket in range(BUCKETS):
                flag = flags[which * BUCKETS + bucket : which * BUCKETS + bucket + 1, 0:piece]
                piece_of = acts[chip][:, bucket * piece : (bucket + 1) * piece].astype(jnp.float32)
                chosen = jnp.where(flag > 0.5, piece_of, chosen)
            picked.append(chosen.astype(jnp.bfloat16))
        placing = jnp.where(matches & (chip_at == chip), 1.0, 0.0).astype(jnp.bfloat16)
        placed = placed + jnp.dot(
            placing, jnp.concatenate(picked, axis=1), preferred_element_type=jnp.float32
        )
    placed = placed.astype(jnp.bfloat16)
    above, below = placed[:used], placed[used:]
    step = half // 7 if half % (7 * 128) == 0 else half
    for start in range(0, half, step):
        out = jnp.dot(above, down[:, start : start + step], preferred_element_type=jnp.float32)
        out = out + jnp.dot(
            below, down[:, half + start : half + start + step], preferred_element_type=jnp.float32
        )
        for index in range(devices):
            partials[index][:, start : start + step] = out[
                index * block : (index + 1) * block
            ].astype(jnp.bfloat16)


def combine_body(devices, chips, shards, *refs):
    acts, blocks = refs[:chips], refs[chips : chips + devices]
    outs, codes = refs[chips + devices : -1], refs[-1]
    block, half = blocks[0].shape
    row_count = outs[0].shape[0]
    mine = lax.axis_index("exp") // shards
    diagonal = lax.broadcasted_iota(jnp.int32, (row_count, CODE), 0) == lax.broadcasted_iota(
        jnp.int32, (row_count, CODE), 1
    )
    for chip in range(chips):
        line = acts[chip][:, :CODE].astype(jnp.float32)[CAP : CAP + 1, :]
        mark = jnp.sum(jnp.where(diagonal, line, 0.0), axis=1, keepdims=True)
        codes[chip * row_count : (chip + 1) * row_count, :] = jnp.broadcast_to(
            mark, (row_count, CODE)
        )
    code = codes[...]
    home = lax.broadcasted_iota(jnp.int32, code.shape, 0) // row_count
    at = lax.broadcasted_iota(jnp.int32, code.shape, 1)
    at_slot, at_part, at_chip = at // (2 * chips), (at % (2 * chips)) // chips, at % chips
    placing = []
    for expert in range(E_WIN):
        wanted = ((mine ^ expert) * row_count + at_slot).astype(jnp.float32)
        chosen = (wanted == code) & (at_chip == home) & (at < block)
        placing.append(
            [
                jnp.where(chosen & (at_part == part), 1.0, 0.0).astype(jnp.bfloat16)[:, :block]
                for part in range(2)
            ]
        )
    for part in range(2):
        total = 0.0
        for index in range(devices):
            total = total + jnp.dot(
                placing[index // shards][part],
                blocks[index][...],
                preferred_element_type=jnp.float32,
            )
        for chip in range(chips):
            outs[chip][:, part * half : (part + 1) * half] = total[
                chip * row_count : (chip + 1) * row_count
            ].astype(outs[chip].dtype)


def exchange(values, axis, unit):
    moved = [values[0]]
    for bits in range(1, len(values)):
        moved.append(swap(values[bits], axis, bits * unit))
    return moved


def move_rows(hidden, norm_gain, route, route_weight, resident, sectioned, owner):
    rows, own_piece = hidden[0], sectioned[0]
    row_count, width = rows.shape
    devices = lax.axis_size("exp")
    chips = lax.axis_size("grp") // PAIR
    shards = devices // E_WIN
    half, block = width // 2, 2 * CAP * chips
    piece, units = own_piece.shape[0], resident.shape[1]
    row_block = pltpu.VMEM((row_count, width), jnp.bfloat16)
    *packed, code = pl.pallas_call(
        functools.partial(prepare_body, shards),
        out_shape=[row_block] * E_WIN + [pltpu.VMEM((8, CODE), jnp.float32)],
        in_specs=[HBM] * 3,
        out_specs=[VMEM] * (E_WIN + 1),
        scratch_shapes=[
            pltpu.SMEM((1, row_count), jnp.int32),
            pltpu.VMEM((row_count, width), jnp.bfloat16),
            pltpu.VMEM((1, width), jnp.float32),
            pltpu.SemaphoreType.DMA((3,)),
        ],
        compiler_params=limit(4),
        name="prepare",
    )(*in_hbm(route.reshape(1, row_count), rows, norm_gain.reshape(1, width)))
    arrived = exchange([packed[bits // shards] for bits in range(devices)], "exp", 1)
    other_piece = swap(own_piece, "grp", 1)
    weights = swap(resident, "grp", 0)
    flags = pl.pallas_call(
        flag_body,
        out_shape=pltpu.VMEM((8, CODE), jnp.float32),
        in_specs=[HBM, ANY],
        out_specs=VMEM,
        scratch_shapes=[
            pltpu.SMEM((1, owner.shape[0]), jnp.int32),
            pltpu.SemaphoreType.DMA((1,)),
        ],
        compiler_params=limit(2),
        name="flag",
    )(*in_hbm(owner.reshape(1, -1)), *held(code))
    act = pl.pallas_call(
        functools.partial(activate_body, devices),
        out_shape=pltpu.VMEM((devices * row_count, units), jnp.bfloat16),
        in_specs=[VMEM] * (2 + devices),
        out_specs=VMEM,
        scratch_shapes=[pltpu.VMEM((devices * row_count, width), jnp.float32)],
        compiler_params=limit(8),
        name="activate",
    )(*held(weights, code, *arrived))
    acts = exchange([act] * chips, "grp", PAIR)
    down = pl.pallas_call(
        hold_body,
        out_shape=pltpu.VMEM((PAIR * piece, width), jnp.bfloat16),
        in_specs=[HBM, ANY, ANY],
        out_specs=VMEM,
        scratch_shapes=[pltpu.SemaphoreType.DMA((PAIR,))],
        compiler_params=limit(2),
        name="hold",
    )(*in_hbm(own_piece), *held(other_piece, act))
    half_block = pltpu.VMEM((block, half), jnp.bfloat16)
    partials = pl.pallas_call(
        functools.partial(down_body, devices, chips),
        out_shape=[half_block] * devices,
        in_specs=[VMEM] * (2 + chips),
        out_specs=[VMEM] * devices,
        compiler_params=limit(12),
        name="down",
    )(*held(down, flags, *acts))
    returned = exchange(partials, "exp", 1)
    sums = pl.pallas_call(
        functools.partial(combine_body, devices, chips, shards),
        out_shape=[row_block] * chips,
        in_specs=[VMEM] * (chips + devices),
        out_specs=[VMEM] * chips,
        scratch_shapes=[pltpu.VMEM((chips * row_count, CODE), jnp.float32)],
        compiler_params=limit(8),
        name="combine",
    )(*held(*acts, *returned))
    combined = 0.0
    for share in exchange(sums, "grp", PAIR):
        combined = combined + share.astype(jnp.float32)
    result = (combined * route_weight[0][:, None]).astype(jnp.bfloat16)
    return result.reshape(1, row_count, width)


def per_device(hidden, norm_gain, route, route_weight, resident, sectioned, owner):
    weight_rows = BUCKETS * sectioned.shape[1]
    partial_rows = lax.axis_size("exp") * lax.axis_size("grp") // PAIR * hidden.shape[1]
    plan = move_rows if partial_rows < weight_rows else move_weights
    return plan(hidden, norm_gain, route, route_weight, resident, sectioned, owner)


def solution(mesh):
    in_specs = (
        P("grp", "exp", None),
        P(),
        P("grp", "exp", None),
        P("grp", "exp"),
        P(None, "exp", None),
        P("grp", "exp", None),
        P(),
    )
    out_specs = P("grp", "exp", None)
    return jax.shard_map(
        per_device, mesh=mesh, in_specs=in_specs, out_specs=out_specs, check_vma=False
    )
```

```python
import functools

import jax
import jax.numpy as jnp
from jax import lax
from jax.experimental import pallas as pl
from jax.experimental.pallas import tpu as pltpu
from jax.sharding import PartitionSpec as P


E_WIN = 2
BUCKETS = 4
CAP = 3
PAIR = 2


epsilon = 1e-06


def from_root(value, axis, source):
    kept = jnp.where(lax.axis_index(axis) == source, value, 0).astype(value.dtype)
    return lax.psum(kept, axis)


def activate(slot_rows, gate_up):
    gate_part = lax.dot_general(
        slot_rows, gate_up[0], (((1,), (1,)), ((), ())), preferred_element_type=jnp.float32
    )
    up_part = lax.dot_general(
        slot_rows, gate_up[1], (((1,), (1,)), ((), ())), preferred_element_type=jnp.float32
    )
    return (jax.nn.silu(gate_part) * up_part).astype(jnp.bfloat16)


def normalize(rows, norm_gain):
    row_data = rows.astype(jnp.float32)
    scale = lax.rsqrt(jnp.mean(row_data * row_data, axis=1, keepdims=True) + epsilon)
    return (row_data * scale * norm_gain[None, :]).astype(jnp.bfloat16)


def move_weights(hidden, norm_gain, route, route_weight, resident, sectioned, owner):
    normed = normalize(hidden[0], norm_gain)
    row_count, width = normed.shape
    devices = lax.axis_size("exp")
    shards = devices // E_WIN
    expert_ids = route[0, :, 0]
    onehot = (expert_ids[:, None] == jnp.arange(E_WIN, dtype=jnp.int32)[None, :]).astype(jnp.int32)
    position = jnp.cumsum(onehot, axis=0) - onehot
    slot_index = jnp.sum(position * onehot, axis=1)
    placing = onehot[:, :, None] * (
        slot_index[:, None, None] == jnp.arange(CAP, dtype=jnp.int32)[None, None, :]
    ).astype(jnp.int32)
    placing = placing.reshape(row_count, E_WIN * CAP)
    packed = jnp.dot(
        placing.astype(jnp.bfloat16).T, normed, preferred_element_type=jnp.float32
    ).astype(jnp.bfloat16)
    packed = packed.reshape(E_WIN, 1, CAP, width)
    outgoing = jnp.broadcast_to(packed, (E_WIN, shards, CAP, width)).reshape(devices, CAP, width)
    piece_rows = sectioned.shape[1]
    arrived = lax.all_to_all(outgoing, "exp", split_axis=0, concat_axis=0, tiled=True)
    flat_slots = arrived.reshape(-1, width)
    activation = activate(flat_slots, resident)
    running_sum = jnp.zeros((flat_slots.shape[0], width), jnp.float32)
    for bucket in range(BUCKETS):
        weight_piece = from_root(sectioned[0], "grp", owner[bucket])
        act_piece = activation[:, bucket * piece_rows : (bucket + 1) * piece_rows]
        running_sum = running_sum + jnp.dot(
            act_piece, weight_piece, preferred_element_type=jnp.float32
        )
    partials = running_sum.astype(jnp.bfloat16).reshape(arrived.shape)
    returned = lax.all_to_all(partials, "exp", split_axis=0, concat_axis=0, tiled=True)
    summed = jnp.sum(returned.astype(jnp.float32).reshape(E_WIN, shards, CAP, width), axis=1)
    summed = summed.reshape(E_WIN * CAP, width)
    combined = jnp.dot(placing.astype(jnp.float32), summed, precision=lax.Precision.HIGHEST)
    result = (combined * route_weight[0][:, None]).astype(jnp.bfloat16)
    return result.reshape(1, row_count, width)


def swap(value, axis, bits):
    size = lax.axis_size(axis)
    return lax.ppermute(value, axis, [(i, i ^ bits) for i in range(size)])


NT = (((1,), (1,)), ((), ()))
VMEM = pl.BlockSpec(memory_space=pltpu.VMEM)
ANY = pl.BlockSpec(memory_space=pl.ANY)
HBM = pl.BlockSpec(memory_space=pltpu.HBM)
CODE = 128
MIB = 1 << 20


def held(*values):
    return [pltpu.with_memory_space_constraint(value, pltpu.VMEM) for value in values]


def in_hbm(*values):
    return [pltpu.with_memory_space_constraint(value, pltpu.HBM) for value in values]


def limit(mib):
    return pltpu.CompilerParams(vmem_limit_bytes=mib * MIB)


def prepare_body(shards, route_hbm, rows_hbm, gain_hbm, resident, *refs):
    blocks, code_ref, early = refs[:E_WIN], refs[E_WIN], refs[E_WIN + 1]
    route_ref, rows_ref, gain_ref, sems = refs[E_WIN + 2 :]
    early_copy = pltpu.make_async_copy(
        resident.at[:, pl.ds(0, early.shape[1])], early, sems.at[3]
    )
    copies = [
        pltpu.make_async_copy(source, target, sems.at[index])
        for index, (source, target) in enumerate(
            ((rows_hbm, rows_ref), (gain_hbm, gain_ref), (route_hbm, route_ref))
        )
    ]
    for copy in copies:
        copy.start()
    early_copy.start()
    for copy in copies:
        copy.wait()
    row_count, width = rows_ref.shape
    rows = rows_ref[...].astype(jnp.float32)
    scale = lax.rsqrt(jnp.sum(rows * rows, axis=1, keepdims=True) * (1.0 / width) + epsilon)
    normed = (rows * scale * gain_ref[...]).astype(jnp.bfloat16)
    named = [route_ref[0, row] for row in range(row_count)]
    at = lax.broadcasted_iota(jnp.int32, code_ref.shape, 1)
    code = jnp.full(code_ref.shape, -1, jnp.int32)
    for row in range(row_count):
        slot = jnp.int32(0)
        for before in range(row):
            slot = slot + jnp.where(named[before] == named[row], 1, 0)
        code = jnp.where(at == row, named[row] * row_count + slot, code)
    code_ref[...] = code.astype(jnp.float32)
    mine = lax.axis_index("exp") // shards
    height = E_WIN * row_count
    row = lax.broadcasted_iota(jnp.int32, (height, CODE), 0)
    wanted = (mine ^ (row // row_count)) * row_count + row % row_count
    placing = jnp.where(wanted == code[0:1], 1.0, 0.0).astype(jnp.bfloat16)[:, :row_count]
    packed = jnp.dot(placing, normed, preferred_element_type=jnp.float32)
    for expert in range(E_WIN):
        blocks[expert][...] = packed[expert * row_count : (expert + 1) * row_count].astype(
            jnp.bfloat16
        )
    early_copy.wait()


def ahead_body(owner, resident, after, late, flags, owner_ref, sems):
    late_rows = late.shape[1]
    late_copy = pltpu.make_async_copy(
        resident.at[:, pl.ds(resident.shape[1] - late_rows, late_rows)], late, sems.at[0]
    )
    late_copy.start()
    owner_copy = pltpu.make_async_copy(owner, owner_ref, sems.at[1])
    owner_copy.start()
    owner_copy.wait()
    group = lax.axis_index("grp")
    row = lax.broadcasted_iota(jnp.int32, flags.shape, 0)
    values = jnp.zeros(flags.shape, jnp.float32)
    for which in range(PAIR):
        for bucket in range(BUCKETS):
            hit = jnp.where(owner_ref[0, bucket] == (group ^ which), 1.0, 0.0)
            values = jnp.where(row == which * BUCKETS + bucket, hit, values)
    flags[...] = values
    late_copy.wait()


def activate_body(devices, early, late, code_ref, *refs):
    blocks, out, stacked = refs[:devices], refs[devices], refs[devices + 1]
    first = early.shape[1]
    row_count = blocks[0].shape[0]
    for index in range(devices):
        stacked[index * row_count : (index + 1) * row_count, :] = blocks[index][...].astype(
            jnp.float32
        )
    rows = stacked[...].astype(jnp.bfloat16)
    spare = lax.broadcasted_iota(jnp.int32, (devices * row_count, CODE), 0) == CAP
    for start, weights in ((0, early), (first, late)):
        gate = lax.dot_general(weights[0], rows, NT, preferred_element_type=jnp.float32)
        up = lax.dot_general(weights[1], rows, NT, preferred_element_type=jnp.float32)
        act = (gate * jax.nn.sigmoid(gate) * up).T
        out[:, start : start + act.shape[1]] = act.astype(jnp.bfloat16)
    head = out[:, :CODE].astype(jnp.float32)
    out[:, :CODE] = jnp.where(spare, code_ref[0:1, :], head).astype(jnp.bfloat16)


def hold_body(chips, row_count, own, other, after, down, placing, sems):
    piece = own.shape[0]
    copies = [
        pltpu.make_async_copy(source, down.at[pl.ds(index * piece, piece)], sems.at[index])
        for index, source in enumerate((own, other))
    ]
    for copy in copies:
        copy.start()
    shape = placing.shape[1:]
    row, column = (lax.broadcasted_iota(jnp.int32, shape, axis) for axis in (0, 1))
    block, used = 2 * CAP * chips, shape[0] // 2
    lower, home, spot = row // used, (row % used) // block, row % block
    slot, part, at = spot // (2 * chips), (spot % (2 * chips)) // chips, spot % chips
    matches = (part == lower) & (home == column // row_count) & (slot == column % row_count)
    for chip in range(chips):
        placing[chip] = jnp.where(matches & (at == chip), 1.0, 0.0).astype(jnp.bfloat16)
    for copy in copies:
        copy.wait()


def down_body(devices, chips, down, flags, placing, *refs):
    acts, partials = refs[:chips], refs[chips:]
    block, half = partials[0].shape
    used = devices * block
    rows, units = acts[0].shape
    piece = units // BUCKETS
    placed = jnp.zeros((2 * used, PAIR * piece), jnp.float32)
    for chip in range(chips):
        picked = []
        for which in range(PAIR):
            chosen = jnp.zeros((rows, piece), jnp.float32)
            for bucket in range(BUCKETS):
                flag = flags[which * BUCKETS + bucket : which * BUCKETS + bucket + 1, 0:piece]
                piece_of = acts[chip][:, bucket * piece : (bucket + 1) * piece].astype(jnp.float32)
                chosen = jnp.where(flag > 0.5, piece_of, chosen)
            picked.append(chosen.astype(jnp.bfloat16))
        placed = placed + jnp.dot(
            placing[chip], jnp.concatenate(picked, axis=1), preferred_element_type=jnp.float32
        )
    placed = placed.astype(jnp.bfloat16)
    above, below = placed[:used], placed[used:]
    step = half // 7 if half % (7 * 128) == 0 else half
    for start in range(0, half, step):
        out = jnp.dot(above, down[:, start : start + step], preferred_element_type=jnp.float32)
        out = out + jnp.dot(
            below, down[:, half + start : half + start + step], preferred_element_type=jnp.float32
        )
        for index in range(devices):
            partials[index][:, start : start + step] = out[
                index * block : (index + 1) * block
            ].astype(jnp.bfloat16)


def place_body(chips, shards, row_count, block, *refs):
    acts, placing, codes = refs[:chips], refs[-2], refs[-1]
    mine = lax.axis_index("exp") // shards
    diagonal = lax.broadcasted_iota(jnp.int32, (row_count, CODE), 0) == lax.broadcasted_iota(
        jnp.int32, (row_count, CODE), 1
    )
    for chip in range(chips):
        line = acts[chip][:, :CODE].astype(jnp.float32)[CAP : CAP + 1, :]
        mark = jnp.sum(jnp.where(diagonal, line, 0.0), axis=1, keepdims=True)
        codes[chip * row_count : (chip + 1) * row_count, :] = jnp.broadcast_to(
            mark, (row_count, CODE)
        )
    code = codes[...]
    home = lax.broadcasted_iota(jnp.int32, code.shape, 0) // row_count
    at = lax.broadcasted_iota(jnp.int32, code.shape, 1)
    at_slot, at_part, at_chip = at // (2 * chips), (at % (2 * chips)) // chips, at % chips
    for expert in range(E_WIN):
        wanted = ((mine ^ expert) * row_count + at_slot).astype(jnp.float32)
        chosen = (wanted == code) & (at_chip == home) & (at < block)
        for part in range(2):
            placing[2 * expert + part] = jnp.where(chosen & (at_part == part), 1.0, 0.0).astype(
                jnp.bfloat16
            )


def combine_body(devices, chips, shards, placing, *refs):
    blocks, outs = refs[:devices], refs[devices:]
    block, half = blocks[0].shape
    row_count = outs[0].shape[0]
    for part in range(2):
        total = 0.0
        for index in range(devices):
            total = total + jnp.dot(
                placing[2 * (index // shards) + part][:, :block],
                blocks[index][...],
                preferred_element_type=jnp.float32,
            )
        for chip in range(chips):
            outs[chip][:, part * half : (part + 1) * half] = total[
                chip * row_count : (chip + 1) * row_count
            ].astype(outs[chip].dtype)


def exchange(values, axis, unit):
    moved = [values[0]]
    for bits in range(1, len(values)):
        moved.append(swap(values[bits], axis, bits * unit))
    return moved


def move_rows(hidden, norm_gain, route, route_weight, resident, sectioned, owner):
    rows, own_piece = hidden[0], sectioned[0]
    row_count, width = rows.shape
    devices = lax.axis_size("exp")
    chips = lax.axis_size("grp") // PAIR
    shards = devices // E_WIN
    half, block = width // 2, 2 * CAP * chips
    piece, units = own_piece.shape[0], resident.shape[1]
    early_units = units // 8
    row_block = pltpu.VMEM((row_count, width), jnp.bfloat16)
    *packed, code, early = pl.pallas_call(
        functools.partial(prepare_body, shards),
        out_shape=[row_block] * E_WIN
        + [
            pltpu.VMEM((8, CODE), jnp.float32),
            pltpu.VMEM((2, early_units, width), jnp.bfloat16),
        ],
        in_specs=[HBM] * 4,
        out_specs=[VMEM] * (E_WIN + 2),
        scratch_shapes=[
            pltpu.SMEM((1, row_count), jnp.int32),
            pltpu.VMEM((row_count, width), jnp.bfloat16),
            pltpu.VMEM((1, width), jnp.float32),
            pltpu.SemaphoreType.DMA((4,)),
        ],
        compiler_params=limit(4),
        name="prepare",
    )(*in_hbm(route.reshape(1, row_count), rows, norm_gain.reshape(1, width), resident))
    arrived = exchange([packed[bits // shards] for bits in range(devices)], "exp", 1)
    other_piece = swap(own_piece, "grp", 1)
    late, flags = pl.pallas_call(
        ahead_body,
        out_shape=[
            pltpu.VMEM((2, units - early_units, width), jnp.bfloat16),
            pltpu.VMEM((8, CODE), jnp.float32),
        ],
        in_specs=[HBM, HBM, ANY],
        out_specs=[VMEM] * 2,
        scratch_shapes=[
            pltpu.SMEM((1, owner.shape[0]), jnp.int32),
            pltpu.SemaphoreType.DMA((2,)),
        ],
        compiler_params=limit(2),
        name="ahead",
    )(*in_hbm(owner.reshape(1, -1), resident), *held(code))
    act = pl.pallas_call(
        functools.partial(activate_body, devices),
        out_shape=pltpu.VMEM((devices * row_count, units), jnp.bfloat16),
        in_specs=[VMEM] * (3 + devices),
        out_specs=VMEM,
        scratch_shapes=[pltpu.VMEM((devices * row_count, width), jnp.float32)],
        compiler_params=limit(8),
        name="activate",
    )(*held(early, late, code, *arrived))
    acts = exchange([act] * chips, "grp", PAIR)
    down, placing = pl.pallas_call(
        functools.partial(hold_body, chips, row_count),
        out_shape=[
            pltpu.VMEM((PAIR * piece, width), jnp.bfloat16),
            pltpu.VMEM((chips, 2 * devices * block, devices * row_count), jnp.bfloat16),
        ],
        in_specs=[HBM, ANY, ANY],
        out_specs=[VMEM] * 2,
        scratch_shapes=[pltpu.SemaphoreType.DMA((PAIR,))],
        compiler_params=limit(2),
        name="hold",
    )(*in_hbm(own_piece), *held(other_piece, act))
    half_block = pltpu.VMEM((block, half), jnp.bfloat16)
    partials = pl.pallas_call(
        functools.partial(down_body, devices, chips),
        out_shape=[half_block] * devices,
        in_specs=[VMEM] * (3 + chips),
        out_specs=[VMEM] * devices,
        compiler_params=limit(12),
        name="down",
    )(*held(down, flags, placing, *acts))
    returned = exchange(partials, "exp", 1)
    placing = pl.pallas_call(
        functools.partial(place_body, chips, shards, row_count, block),
        out_shape=pltpu.VMEM((2 * E_WIN, chips * row_count, CODE), jnp.bfloat16),
        in_specs=[VMEM] * chips + [ANY],
        out_specs=VMEM,
        scratch_shapes=[pltpu.VMEM((chips * row_count, CODE), jnp.float32)],
        compiler_params=limit(2),
        name="place",
    )(*held(*acts, partials[0]))
    sums = pl.pallas_call(
        functools.partial(combine_body, devices, chips, shards),
        out_shape=[row_block] * chips,
        in_specs=[VMEM] * (1 + devices),
        out_specs=[VMEM] * chips,
        compiler_params=limit(8),
        name="combine",
    )(*held(placing, *returned))
    combined = 0.0
    for share in exchange(sums, "grp", PAIR):
        combined = combined + share.astype(jnp.float32)
    result = (combined * route_weight[0][:, None]).astype(jnp.bfloat16)
    return result.reshape(1, row_count, width)


def per_device(hidden, norm_gain, route, route_weight, resident, sectioned, owner):
    weight_rows = BUCKETS * sectioned.shape[1]
    partial_rows = lax.axis_size("exp") * lax.axis_size("grp") // PAIR * hidden.shape[1]
    plan = move_rows if partial_rows < weight_rows else move_weights
    return plan(hidden, norm_gain, route, route_weight, resident, sectioned, owner)


def solution(mesh):
    in_specs = (
        P("grp", "exp", None),
        P(),
        P("grp", "exp", None),
        P("grp", "exp"),
        P(None, "exp", None),
        P("grp", "exp", None),
        P(),
    )
    out_specs = P("grp", "exp", None)
    return jax.shard_map(
        per_device, mesh=mesh, in_specs=in_specs, out_specs=out_specs, check_vma=False
    )
```

```python
import functools

import jax
import jax.numpy as jnp
from jax import lax
from jax.experimental import pallas as pl
from jax.experimental.pallas import tpu as pltpu
from jax.sharding import PartitionSpec as P


E_WIN = 2
BUCKETS = 4
CAP = 3
PAIR = 2


epsilon = 1e-06


def from_root(value, axis, source):
    kept = jnp.where(lax.axis_index(axis) == source, value, 0).astype(value.dtype)
    return lax.psum(kept, axis)


def activate(slot_rows, gate_up):
    gate_part = lax.dot_general(
        slot_rows, gate_up[0], (((1,), (1,)), ((), ())), preferred_element_type=jnp.float32
    )
    up_part = lax.dot_general(
        slot_rows, gate_up[1], (((1,), (1,)), ((), ())), preferred_element_type=jnp.float32
    )
    return (jax.nn.silu(gate_part) * up_part).astype(jnp.bfloat16)


def normalize(rows, norm_gain):
    row_data = rows.astype(jnp.float32)
    scale = lax.rsqrt(jnp.mean(row_data * row_data, axis=1, keepdims=True) + epsilon)
    return (row_data * scale * norm_gain[None, :]).astype(jnp.bfloat16)


def move_weights(hidden, norm_gain, route, route_weight, resident, sectioned, owner):
    normed = normalize(hidden[0], norm_gain)
    row_count, width = normed.shape
    devices = lax.axis_size("exp")
    shards = devices // E_WIN
    expert_ids = route[0, :, 0]
    onehot = (expert_ids[:, None] == jnp.arange(E_WIN, dtype=jnp.int32)[None, :]).astype(jnp.int32)
    position = jnp.cumsum(onehot, axis=0) - onehot
    slot_index = jnp.sum(position * onehot, axis=1)
    placing = onehot[:, :, None] * (
        slot_index[:, None, None] == jnp.arange(CAP, dtype=jnp.int32)[None, None, :]
    ).astype(jnp.int32)
    placing = placing.reshape(row_count, E_WIN * CAP)
    packed = jnp.dot(
        placing.astype(jnp.bfloat16).T, normed, preferred_element_type=jnp.float32
    ).astype(jnp.bfloat16)
    packed = packed.reshape(E_WIN, 1, CAP, width)
    outgoing = jnp.broadcast_to(packed, (E_WIN, shards, CAP, width)).reshape(devices, CAP, width)
    piece_rows = sectioned.shape[1]
    arrived = lax.all_to_all(outgoing, "exp", split_axis=0, concat_axis=0, tiled=True)
    flat_slots = arrived.reshape(-1, width)
    activation = activate(flat_slots, resident)
    running_sum = jnp.zeros((flat_slots.shape[0], width), jnp.float32)
    for bucket in range(BUCKETS):
        weight_piece = from_root(sectioned[0], "grp", owner[bucket])
        act_piece = activation[:, bucket * piece_rows : (bucket + 1) * piece_rows]
        running_sum = running_sum + jnp.dot(
            act_piece, weight_piece, preferred_element_type=jnp.float32
        )
    partials = running_sum.astype(jnp.bfloat16).reshape(arrived.shape)
    returned = lax.all_to_all(partials, "exp", split_axis=0, concat_axis=0, tiled=True)
    summed = jnp.sum(returned.astype(jnp.float32).reshape(E_WIN, shards, CAP, width), axis=1)
    summed = summed.reshape(E_WIN * CAP, width)
    combined = jnp.dot(placing.astype(jnp.float32), summed, precision=lax.Precision.HIGHEST)
    result = (combined * route_weight[0][:, None]).astype(jnp.bfloat16)
    return result.reshape(1, row_count, width)


def swap(value, axis, bits):
    size = lax.axis_size(axis)
    return lax.ppermute(value, axis, [(i, i ^ bits) for i in range(size)])


NT = (((1,), (1,)), ((), ()))
VMEM = pl.BlockSpec(memory_space=pltpu.VMEM)
ANY = pl.BlockSpec(memory_space=pl.ANY)
HBM = pl.BlockSpec(memory_space=pltpu.HBM)
CODE = 128
MIB = 1 << 20


def held(*values):
    return [pltpu.with_memory_space_constraint(value, pltpu.VMEM) for value in values]


def in_hbm(*values):
    return [pltpu.with_memory_space_constraint(value, pltpu.HBM) for value in values]


def limit(mib):
    return pltpu.CompilerParams(vmem_limit_bytes=mib * MIB)


def prepare_body(shards, route_hbm, rows_hbm, gain_hbm, *refs):
    blocks, code_ref = refs[:E_WIN], refs[E_WIN]
    route_ref, rows_ref, gain_ref, sems = refs[E_WIN + 1 :]
    copies = [
        pltpu.make_async_copy(source, target, sems.at[index])
        for index, (source, target) in enumerate(
            ((rows_hbm, rows_ref), (gain_hbm, gain_ref), (route_hbm, route_ref))
        )
    ]
    for copy in copies:
        copy.start()
    for copy in copies:
        copy.wait()
    row_count, width = rows_ref.shape
    rows = rows_ref[...].astype(jnp.float32)
    scale = lax.rsqrt(jnp.sum(rows * rows, axis=1, keepdims=True) * (1.0 / width) + epsilon)
    normed = (rows * scale * gain_ref[...]).astype(jnp.bfloat16)
    named = [route_ref[0, row] for row in range(row_count)]
    at = lax.broadcasted_iota(jnp.int32, code_ref.shape, 1)
    code = jnp.full(code_ref.shape, -1, jnp.int32)
    for row in range(row_count):
        slot = jnp.int32(0)
        for before in range(row):
            slot = slot + jnp.where(named[before] == named[row], 1, 0)
        code = jnp.where(at == row, named[row] * row_count + slot, code)
    code_ref[...] = code.astype(jnp.float32)
    mine = lax.axis_index("exp") // shards
    height = E_WIN * row_count
    row = lax.broadcasted_iota(jnp.int32, (height, CODE), 0)
    wanted = (mine ^ (row // row_count)) * row_count + row % row_count
    placing = jnp.where(wanted == code[0:1], 1.0, 0.0).astype(jnp.bfloat16)[:, :row_count]
    packed = jnp.dot(placing, normed, preferred_element_type=jnp.float32)
    for expert in range(E_WIN):
        blocks[expert][...] = packed[expert * row_count : (expert + 1) * row_count].astype(
            jnp.bfloat16
        )


def flag_body(owner, after, flags, owner_ref, sems):
    owner_copy = pltpu.make_async_copy(owner, owner_ref, sems.at[0])
    owner_copy.start()
    owner_copy.wait()
    group = lax.axis_index("grp")
    row = lax.broadcasted_iota(jnp.int32, flags.shape, 0)
    values = jnp.zeros(flags.shape, jnp.float32)
    for which in range(PAIR):
        for bucket in range(BUCKETS):
            hit = jnp.where(owner_ref[0, bucket] == (group ^ which), 1.0, 0.0)
            values = jnp.where(row == which * BUCKETS + bucket, hit, values)
    flags[...] = values


def activate_body(devices, weights, code_ref, *refs):
    blocks, out, stacked = refs[:devices], refs[devices], refs[devices + 1]
    row_count = blocks[0].shape[0]
    for index in range(devices):
        stacked[index * row_count : (index + 1) * row_count, :] = blocks[index][...].astype(
            jnp.float32
        )
    rows = stacked[...].astype(jnp.bfloat16)
    gate = lax.dot_general(weights[0], rows, NT, preferred_element_type=jnp.float32)
    up = lax.dot_general(weights[1], rows, NT, preferred_element_type=jnp.float32)
    act = (gate * jax.nn.sigmoid(gate) * up).T
    spare = lax.broadcasted_iota(jnp.int32, (act.shape[0], CODE), 0) == CAP
    out[:, :CODE] = jnp.where(spare, code_ref[0:1, :], act[:, :CODE]).astype(jnp.bfloat16)
    out[:, CODE:] = act[:, CODE:].astype(jnp.bfloat16)


def hold_body(chips, row_count, own, other, after, down, placing, sems):
    piece = own.shape[0]
    copies = [
        pltpu.make_async_copy(source, down.at[pl.ds(index * piece, piece)], sems.at[index])
        for index, source in enumerate((own, other))
    ]
    for copy in copies:
        copy.start()
    shape = placing.shape[1:]
    row, column = (lax.broadcasted_iota(jnp.int32, shape, axis) for axis in (0, 1))
    block, used = 2 * CAP * chips, shape[0] // 2
    lower, home, spot = row // used, (row % used) // block, row % block
    slot, part, at = spot // (2 * chips), (spot % (2 * chips)) // chips, spot % chips
    matches = (part == lower) & (home == column // row_count) & (slot == column % row_count)
    for chip in range(chips):
        placing[chip] = jnp.where(matches & (at == chip), 1.0, 0.0).astype(jnp.bfloat16)
    for copy in copies:
        copy.wait()


def down_body(devices, chips, down, flags, placing, *refs):
    acts, partials = refs[:chips], refs[chips:]
    block, half = partials[0].shape
    used = devices * block
    rows, units = acts[0].shape
    piece = units // BUCKETS
    placed = jnp.zeros((2 * used, PAIR * piece), jnp.float32)
    for chip in range(chips):
        picked = []
        for which in range(PAIR):
            chosen = jnp.zeros((rows, piece), jnp.float32)
            for bucket in range(BUCKETS):
                flag = flags[which * BUCKETS + bucket : which * BUCKETS + bucket + 1, 0:piece]
                piece_of = acts[chip][:, bucket * piece : (bucket + 1) * piece].astype(jnp.float32)
                chosen = jnp.where(flag > 0.5, piece_of, chosen)
            picked.append(chosen.astype(jnp.bfloat16))
        placed = placed + jnp.dot(
            placing[chip], jnp.concatenate(picked, axis=1), preferred_element_type=jnp.float32
        )
    placed = placed.astype(jnp.bfloat16)
    above, below = placed[:used], placed[used:]
    step = half // 7 if half % (7 * 128) == 0 else half
    for start in range(0, half, step):
        out = jnp.dot(above, down[:, start : start + step], preferred_element_type=jnp.float32)
        out = out + jnp.dot(
            below, down[:, half + start : half + start + step], preferred_element_type=jnp.float32
        )
        for index in range(devices):
            partials[index][:, start : start + step] = out[
                index * block : (index + 1) * block
            ].astype(jnp.bfloat16)


def place_body(chips, shards, row_count, block, *refs):
    acts, placing, codes = refs[:chips], refs[-2], refs[-1]
    mine = lax.axis_index("exp") // shards
    diagonal = lax.broadcasted_iota(jnp.int32, (row_count, CODE), 0) == lax.broadcasted_iota(
        jnp.int32, (row_count, CODE), 1
    )
    for chip in range(chips):
        line = acts[chip][:, :CODE].astype(jnp.float32)[CAP : CAP + 1, :]
        mark = jnp.sum(jnp.where(diagonal, line, 0.0), axis=1, keepdims=True)
        codes[chip * row_count : (chip + 1) * row_count, :] = jnp.broadcast_to(
            mark, (row_count, CODE)
        )
    code = codes[...]
    home = lax.broadcasted_iota(jnp.int32, code.shape, 0) // row_count
    at = lax.broadcasted_iota(jnp.int32, code.shape, 1)
    at_slot, at_part, at_chip = at // (2 * chips), (at % (2 * chips)) // chips, at % chips
    for expert in range(E_WIN):
        wanted = ((mine ^ expert) * row_count + at_slot).astype(jnp.float32)
        chosen = (wanted == code) & (at_chip == home) & (at < block)
        for part in range(2):
            placing[2 * expert + part] = jnp.where(chosen & (at_part == part), 1.0, 0.0).astype(
                jnp.bfloat16
            )


def combine_body(devices, chips, shards, placing, *refs):
    blocks, outs = refs[:devices], refs[devices:]
    block, half = blocks[0].shape
    row_count = outs[0].shape[0]
    for part in range(2):
        total = 0.0
        for index in range(devices):
            total = total + jnp.dot(
                placing[2 * (index // shards) + part][:, :block],
                blocks[index][...],
                preferred_element_type=jnp.float32,
            )
        for chip in range(chips):
            outs[chip][:, part * half : (part + 1) * half] = total[
                chip * row_count : (chip + 1) * row_count
            ].astype(outs[chip].dtype)


def exchange(values, axis, unit):
    moved = [values[0]]
    for bits in range(1, len(values)):
        moved.append(swap(values[bits], axis, bits * unit))
    return moved


def move_rows(hidden, norm_gain, route, route_weight, resident, sectioned, owner):
    rows, own_piece = hidden[0], sectioned[0]
    row_count, width = rows.shape
    devices = lax.axis_size("exp")
    chips = lax.axis_size("grp") // PAIR
    shards = devices // E_WIN
    half, block = width // 2, 2 * CAP * chips
    piece, units = own_piece.shape[0], resident.shape[1]
    row_block = pltpu.VMEM((row_count, width), jnp.bfloat16)
    *packed, code = pl.pallas_call(
        functools.partial(prepare_body, shards),
        out_shape=[row_block] * E_WIN + [pltpu.VMEM((8, CODE), jnp.float32)],
        in_specs=[HBM] * 3,
        out_specs=[VMEM] * (E_WIN + 1),
        scratch_shapes=[
            pltpu.SMEM((1, row_count), jnp.int32),
            pltpu.VMEM((row_count, width), jnp.bfloat16),
            pltpu.VMEM((1, width), jnp.float32),
            pltpu.SemaphoreType.DMA((3,)),
        ],
        compiler_params=limit(4),
        cost_estimate=pl.CostEstimate(flops=10**10, transcendentals=0, bytes_accessed=2 * 10**7),
        name="prepare",
    )(*in_hbm(route.reshape(1, row_count), rows, norm_gain.reshape(1, width)))
    arrived = exchange([packed[bits // shards] for bits in range(devices)], "exp", 1)
    other_piece = swap(own_piece, "grp", 1)
    flags = pl.pallas_call(
        flag_body,
        out_shape=pltpu.VMEM((8, CODE), jnp.float32),
        in_specs=[HBM, ANY],
        out_specs=VMEM,
        scratch_shapes=[
            pltpu.SMEM((1, owner.shape[0]), jnp.int32),
            pltpu.SemaphoreType.DMA((1,)),
        ],
        compiler_params=limit(2),
        name="flag",
    )(*in_hbm(owner.reshape(1, -1)), *held(code))
    act = pl.pallas_call(
        functools.partial(activate_body, devices),
        out_shape=pltpu.VMEM((devices * row_count, units), jnp.bfloat16),
        in_specs=[VMEM] * (2 + devices),
        out_specs=VMEM,
        scratch_shapes=[pltpu.VMEM((devices * row_count, width), jnp.float32)],
        compiler_params=limit(20),
        name="activate",
    )(resident, *held(code, *arrived))
    acts = exchange([act] * chips, "grp", PAIR)
    down, placing = pl.pallas_call(
        functools.partial(hold_body, chips, row_count),
        out_shape=[
            pltpu.VMEM((PAIR * piece, width), jnp.bfloat16),
            pltpu.VMEM((chips, 2 * devices * block, devices * row_count), jnp.bfloat16),
        ],
        in_specs=[HBM, ANY, ANY],
        out_specs=[VMEM] * 2,
        scratch_shapes=[pltpu.SemaphoreType.DMA((PAIR,))],
        compiler_params=limit(2),
        name="hold",
    )(*in_hbm(own_piece), *held(other_piece, act))
    half_block = pltpu.VMEM((block, half), jnp.bfloat16)
    partials = pl.pallas_call(
        functools.partial(down_body, devices, chips),
        out_shape=[half_block] * devices,
        in_specs=[VMEM] * (3 + chips),
        out_specs=[VMEM] * devices,
        compiler_params=limit(12),
        name="down",
    )(*held(down, flags, placing, *acts))
    returned = exchange(partials, "exp", 1)
    placing = pl.pallas_call(
        functools.partial(place_body, chips, shards, row_count, block),
        out_shape=pltpu.VMEM((2 * E_WIN, chips * row_count, CODE), jnp.bfloat16),
        in_specs=[VMEM] * chips + [ANY],
        out_specs=VMEM,
        scratch_shapes=[pltpu.VMEM((chips * row_count, CODE), jnp.float32)],
        compiler_params=limit(2),
        name="place",
    )(*held(*acts, partials[0]))
    sums = pl.pallas_call(
        functools.partial(combine_body, devices, chips, shards),
        out_shape=[row_block] * chips,
        in_specs=[VMEM] * (1 + devices),
        out_specs=[VMEM] * chips,
        compiler_params=limit(8),
        name="combine",
    )(*held(placing, *returned))
    combined = 0.0
    for share in exchange(sums, "grp", PAIR):
        combined = combined + share.astype(jnp.float32)
    result = (combined * route_weight[0][:, None]).astype(jnp.bfloat16)
    return result.reshape(1, row_count, width)


def per_device(hidden, norm_gain, route, route_weight, resident, sectioned, owner):
    weight_rows = BUCKETS * sectioned.shape[1]
    partial_rows = lax.axis_size("exp") * lax.axis_size("grp") // PAIR * hidden.shape[1]
    plan = move_rows if partial_rows < weight_rows else move_weights
    return plan(hidden, norm_gain, route, route_weight, resident, sectioned, owner)


def solution(mesh):
    in_specs = (
        P("grp", "exp", None),
        P(),
        P("grp", "exp", None),
        P("grp", "exp"),
        P(None, "exp", None),
        P("grp", "exp", None),
        P(),
    )
    out_specs = P("grp", "exp", None)
    return jax.shard_map(
        per_device, mesh=mesh, in_specs=in_specs, out_specs=out_specs, check_vma=False
    )
```

```python
import functools

import jax
import jax.numpy as jnp
from jax import lax
from jax.experimental import pallas as pl
from jax.experimental.pallas import tpu as pltpu
from jax.sharding import PartitionSpec as P


E_WIN = 2
BUCKETS = 4
CAP = 3
PAIR = 2


epsilon = 1e-06


def from_root(value, axis, source):
    kept = jnp.where(lax.axis_index(axis) == source, value, 0).astype(value.dtype)
    return lax.psum(kept, axis)


def activate(slot_rows, gate_up):
    gate_part = lax.dot_general(
        slot_rows, gate_up[0], (((1,), (1,)), ((), ())), preferred_element_type=jnp.float32
    )
    up_part = lax.dot_general(
        slot_rows, gate_up[1], (((1,), (1,)), ((), ())), preferred_element_type=jnp.float32
    )
    return (jax.nn.silu(gate_part) * up_part).astype(jnp.bfloat16)


def normalize(rows, norm_gain):
    row_data = rows.astype(jnp.float32)
    scale = lax.rsqrt(jnp.mean(row_data * row_data, axis=1, keepdims=True) + epsilon)
    return (row_data * scale * norm_gain[None, :]).astype(jnp.bfloat16)


def move_weights(hidden, norm_gain, route, route_weight, resident, sectioned, owner):
    normed = normalize(hidden[0], norm_gain)
    row_count, width = normed.shape
    devices = lax.axis_size("exp")
    shards = devices // E_WIN
    expert_ids = route[0, :, 0]
    onehot = (expert_ids[:, None] == jnp.arange(E_WIN, dtype=jnp.int32)[None, :]).astype(jnp.int32)
    position = jnp.cumsum(onehot, axis=0) - onehot
    slot_index = jnp.sum(position * onehot, axis=1)
    placing = onehot[:, :, None] * (
        slot_index[:, None, None] == jnp.arange(CAP, dtype=jnp.int32)[None, None, :]
    ).astype(jnp.int32)
    placing = placing.reshape(row_count, E_WIN * CAP)
    packed = jnp.dot(
        placing.astype(jnp.bfloat16).T, normed, preferred_element_type=jnp.float32
    ).astype(jnp.bfloat16)
    packed = packed.reshape(E_WIN, 1, CAP, width)
    outgoing = jnp.broadcast_to(packed, (E_WIN, shards, CAP, width)).reshape(devices, CAP, width)
    piece_rows = sectioned.shape[1]
    arrived = lax.all_to_all(outgoing, "exp", split_axis=0, concat_axis=0, tiled=True)
    flat_slots = arrived.reshape(-1, width)
    activation = activate(flat_slots, resident)
    running_sum = jnp.zeros((flat_slots.shape[0], width), jnp.float32)
    for bucket in range(BUCKETS):
        weight_piece = from_root(sectioned[0], "grp", owner[bucket])
        act_piece = activation[:, bucket * piece_rows : (bucket + 1) * piece_rows]
        running_sum = running_sum + jnp.dot(
            act_piece, weight_piece, preferred_element_type=jnp.float32
        )
    partials = running_sum.astype(jnp.bfloat16).reshape(arrived.shape)
    returned = lax.all_to_all(partials, "exp", split_axis=0, concat_axis=0, tiled=True)
    summed = jnp.sum(returned.astype(jnp.float32).reshape(E_WIN, shards, CAP, width), axis=1)
    summed = summed.reshape(E_WIN * CAP, width)
    combined = jnp.dot(placing.astype(jnp.float32), summed, precision=lax.Precision.HIGHEST)
    result = (combined * route_weight[0][:, None]).astype(jnp.bfloat16)
    return result.reshape(1, row_count, width)


def swap(value, axis, bits):
    size = lax.axis_size(axis)
    return lax.ppermute(value, axis, [(i, i ^ bits) for i in range(size)])


NT = (((1,), (1,)), ((), ()))
VMEM = pl.BlockSpec(memory_space=pltpu.VMEM)
ANY = pl.BlockSpec(memory_space=pl.ANY)
HBM = pl.BlockSpec(memory_space=pltpu.HBM)
CODE = 128
MIB = 1 << 20


def held(*values):
    return [pltpu.with_memory_space_constraint(value, pltpu.VMEM) for value in values]


def in_hbm(*values):
    return [pltpu.with_memory_space_constraint(value, pltpu.HBM) for value in values]


def limit(mib):
    return pltpu.CompilerParams(vmem_limit_bytes=mib * MIB)


def prepare_body(shards, route_hbm, rows_hbm, gain_hbm, *refs):
    blocks, code_ref = refs[:E_WIN], refs[E_WIN]
    route_ref, rows_ref, gain_ref, sems = refs[E_WIN + 1 :]
    copies = [
        pltpu.make_async_copy(source, target, sems.at[index])
        for index, (source, target) in enumerate(
            ((rows_hbm, rows_ref), (gain_hbm, gain_ref), (route_hbm, route_ref))
        )
    ]
    for copy in copies:
        copy.start()
    for copy in copies:
        copy.wait()
    row_count, width = rows_ref.shape
    rows = rows_ref[...].astype(jnp.float32)
    scale = lax.rsqrt(jnp.sum(rows * rows, axis=1, keepdims=True) * (1.0 / width) + epsilon)
    normed = (rows * scale * gain_ref[...]).astype(jnp.bfloat16)
    named = [route_ref[0, row] for row in range(row_count)]
    at = lax.broadcasted_iota(jnp.int32, code_ref.shape, 1)
    code = jnp.full(code_ref.shape, -1, jnp.int32)
    for row in range(row_count):
        slot = jnp.int32(0)
        for before in range(row):
            slot = slot + jnp.where(named[before] == named[row], 1, 0)
        code = jnp.where(at == row, named[row] * row_count + slot, code)
    code_ref[...] = code.astype(jnp.float32)
    mine = lax.axis_index("exp") // shards
    height = E_WIN * row_count
    row = lax.broadcasted_iota(jnp.int32, (height, CODE), 0)
    wanted = (mine ^ (row // row_count)) * row_count + row % row_count
    placing = jnp.where(wanted == code[0:1], 1.0, 0.0).astype(jnp.bfloat16)[:, :row_count]
    packed = jnp.dot(placing, normed, preferred_element_type=jnp.float32)
    for expert in range(E_WIN):
        blocks[expert][...] = packed[expert * row_count : (expert + 1) * row_count].astype(
            jnp.bfloat16
        )


def flag_body(owner, after, flags, owner_ref, sems):
    owner_copy = pltpu.make_async_copy(owner, owner_ref, sems.at[0])
    owner_copy.start()
    owner_copy.wait()
    group = lax.axis_index("grp")
    row = lax.broadcasted_iota(jnp.int32, flags.shape, 0)
    values = jnp.zeros(flags.shape, jnp.float32)
    for which in range(PAIR):
        for bucket in range(BUCKETS):
            hit = jnp.where(owner_ref[0, bucket] == (group ^ which), 1.0, 0.0)
            values = jnp.where(row == which * BUCKETS + bucket, hit, values)
    flags[...] = values


def activate_body(devices, weights, code_ref, *refs):
    blocks, out, stacked = refs[:devices], refs[devices], refs[devices + 1]
    row_count = blocks[0].shape[0]
    for index in range(devices):
        stacked[index * row_count : (index + 1) * row_count, :] = blocks[index][...].astype(
            jnp.float32
        )
    rows = stacked[...].astype(jnp.bfloat16)
    width = rows.shape[1]
    step = width // 4 if width % 512 == 0 else width
    gate, up = 0.0, 0.0
    for start in range(0, width, step):
        part = rows[:, start : start + step]
        gate = gate + lax.dot_general(
            part, weights[0, :, start : start + step], NT, preferred_element_type=jnp.float32
        )
        up = up + lax.dot_general(
            part, weights[1, :, start : start + step], NT, preferred_element_type=jnp.float32
        )
    act = gate * jax.nn.sigmoid(gate) * up
    spare = lax.broadcasted_iota(jnp.int32, (act.shape[0], CODE), 0) == CAP
    out[:, :CODE] = jnp.where(spare, code_ref[0:1, :], act[:, :CODE]).astype(jnp.bfloat16)
    out[:, CODE:] = act[:, CODE:].astype(jnp.bfloat16)


def hold_body(chips, row_count, own, other, after, down, placing, sems):
    piece = own.shape[0]
    copies = [
        pltpu.make_async_copy(source, down.at[pl.ds(index * piece, piece)], sems.at[index])
        for index, source in enumerate((own, other))
    ]
    for copy in copies:
        copy.start()
    shape = placing.shape[1:]
    row, column = (lax.broadcasted_iota(jnp.int32, shape, axis) for axis in (0, 1))
    block, used = 2 * CAP * chips, shape[0] // 2
    lower, home, spot = row // used, (row % used) // block, row % block
    slot, part, at = spot // (2 * chips), (spot % (2 * chips)) // chips, spot % chips
    matches = (part == lower) & (home == column // row_count) & (slot == column % row_count)
    for chip in range(chips):
        placing[chip] = jnp.where(matches & (at == chip), 1.0, 0.0).astype(jnp.bfloat16)
    for copy in copies:
        copy.wait()


def down_body(devices, chips, down, flags, placing, *refs):
    acts, partials = refs[:chips], refs[chips:]
    block, half = partials[0].shape
    used = devices * block
    rows, units = acts[0].shape
    piece = units // BUCKETS
    placed = jnp.zeros((2 * used, PAIR * piece), jnp.float32)
    for chip in range(chips):
        picked = []
        for which in range(PAIR):
            chosen = jnp.zeros((rows, piece), jnp.float32)
            for bucket in range(BUCKETS):
                flag = flags[which * BUCKETS + bucket : which * BUCKETS + bucket + 1, 0:piece]
                piece_of = acts[chip][:, bucket * piece : (bucket + 1) * piece].astype(jnp.float32)
                chosen = jnp.where(flag > 0.5, piece_of, chosen)
            picked.append(chosen.astype(jnp.bfloat16))
        placed = placed + jnp.dot(
            placing[chip], jnp.concatenate(picked, axis=1), preferred_element_type=jnp.float32
        )
    placed = placed.astype(jnp.bfloat16)
    above, below = placed[:used], placed[used:]
    step = half // 7 if half % (7 * 128) == 0 else half
    for start in range(0, half, step):
        out = jnp.dot(above, down[:, start : start + step], preferred_element_type=jnp.float32)
        out = out + jnp.dot(
            below, down[:, half + start : half + start + step], preferred_element_type=jnp.float32
        )
        for index in range(devices):
            partials[index][:, start : start + step] = out[
                index * block : (index + 1) * block
            ].astype(jnp.bfloat16)


def place_body(chips, shards, row_count, block, *refs):
    acts, placing, codes = refs[:chips], refs[-2], refs[-1]
    mine = lax.axis_index("exp") // shards
    diagonal = lax.broadcasted_iota(jnp.int32, (row_count, CODE), 0) == lax.broadcasted_iota(
        jnp.int32, (row_count, CODE), 1
    )
    for chip in range(chips):
        line = acts[chip][:, :CODE].astype(jnp.float32)[CAP : CAP + 1, :]
        mark = jnp.sum(jnp.where(diagonal, line, 0.0), axis=1, keepdims=True)
        codes[chip * row_count : (chip + 1) * row_count, :] = jnp.broadcast_to(
            mark, (row_count, CODE)
        )
    code = codes[...]
    home = lax.broadcasted_iota(jnp.int32, code.shape, 0) // row_count
    at = lax.broadcasted_iota(jnp.int32, code.shape, 1)
    at_slot, at_part, at_chip = at // (2 * chips), (at % (2 * chips)) // chips, at % chips
    for expert in range(E_WIN):
        wanted = ((mine ^ expert) * row_count + at_slot).astype(jnp.float32)
        chosen = (wanted == code) & (at_chip == home) & (at < block)
        for part in range(2):
            placing[2 * expert + part] = jnp.where(chosen & (at_part == part), 1.0, 0.0).astype(
                jnp.bfloat16
            )


def combine_body(devices, chips, shards, placing, *refs):
    blocks, outs = refs[:devices], refs[devices:]
    block, half = blocks[0].shape
    row_count = outs[0].shape[0]
    for part in range(2):
        total = 0.0
        for index in range(devices):
            total = total + jnp.dot(
                placing[2 * (index // shards) + part][:, :block],
                blocks[index][...],
                preferred_element_type=jnp.float32,
            )
        for chip in range(chips):
            outs[chip][:, part * half : (part + 1) * half] = total[
                chip * row_count : (chip + 1) * row_count
            ].astype(outs[chip].dtype)


def exchange(values, axis, unit):
    moved = [values[0]]
    for bits in range(1, len(values)):
        moved.append(swap(values[bits], axis, bits * unit))
    return moved


def move_rows(hidden, norm_gain, route, route_weight, resident, sectioned, owner):
    rows, own_piece = hidden[0], sectioned[0]
    row_count, width = rows.shape
    devices = lax.axis_size("exp")
    chips = lax.axis_size("grp") // PAIR
    shards = devices // E_WIN
    half, block = width // 2, 2 * CAP * chips
    piece, units = own_piece.shape[0], resident.shape[1]
    row_block = pltpu.VMEM((row_count, width), jnp.bfloat16)
    *packed, code = pl.pallas_call(
        functools.partial(prepare_body, shards),
        out_shape=[row_block] * E_WIN + [pltpu.VMEM((8, CODE), jnp.float32)],
        in_specs=[HBM] * 3,
        out_specs=[VMEM] * (E_WIN + 1),
        scratch_shapes=[
            pltpu.SMEM((1, row_count), jnp.int32),
            pltpu.VMEM((row_count, width), jnp.bfloat16),
            pltpu.VMEM((1, width), jnp.float32),
            pltpu.SemaphoreType.DMA((3,)),
        ],
        compiler_params=limit(4),
        cost_estimate=pl.CostEstimate(flops=10**10, transcendentals=0, bytes_accessed=2 * 10**7),
        name="prepare",
    )(*in_hbm(route.reshape(1, row_count), rows, norm_gain.reshape(1, width)))
    arrived = exchange([packed[bits // shards] for bits in range(devices)], "exp", 1)
    other_piece = swap(own_piece, "grp", 1)
    flags = pl.pallas_call(
        flag_body,
        out_shape=pltpu.VMEM((8, CODE), jnp.float32),
        in_specs=[HBM, ANY],
        out_specs=VMEM,
        scratch_shapes=[
            pltpu.SMEM((1, owner.shape[0]), jnp.int32),
            pltpu.SemaphoreType.DMA((1,)),
        ],
        compiler_params=limit(2),
        name="flag",
    )(*in_hbm(owner.reshape(1, -1)), *held(code))
    act = pl.pallas_call(
        functools.partial(activate_body, devices),
        out_shape=pltpu.VMEM((devices * row_count, units), jnp.bfloat16),
        in_specs=[VMEM] * (2 + devices),
        out_specs=VMEM,
        scratch_shapes=[pltpu.VMEM((devices * row_count, width), jnp.float32)],
        compiler_params=limit(20),
        name="activate",
    )(resident, *held(code, *arrived))
    acts = exchange([act] * chips, "grp", PAIR)
    down, placing = pl.pallas_call(
        functools.partial(hold_body, chips, row_count),
        out_shape=[
            pltpu.VMEM((PAIR * piece, width), jnp.bfloat16),
            pltpu.VMEM((chips, 2 * devices * block, devices * row_count), jnp.bfloat16),
        ],
        in_specs=[HBM, ANY, ANY],
        out_specs=[VMEM] * 2,
        scratch_shapes=[pltpu.SemaphoreType.DMA((PAIR,))],
        compiler_params=limit(2),
        name="hold",
    )(*in_hbm(own_piece), *held(other_piece, act))
    half_block = pltpu.VMEM((block, half), jnp.bfloat16)
    partials = pl.pallas_call(
        functools.partial(down_body, devices, chips),
        out_shape=[half_block] * devices,
        in_specs=[VMEM] * (3 + chips),
        out_specs=[VMEM] * devices,
        compiler_params=limit(12),
        name="down",
    )(*held(down, flags, placing, *acts))
    returned = exchange(partials, "exp", 1)
    placing = pl.pallas_call(
        functools.partial(place_body, chips, shards, row_count, block),
        out_shape=pltpu.VMEM((2 * E_WIN, chips * row_count, CODE), jnp.bfloat16),
        in_specs=[VMEM] * chips + [ANY],
        out_specs=VMEM,
        scratch_shapes=[pltpu.VMEM((chips * row_count, CODE), jnp.float32)],
        compiler_params=limit(2),
        name="place",
    )(*held(*acts, partials[0]))
    sums = pl.pallas_call(
        functools.partial(combine_body, devices, chips, shards),
        out_shape=[row_block] * chips,
        in_specs=[VMEM] * (1 + devices),
        out_specs=[VMEM] * chips,
        compiler_params=limit(8),
        name="combine",
    )(*held(placing, *returned))
    combined = 0.0
    for share in exchange(sums, "grp", PAIR):
        combined = combined + share.astype(jnp.float32)
    result = (combined * route_weight[0][:, None]).astype(jnp.bfloat16)
    return result.reshape(1, row_count, width)


def per_device(hidden, norm_gain, route, route_weight, resident, sectioned, owner):
    weight_rows = BUCKETS * sectioned.shape[1]
    partial_rows = lax.axis_size("exp") * lax.axis_size("grp") // PAIR * hidden.shape[1]
    plan = move_rows if partial_rows < weight_rows else move_weights
    return plan(hidden, norm_gain, route, route_weight, resident, sectioned, owner)


def solution(mesh):
    in_specs = (
        P("grp", "exp", None),
        P(),
        P("grp", "exp", None),
        P("grp", "exp"),
        P(None, "exp", None),
        P("grp", "exp", None),
        P(),
    )
    out_specs = P("grp", "exp", None)
    return jax.shard_map(
        per_device, mesh=mesh, in_specs=in_specs, out_specs=out_specs, check_vma=False
    )
```

```python
import functools

import jax
import jax.numpy as jnp
from jax import lax
from jax.experimental import pallas as pl
from jax.experimental.pallas import tpu as pltpu
from jax.sharding import PartitionSpec as P


E_WIN = 2
BUCKETS = 4
CAP = 3
PAIR = 2


epsilon = 1e-06


def from_root(value, axis, source):
    kept = jnp.where(lax.axis_index(axis) == source, value, 0).astype(value.dtype)
    return lax.psum(kept, axis)


def activate(slot_rows, gate_up):
    gate_part = lax.dot_general(
        slot_rows, gate_up[0], (((1,), (1,)), ((), ())), preferred_element_type=jnp.float32
    )
    up_part = lax.dot_general(
        slot_rows, gate_up[1], (((1,), (1,)), ((), ())), preferred_element_type=jnp.float32
    )
    return (jax.nn.silu(gate_part) * up_part).astype(jnp.bfloat16)


def normalize(rows, norm_gain):
    row_data = rows.astype(jnp.float32)
    scale = lax.rsqrt(jnp.mean(row_data * row_data, axis=1, keepdims=True) + epsilon)
    return (row_data * scale * norm_gain[None, :]).astype(jnp.bfloat16)


def move_weights(hidden, norm_gain, route, route_weight, resident, sectioned, owner):
    normed = normalize(hidden[0], norm_gain)
    row_count, width = normed.shape
    devices = lax.axis_size("exp")
    shards = devices // E_WIN
    expert_ids = route[0, :, 0]
    onehot = (expert_ids[:, None] == jnp.arange(E_WIN, dtype=jnp.int32)[None, :]).astype(jnp.int32)
    position = jnp.cumsum(onehot, axis=0) - onehot
    slot_index = jnp.sum(position * onehot, axis=1)
    placing = onehot[:, :, None] * (
        slot_index[:, None, None] == jnp.arange(CAP, dtype=jnp.int32)[None, None, :]
    ).astype(jnp.int32)
    placing = placing.reshape(row_count, E_WIN * CAP)
    packed = jnp.dot(
        placing.astype(jnp.bfloat16).T, normed, preferred_element_type=jnp.float32
    ).astype(jnp.bfloat16)
    packed = packed.reshape(E_WIN, 1, CAP, width)
    outgoing = jnp.broadcast_to(packed, (E_WIN, shards, CAP, width)).reshape(devices, CAP, width)
    piece_rows = sectioned.shape[1]
    arrived = lax.all_to_all(outgoing, "exp", split_axis=0, concat_axis=0, tiled=True)
    flat_slots = arrived.reshape(-1, width)
    activation = activate(flat_slots, resident)
    running_sum = jnp.zeros((flat_slots.shape[0], width), jnp.float32)
    for bucket in range(BUCKETS):
        weight_piece = from_root(sectioned[0], "grp", owner[bucket])
        act_piece = activation[:, bucket * piece_rows : (bucket + 1) * piece_rows]
        running_sum = running_sum + jnp.dot(
            act_piece, weight_piece, preferred_element_type=jnp.float32
        )
    partials = running_sum.astype(jnp.bfloat16).reshape(arrived.shape)
    returned = lax.all_to_all(partials, "exp", split_axis=0, concat_axis=0, tiled=True)
    summed = jnp.sum(returned.astype(jnp.float32).reshape(E_WIN, shards, CAP, width), axis=1)
    summed = summed.reshape(E_WIN * CAP, width)
    combined = jnp.dot(placing.astype(jnp.float32), summed, precision=lax.Precision.HIGHEST)
    result = (combined * route_weight[0][:, None]).astype(jnp.bfloat16)
    return result.reshape(1, row_count, width)


def swap(value, axis, bits):
    size = lax.axis_size(axis)
    return lax.ppermute(value, axis, [(i, i ^ bits) for i in range(size)])


NT = (((1,), (1,)), ((), ()))
VMEM = pl.BlockSpec(memory_space=pltpu.VMEM)
ANY = pl.BlockSpec(memory_space=pl.ANY)
HBM = pl.BlockSpec(memory_space=pltpu.HBM)
CODE = 128
MIB = 1 << 20


def held(*values):
    return [pltpu.with_memory_space_constraint(value, pltpu.VMEM) for value in values]


def in_hbm(*values):
    return [pltpu.with_memory_space_constraint(value, pltpu.HBM) for value in values]


def limit(mib):
    return pltpu.CompilerParams(vmem_limit_bytes=mib * MIB)


def prepare_body(shards, route_hbm, rows_hbm, gain_hbm, *refs):
    blocks, code_ref = refs[:E_WIN], refs[E_WIN]
    route_ref, rows_ref, gain_ref, sems = refs[E_WIN + 1 :]
    copies = [
        pltpu.make_async_copy(source, target, sems.at[index])
        for index, (source, target) in enumerate(
            ((rows_hbm, rows_ref), (gain_hbm, gain_ref), (route_hbm, route_ref))
        )
    ]
    for copy in copies:
        copy.start()
    for copy in copies:
        copy.wait()
    row_count, width = rows_ref.shape
    rows = rows_ref[...].astype(jnp.float32)
    scale = lax.rsqrt(jnp.sum(rows * rows, axis=1, keepdims=True) * (1.0 / width) + epsilon)
    normed = (rows * scale * gain_ref[...]).astype(jnp.bfloat16)
    named = [route_ref[0, row] for row in range(row_count)]
    at = lax.broadcasted_iota(jnp.int32, code_ref.shape, 1)
    code = jnp.full(code_ref.shape, -1, jnp.int32)
    for row in range(row_count):
        slot = jnp.int32(0)
        for before in range(row):
            slot = slot + jnp.where(named[before] == named[row], 1, 0)
        code = jnp.where(at == row, named[row] * row_count + slot, code)
    code_ref[...] = code.astype(jnp.float32)
    mine = lax.axis_index("exp") // shards
    height = E_WIN * row_count
    row = lax.broadcasted_iota(jnp.int32, (height, CODE), 0)
    wanted = (mine ^ (row // row_count)) * row_count + row % row_count
    placing = jnp.where(wanted == code[0:1], 1.0, 0.0).astype(jnp.bfloat16)[:, :row_count]
    packed = jnp.dot(placing, normed, preferred_element_type=jnp.float32)
    for expert in range(E_WIN):
        blocks[expert][...] = packed[expert * row_count : (expert + 1) * row_count].astype(
            jnp.bfloat16
        )


def flag_body(chips, row_count, owner, after, flags, placing, owner_ref, sems):
    owner_copy = pltpu.make_async_copy(owner, owner_ref, sems.at[0])
    owner_copy.start()
    shape = placing.shape[1:]
    row, column = (lax.broadcasted_iota(jnp.int32, shape, axis) for axis in (0, 1))
    block, used = 2 * CAP * chips, shape[0] // 2
    lower, home, spot = row // used, (row % used) // block, row % block
    slot, part, at = spot // (2 * chips), (spot % (2 * chips)) // chips, spot % chips
    matches = (part == lower) & (home == column // row_count) & (slot == column % row_count)
    for chip in range(chips):
        placing[chip] = jnp.where(matches & (at == chip), 1.0, 0.0).astype(jnp.bfloat16)
    owner_copy.wait()
    group = lax.axis_index("grp")
    row = lax.broadcasted_iota(jnp.int32, flags.shape, 0)
    values = jnp.zeros(flags.shape, jnp.float32)
    for which in range(PAIR):
        for bucket in range(BUCKETS):
            hit = jnp.where(owner_ref[0, bucket] == (group ^ which), 1.0, 0.0)
            values = jnp.where(row == which * BUCKETS + bucket, hit, values)
    flags[...] = values


def activate_body(devices, weights, code_ref, *refs):
    blocks, out, stacked = refs[:devices], refs[devices], refs[devices + 1]
    row_count = blocks[0].shape[0]
    for index in range(devices):
        stacked[index * row_count : (index + 1) * row_count, :] = blocks[index][...].astype(
            jnp.float32
        )
    rows = stacked[...].astype(jnp.bfloat16)
    width = rows.shape[1]
    step = width // 4 if width % 512 == 0 else width
    gate, up = 0.0, 0.0
    for start in range(0, width, step):
        part = rows[:, start : start + step]
        gate = gate + lax.dot_general(
            part, weights[0, :, start : start + step], NT, preferred_element_type=jnp.float32
        )
        up = up + lax.dot_general(
            part, weights[1, :, start : start + step], NT, preferred_element_type=jnp.float32
        )
    act = gate * jax.nn.sigmoid(gate) * up
    spare = lax.broadcasted_iota(jnp.int32, (act.shape[0], CODE), 0) == CAP
    out[:, :CODE] = jnp.where(spare, code_ref[0:1, :], act[:, :CODE]).astype(jnp.bfloat16)
    out[:, CODE:] = act[:, CODE:].astype(jnp.bfloat16)


def down_body(devices, chips, own, other, flags, placing, *refs):
    acts, partials = refs[:chips], refs[chips:]
    block, half = partials[0].shape
    used = devices * block
    rows, units = acts[0].shape
    piece = units // BUCKETS
    placed = [jnp.zeros((2 * used, piece), jnp.float32) for _ in range(PAIR)]
    for chip in range(chips):
        for which in range(PAIR):
            chosen = jnp.zeros((rows, piece), jnp.float32)
            for bucket in range(BUCKETS):
                flag = flags[which * BUCKETS + bucket : which * BUCKETS + bucket + 1, 0:piece]
                piece_of = acts[chip][:, bucket * piece : (bucket + 1) * piece].astype(jnp.float32)
                chosen = jnp.where(flag > 0.5, piece_of, chosen)
            placed[which] = placed[which] + jnp.dot(
                placing[chip], chosen.astype(jnp.bfloat16), preferred_element_type=jnp.float32
            )
    placed = [part.astype(jnp.bfloat16) for part in placed]
    step = half // 7 if half % (7 * 128) == 0 else half
    for start in range(0, half, step):
        out = 0.0
        for rows_at, column in ((0, start), (used, half + start)):
            for part, weights in zip(placed, (own, other)):
                out = out + jnp.dot(
                    part[rows_at : rows_at + used],
                    weights[:, column : column + step],
                    preferred_element_type=jnp.float32,
                )
        for index in range(devices):
            partials[index][:, start : start + step] = out[
                index * block : (index + 1) * block
            ].astype(jnp.bfloat16)


def place_body(chips, shards, row_count, block, *refs):
    acts, placing, codes = refs[:chips], refs[-2], refs[-1]
    mine = lax.axis_index("exp") // shards
    diagonal = lax.broadcasted_iota(jnp.int32, (row_count, CODE), 0) == lax.broadcasted_iota(
        jnp.int32, (row_count, CODE), 1
    )
    for chip in range(chips):
        line = acts[chip][:, :CODE].astype(jnp.float32)[CAP : CAP + 1, :]
        mark = jnp.sum(jnp.where(diagonal, line, 0.0), axis=1, keepdims=True)
        codes[chip * row_count : (chip + 1) * row_count, :] = jnp.broadcast_to(
            mark, (row_count, CODE)
        )
    code = codes[...]
    home = lax.broadcasted_iota(jnp.int32, code.shape, 0) // row_count
    at = lax.broadcasted_iota(jnp.int32, code.shape, 1)
    at_slot, at_part, at_chip = at // (2 * chips), (at % (2 * chips)) // chips, at % chips
    for expert in range(E_WIN):
        wanted = ((mine ^ expert) * row_count + at_slot).astype(jnp.float32)
        chosen = (wanted == code) & (at_chip == home) & (at < block)
        for part in range(2):
            placing[2 * expert + part] = jnp.where(chosen & (at_part == part), 1.0, 0.0).astype(
                jnp.bfloat16
            )


def combine_body(devices, chips, shards, placing, *refs):
    blocks, outs = refs[:devices], refs[devices:]
    block, half = blocks[0].shape
    row_count = outs[0].shape[0]
    for part in range(2):
        total = 0.0
        for index in range(devices):
            total = total + jnp.dot(
                placing[2 * (index // shards) + part][:, :block],
                blocks[index][...],
                preferred_element_type=jnp.float32,
            )
        for chip in range(chips):
            outs[chip][:, part * half : (part + 1) * half] = total[
                chip * row_count : (chip + 1) * row_count
            ].astype(outs[chip].dtype)


def exchange(values, axis):
    groups, devices = lax.axis_size("grp"), lax.axis_size("exp")
    moved = [values[0]]
    for bits in range(1, len(values)):
        group_bits, bits_along = (1, bits) if axis == "exp" else (PAIR * bits + 1, 0)
        pairs = [
            (group * devices + index, (group ^ group_bits) * devices + (index ^ bits_along))
            for group in range(groups)
            for index in range(devices)
        ]
        moved.append(lax.ppermute(values[bits], ("grp", "exp"), pairs))
    return moved


def move_rows(hidden, norm_gain, route, route_weight, resident, sectioned, owner):
    rows, own_piece = hidden[0], sectioned[0]
    row_count, width = rows.shape
    devices = lax.axis_size("exp")
    chips = lax.axis_size("grp") // PAIR
    shards = devices // E_WIN
    half, block = width // 2, 2 * CAP * chips
    units = resident.shape[1]
    row_block = pltpu.VMEM((row_count, width), jnp.bfloat16)
    *packed, code = pl.pallas_call(
        functools.partial(prepare_body, shards),
        out_shape=[row_block] * E_WIN + [pltpu.VMEM((8, CODE), jnp.float32)],
        in_specs=[HBM] * 3,
        out_specs=[VMEM] * (E_WIN + 1),
        scratch_shapes=[
            pltpu.SMEM((1, row_count), jnp.int32),
            pltpu.VMEM((row_count, width), jnp.bfloat16),
            pltpu.VMEM((1, width), jnp.float32),
            pltpu.SemaphoreType.DMA((3,)),
        ],
        compiler_params=limit(4),
        cost_estimate=pl.CostEstimate(flops=10**10, transcendentals=0, bytes_accessed=2 * 10**7),
        name="prepare",
    )(*in_hbm(route.reshape(1, row_count), rows, norm_gain.reshape(1, width)))
    arrived = exchange([packed[bits // shards] for bits in range(devices)], "exp")
    other_piece = swap(own_piece, "grp", 1)
    flags, spots = pl.pallas_call(
        functools.partial(flag_body, chips, row_count),
        out_shape=[
            pltpu.VMEM((8, CODE), jnp.float32),
            pltpu.VMEM((chips, 2 * devices * block, devices * row_count), jnp.bfloat16),
        ],
        in_specs=[HBM, ANY],
        out_specs=[VMEM] * 2,
        scratch_shapes=[pltpu.SMEM((1, owner.shape[0]), jnp.int32), pltpu.SemaphoreType.DMA((1,))],
        compiler_params=limit(2),
        name="flag",
    )(*in_hbm(owner.reshape(1, -1)), *held(code))
    act = pl.pallas_call(
        functools.partial(activate_body, devices),
        out_shape=pltpu.VMEM((devices * row_count, units), jnp.bfloat16),
        in_specs=[VMEM] * (2 + devices),
        out_specs=VMEM,
        scratch_shapes=[pltpu.VMEM((devices * row_count, width), jnp.float32)],
        compiler_params=limit(20),
        name="activate",
    )(resident, *held(code, *arrived))
    acts = exchange([act] * chips, "grp")
    half_block = pltpu.VMEM((block, half), jnp.bfloat16)
    partials = pl.pallas_call(
        functools.partial(down_body, devices, chips),
        out_shape=[half_block] * devices,
        in_specs=[VMEM] * (4 + chips),
        out_specs=[VMEM] * devices,
        compiler_params=limit(12),
        name="down",
    )(*held(own_piece, other_piece, flags, spots, *acts))
    returned = exchange(partials, "exp")
    placing = pl.pallas_call(
        functools.partial(place_body, chips, shards, row_count, block),
        out_shape=pltpu.VMEM((2 * E_WIN, chips * row_count, CODE), jnp.bfloat16),
        in_specs=[VMEM] * chips + [ANY],
        out_specs=VMEM,
        scratch_shapes=[pltpu.VMEM((chips * row_count, CODE), jnp.float32)],
        compiler_params=limit(2),
        name="place",
    )(*held(*acts, partials[0]))
    sums = pl.pallas_call(
        functools.partial(combine_body, devices, chips, shards),
        out_shape=[row_block] * chips,
        in_specs=[VMEM] * (1 + devices),
        out_specs=[VMEM] * chips,
        compiler_params=limit(8),
        name="combine",
    )(*held(placing, *returned))
    combined = 0.0
    for share in exchange(sums, "grp"):
        combined = combined + share.astype(jnp.float32)
    result = (combined * route_weight[0][:, None]).astype(jnp.bfloat16)
    return result.reshape(1, row_count, width)


def per_device(hidden, norm_gain, route, route_weight, resident, sectioned, owner):
    weight_rows = BUCKETS * sectioned.shape[1]
    partial_rows = lax.axis_size("exp") * lax.axis_size("grp") // PAIR * hidden.shape[1]
    plan = move_rows if partial_rows < weight_rows else move_weights
    return plan(hidden, norm_gain, route, route_weight, resident, sectioned, owner)


def solution(mesh):
    in_specs = (
        P("grp", "exp", None),
        P(),
        P("grp", "exp", None),
        P("grp", "exp"),
        P(None, "exp", None),
        P("grp", "exp", None),
        P(),
    )
    out_specs = P("grp", "exp", None)
    return jax.shard_map(
        per_device, mesh=mesh, in_specs=in_specs, out_specs=out_specs, check_vma=False
    )
```

```python
import functools

import jax
import jax.numpy as jnp
from jax import lax
from jax.experimental import pallas as pl
from jax.experimental.pallas import tpu as pltpu
from jax.sharding import PartitionSpec as P


E_WIN = 2
BUCKETS = 4
CAP = 3
PAIR = 2


epsilon = 1e-06


def from_root(value, axis, source):
    kept = jnp.where(lax.axis_index(axis) == source, value, 0).astype(value.dtype)
    return lax.psum(kept, axis)


def activate(slot_rows, gate_up):
    gate_part = lax.dot_general(
        slot_rows, gate_up[0], (((1,), (1,)), ((), ())), preferred_element_type=jnp.float32
    )
    up_part = lax.dot_general(
        slot_rows, gate_up[1], (((1,), (1,)), ((), ())), preferred_element_type=jnp.float32
    )
    return (jax.nn.silu(gate_part) * up_part).astype(jnp.bfloat16)


def normalize(rows, norm_gain):
    row_data = rows.astype(jnp.float32)
    scale = lax.rsqrt(jnp.mean(row_data * row_data, axis=1, keepdims=True) + epsilon)
    return (row_data * scale * norm_gain[None, :]).astype(jnp.bfloat16)


def move_weights(hidden, norm_gain, route, route_weight, resident, sectioned, owner):
    normed = normalize(hidden[0], norm_gain)
    row_count, width = normed.shape
    devices = lax.axis_size("exp")
    shards = devices // E_WIN
    expert_ids = route[0, :, 0]
    onehot = (expert_ids[:, None] == jnp.arange(E_WIN, dtype=jnp.int32)[None, :]).astype(jnp.int32)
    position = jnp.cumsum(onehot, axis=0) - onehot
    slot_index = jnp.sum(position * onehot, axis=1)
    placing = onehot[:, :, None] * (
        slot_index[:, None, None] == jnp.arange(CAP, dtype=jnp.int32)[None, None, :]
    ).astype(jnp.int32)
    placing = placing.reshape(row_count, E_WIN * CAP)
    packed = jnp.dot(
        placing.astype(jnp.bfloat16).T, normed, preferred_element_type=jnp.float32
    ).astype(jnp.bfloat16)
    packed = packed.reshape(E_WIN, 1, CAP, width)
    outgoing = jnp.broadcast_to(packed, (E_WIN, shards, CAP, width)).reshape(devices, CAP, width)
    piece_rows = sectioned.shape[1]
    arrived = lax.all_to_all(outgoing, "exp", split_axis=0, concat_axis=0, tiled=True)
    flat_slots = arrived.reshape(-1, width)
    activation = activate(flat_slots, resident)
    running_sum = jnp.zeros((flat_slots.shape[0], width), jnp.float32)
    for bucket in range(BUCKETS):
        weight_piece = from_root(sectioned[0], "grp", owner[bucket])
        act_piece = activation[:, bucket * piece_rows : (bucket + 1) * piece_rows]
        running_sum = running_sum + jnp.dot(
            act_piece, weight_piece, preferred_element_type=jnp.float32
        )
    partials = running_sum.astype(jnp.bfloat16).reshape(arrived.shape)
    returned = lax.all_to_all(partials, "exp", split_axis=0, concat_axis=0, tiled=True)
    summed = jnp.sum(returned.astype(jnp.float32).reshape(E_WIN, shards, CAP, width), axis=1)
    summed = summed.reshape(E_WIN * CAP, width)
    combined = jnp.dot(placing.astype(jnp.float32), summed, precision=lax.Precision.HIGHEST)
    result = (combined * route_weight[0][:, None]).astype(jnp.bfloat16)
    return result.reshape(1, row_count, width)


def swap(value, axis, bits):
    size = lax.axis_size(axis)
    return lax.ppermute(value, axis, [(i, i ^ bits) for i in range(size)])


NT = (((1,), (1,)), ((), ()))
VMEM = pl.BlockSpec(memory_space=pltpu.VMEM)
ANY = pl.BlockSpec(memory_space=pl.ANY)
HBM = pl.BlockSpec(memory_space=pltpu.HBM)
CODE = 128
MIB = 1 << 20


def held(*values):
    return [pltpu.with_memory_space_constraint(value, pltpu.VMEM) for value in values]


def in_hbm(*values):
    return [pltpu.with_memory_space_constraint(value, pltpu.HBM) for value in values]


def limit(mib):
    return pltpu.CompilerParams(vmem_limit_bytes=mib * MIB)


def turned(slot, devices):
    bits = devices.bit_length() - 1
    return sum(((slot >> bit) & 1) << (bits - 1 - bit) for bit in range(bits))


def expert_shift(slot, devices, shards, odd):
    return jnp.where(odd, slot // shards, turned(slot, devices) // shards)


def prepare_body(devices, shards, route_hbm, rows_hbm, gain_hbm, *refs):
    blocks, code_ref = refs[:devices], refs[devices]
    route_ref, rows_ref, gain_ref, sems = refs[devices + 1 :]
    copies = [
        pltpu.make_async_copy(source, target, sems.at[index])
        for index, (source, target) in enumerate(
            ((rows_hbm, rows_ref), (gain_hbm, gain_ref), (route_hbm, route_ref))
        )
    ]
    for copy in copies:
        copy.start()
    for copy in copies:
        copy.wait()
    row_count, width = rows_ref.shape
    rows = rows_ref[...].astype(jnp.float32)
    scale = lax.rsqrt(jnp.sum(rows * rows, axis=1, keepdims=True) * (1.0 / width) + epsilon)
    normed = (rows * scale * gain_ref[...]).astype(jnp.bfloat16)
    named = [route_ref[0, row] for row in range(row_count)]
    at = lax.broadcasted_iota(jnp.int32, code_ref.shape, 1)
    code = jnp.full(code_ref.shape, -1, jnp.int32)
    for row in range(row_count):
        slot = jnp.int32(0)
        for before in range(row):
            slot = slot + jnp.where(named[before] == named[row], 1, 0)
        code = jnp.where(at == row, named[row] * row_count + slot, code)
    code_ref[...] = code.astype(jnp.float32)
    mine = lax.axis_index("exp") // shards
    odd = lax.axis_index("grp") % PAIR == 1
    row = lax.broadcasted_iota(jnp.int32, (devices * row_count, CODE), 0)
    expert = jnp.zeros(row.shape, jnp.int32)
    for slot in range(devices):
        named_here = mine ^ expert_shift(slot, devices, shards, odd)
        expert = jnp.where(row // row_count == slot, named_here, expert)
    wanted = expert * row_count + row % row_count
    placing = jnp.where(wanted == code[0:1], 1.0, 0.0).astype(jnp.bfloat16)[:, :row_count]
    packed = jnp.dot(placing, normed, preferred_element_type=jnp.float32)
    for slot in range(devices):
        blocks[slot][...] = packed[slot * row_count : (slot + 1) * row_count].astype(jnp.bfloat16)


def flag_body(chips, row_count, owner, after, flags, placing, owner_ref, sems):
    owner_copy = pltpu.make_async_copy(owner, owner_ref, sems.at[0])
    owner_copy.start()
    shape = placing.shape[1:]
    row, column = (lax.broadcasted_iota(jnp.int32, shape, axis) for axis in (0, 1))
    block, used = 2 * CAP * chips, shape[0] // 2
    lower, home, spot = row // used, (row % used) // block, row % block
    slot, part, at = spot // (2 * chips), (spot % (2 * chips)) // chips, spot % chips
    matches = (part == lower) & (home == column // row_count) & (slot == column % row_count)
    for chip in range(chips):
        placing[chip] = jnp.where(matches & (at == chip), 1.0, 0.0).astype(jnp.bfloat16)
    owner_copy.wait()
    group = lax.axis_index("grp")
    row = lax.broadcasted_iota(jnp.int32, flags.shape, 0)
    values = jnp.zeros(flags.shape, jnp.float32)
    for which in range(PAIR):
        for bucket in range(BUCKETS):
            hit = jnp.where(owner_ref[0, bucket] == (group ^ which), 1.0, 0.0)
            values = jnp.where(row == which * BUCKETS + bucket, hit, values)
    flags[...] = values


def activate_body(devices, weights, code_ref, *refs):
    blocks, out, stacked = refs[:devices], refs[devices], refs[devices + 1]
    row_count = blocks[0].shape[0]
    for index in range(devices):
        stacked[index * row_count : (index + 1) * row_count, :] = blocks[index][...].astype(
            jnp.float32
        )
    rows = stacked[...].astype(jnp.bfloat16)
    width = rows.shape[1]
    step = width // 4 if width % 512 == 0 else width
    gate, up = 0.0, 0.0
    for start in range(0, width, step):
        part = rows[:, start : start + step]
        gate = gate + lax.dot_general(
            part, weights[0, :, start : start + step], NT, preferred_element_type=jnp.float32
        )
        up = up + lax.dot_general(
            part, weights[1, :, start : start + step], NT, preferred_element_type=jnp.float32
        )
    act = gate * jax.nn.sigmoid(gate) * up
    spare = lax.broadcasted_iota(jnp.int32, (act.shape[0], CODE), 0) == CAP
    out[:, :CODE] = jnp.where(spare, code_ref[0:1, :], act[:, :CODE]).astype(jnp.bfloat16)
    out[:, CODE:] = act[:, CODE:].astype(jnp.bfloat16)


def down_body(devices, chips, own, other, flags, placing, *refs):
    acts, partials = refs[:chips], refs[chips:]
    block, half = partials[0].shape
    used = devices * block
    rows, units = acts[0].shape
    piece = units // BUCKETS
    placed = [jnp.zeros((2 * used, piece), jnp.float32) for _ in range(PAIR)]
    for chip in range(chips):
        for which in range(PAIR):
            chosen = jnp.zeros((rows, piece), jnp.float32)
            for bucket in range(BUCKETS):
                flag = flags[which * BUCKETS + bucket : which * BUCKETS + bucket + 1, 0:piece]
                piece_of = acts[chip][:, bucket * piece : (bucket + 1) * piece].astype(jnp.float32)
                chosen = jnp.where(flag > 0.5, piece_of, chosen)
            placed[which] = placed[which] + jnp.dot(
                placing[chip], chosen.astype(jnp.bfloat16), preferred_element_type=jnp.float32
            )
    placed = [part.astype(jnp.bfloat16) for part in placed]
    step = half // 7 if half % (7 * 128) == 0 else half
    for start in range(0, half, step):
        out = 0.0
        for rows_at, column in ((0, start), (used, half + start)):
            for part, weights in zip(placed, (own, other)):
                out = out + jnp.dot(
                    part[rows_at : rows_at + used],
                    weights[:, column : column + step],
                    preferred_element_type=jnp.float32,
                )
        for index in range(devices):
            partials[index][:, start : start + step] = out[
                index * block : (index + 1) * block
            ].astype(jnp.bfloat16)


def place_body(devices, chips, shards, row_count, block, *refs):
    acts, placing, codes = refs[:chips], refs[-2], refs[-1]
    mine = lax.axis_index("exp") // shards
    diagonal = lax.broadcasted_iota(jnp.int32, (row_count, CODE), 0) == lax.broadcasted_iota(
        jnp.int32, (row_count, CODE), 1
    )
    for chip in range(chips):
        line = acts[chip][:, :CODE].astype(jnp.float32)[CAP : CAP + 1, :]
        mark = jnp.sum(jnp.where(diagonal, line, 0.0), axis=1, keepdims=True)
        codes[chip * row_count : (chip + 1) * row_count, :] = jnp.broadcast_to(
            mark, (row_count, CODE)
        )
    code = codes[...]
    home = lax.broadcasted_iota(jnp.int32, code.shape, 0) // row_count
    at = lax.broadcasted_iota(jnp.int32, code.shape, 1)
    at_slot, at_part, at_chip = at // (2 * chips), (at % (2 * chips)) // chips, at % chips
    odd = lax.axis_index("grp") % PAIR == 1
    for slot in range(devices):
        expert = mine ^ expert_shift(slot, devices, shards, odd)
        wanted = (expert * row_count + at_slot).astype(jnp.float32)
        chosen = (wanted == code) & (at_chip == home) & (at < block)
        for part in range(2):
            placing[2 * slot + part] = jnp.where(chosen & (at_part == part), 1.0, 0.0).astype(
                jnp.bfloat16
            )


def combine_body(devices, chips, placing, *refs):
    blocks, outs = refs[:devices], refs[devices:]
    block, half = blocks[0].shape
    row_count = outs[0].shape[0]
    for part in range(2):
        total = 0.0
        for index in range(devices):
            total = total + jnp.dot(
                placing[2 * index + part][:, :block],
                blocks[index][...],
                preferred_element_type=jnp.float32,
            )
        for chip in range(chips):
            outs[chip][:, part * half : (part + 1) * half] = total[
                chip * row_count : (chip + 1) * row_count
            ].astype(outs[chip].dtype)


def exchange(values, axis):
    groups, devices = lax.axis_size("grp"), lax.axis_size("exp")
    moved = [values[0]]
    for turn in range(1, len(values)):
        pairs = []
        for group in range(groups):
            for index in range(devices):
                if axis == "grp":
                    there, partner = group ^ (PAIR * turn), index
                else:
                    there, partner = group, index ^ (turn if group % PAIR else turned(turn, devices))
                pairs.append((group * devices + index, there * devices + partner))
        moved.append(lax.ppermute(values[turn], ("grp", "exp"), pairs))
    return moved


def move_rows(hidden, norm_gain, route, route_weight, resident, sectioned, owner):
    rows, own_piece = hidden[0], sectioned[0]
    row_count, width = rows.shape
    devices = lax.axis_size("exp")
    chips = lax.axis_size("grp") // PAIR
    shards = devices // E_WIN
    half, block = width // 2, 2 * CAP * chips
    units = resident.shape[1]
    row_block = pltpu.VMEM((row_count, width), jnp.bfloat16)
    *packed, code = pl.pallas_call(
        functools.partial(prepare_body, devices, shards),
        out_shape=[row_block] * devices + [pltpu.VMEM((8, CODE), jnp.float32)],
        in_specs=[HBM] * 3,
        out_specs=[VMEM] * (devices + 1),
        scratch_shapes=[
            pltpu.SMEM((1, row_count), jnp.int32),
            pltpu.VMEM((row_count, width), jnp.bfloat16),
            pltpu.VMEM((1, width), jnp.float32),
            pltpu.SemaphoreType.DMA((3,)),
        ],
        compiler_params=limit(4),
        cost_estimate=pl.CostEstimate(flops=10**10, transcendentals=0, bytes_accessed=2 * 10**7),
        name="prepare",
    )(*in_hbm(route.reshape(1, row_count), rows, norm_gain.reshape(1, width)))
    arrived = exchange(packed, "exp")
    other_piece = swap(own_piece, "grp", 1)
    flags, spots = pl.pallas_call(
        functools.partial(flag_body, chips, row_count),
        out_shape=[
            pltpu.VMEM((8, CODE), jnp.float32),
            pltpu.VMEM((chips, 2 * devices * block, devices * row_count), jnp.bfloat16),
        ],
        in_specs=[HBM, ANY],
        out_specs=[VMEM] * 2,
        scratch_shapes=[pltpu.SMEM((1, owner.shape[0]), jnp.int32), pltpu.SemaphoreType.DMA((1,))],
        compiler_params=limit(2),
        name="flag",
    )(*in_hbm(owner.reshape(1, -1)), *held(code))
    act = pl.pallas_call(
        functools.partial(activate_body, devices),
        out_shape=pltpu.VMEM((devices * row_count, units), jnp.bfloat16),
        in_specs=[VMEM] * (2 + devices),
        out_specs=VMEM,
        scratch_shapes=[pltpu.VMEM((devices * row_count, width), jnp.float32)],
        compiler_params=limit(20),
        name="activate",
    )(resident, *held(code, *arrived))
    acts = exchange([act] * chips, "grp")
    half_block = pltpu.VMEM((block, half), jnp.bfloat16)
    partials = pl.pallas_call(
        functools.partial(down_body, devices, chips),
        out_shape=[half_block] * devices,
        in_specs=[VMEM] * (4 + chips),
        out_specs=[VMEM] * devices,
        compiler_params=limit(12),
        name="down",
    )(*held(own_piece, other_piece, flags, spots, *acts))
    returned = exchange(partials, "exp")
    placing = pl.pallas_call(
        functools.partial(place_body, devices, chips, shards, row_count, block),
        out_shape=pltpu.VMEM((2 * devices, chips * row_count, CODE), jnp.bfloat16),
        in_specs=[VMEM] * chips + [ANY],
        out_specs=VMEM,
        scratch_shapes=[pltpu.VMEM((chips * row_count, CODE), jnp.float32)],
        compiler_params=limit(2),
        name="place",
    )(*held(*acts, partials[0]))
    sums = pl.pallas_call(
        functools.partial(combine_body, devices, chips),
        out_shape=[row_block] * chips,
        in_specs=[VMEM] * (1 + devices),
        out_specs=[VMEM] * chips,
        compiler_params=limit(8),
        name="combine",
    )(*held(placing, *returned))
    combined = 0.0
    for share in exchange(sums, "grp"):
        combined = combined + share.astype(jnp.float32)
    result = (combined * route_weight[0][:, None]).astype(jnp.bfloat16)
    return result.reshape(1, row_count, width)


def per_device(hidden, norm_gain, route, route_weight, resident, sectioned, owner):
    weight_rows = BUCKETS * sectioned.shape[1]
    partial_rows = lax.axis_size("exp") * lax.axis_size("grp") // PAIR * hidden.shape[1]
    plan = move_rows if partial_rows < weight_rows else move_weights
    return plan(hidden, norm_gain, route, route_weight, resident, sectioned, owner)


def solution(mesh):
    in_specs = (
        P("grp", "exp", None),
        P(),
        P("grp", "exp", None),
        P("grp", "exp"),
        P(None, "exp", None),
        P("grp", "exp", None),
        P(),
    )
    out_specs = P("grp", "exp", None)
    return jax.shard_map(
        per_device, mesh=mesh, in_specs=in_specs, out_specs=out_specs, check_vma=False
    )
```

```python
import functools

import jax
import jax.numpy as jnp
from jax import lax
from jax.experimental import pallas as pl
from jax.experimental.pallas import tpu as pltpu
from jax.sharding import PartitionSpec as P


E_WIN = 2
BUCKETS = 4
CAP = 3
PAIR = 2


epsilon = 1e-06


def from_root(value, axis, source):
    kept = jnp.where(lax.axis_index(axis) == source, value, 0).astype(value.dtype)
    return lax.psum(kept, axis)


def activate(slot_rows, gate_up):
    gate_part = lax.dot_general(
        slot_rows, gate_up[0], (((1,), (1,)), ((), ())), preferred_element_type=jnp.float32
    )
    up_part = lax.dot_general(
        slot_rows, gate_up[1], (((1,), (1,)), ((), ())), preferred_element_type=jnp.float32
    )
    return (jax.nn.silu(gate_part) * up_part).astype(jnp.bfloat16)


def normalize(rows, norm_gain):
    row_data = rows.astype(jnp.float32)
    scale = lax.rsqrt(jnp.mean(row_data * row_data, axis=1, keepdims=True) + epsilon)
    return (row_data * scale * norm_gain[None, :]).astype(jnp.bfloat16)


def move_weights(hidden, norm_gain, route, route_weight, resident, sectioned, owner):
    normed = normalize(hidden[0], norm_gain)
    row_count, width = normed.shape
    devices = lax.axis_size("exp")
    shards = devices // E_WIN
    expert_ids = route[0, :, 0]
    onehot = (expert_ids[:, None] == jnp.arange(E_WIN, dtype=jnp.int32)[None, :]).astype(jnp.int32)
    position = jnp.cumsum(onehot, axis=0) - onehot
    slot_index = jnp.sum(position * onehot, axis=1)
    placing = onehot[:, :, None] * (
        slot_index[:, None, None] == jnp.arange(CAP, dtype=jnp.int32)[None, None, :]
    ).astype(jnp.int32)
    placing = placing.reshape(row_count, E_WIN * CAP)
    packed = jnp.dot(
        placing.astype(jnp.bfloat16).T, normed, preferred_element_type=jnp.float32
    ).astype(jnp.bfloat16)
    packed = packed.reshape(E_WIN, 1, CAP, width)
    outgoing = jnp.broadcast_to(packed, (E_WIN, shards, CAP, width)).reshape(devices, CAP, width)
    piece_rows = sectioned.shape[1]
    arrived = lax.all_to_all(outgoing, "exp", split_axis=0, concat_axis=0, tiled=True)
    flat_slots = arrived.reshape(-1, width)
    activation = activate(flat_slots, resident)
    running_sum = jnp.zeros((flat_slots.shape[0], width), jnp.float32)
    for bucket in range(BUCKETS):
        weight_piece = from_root(sectioned[0], "grp", owner[bucket])
        act_piece = activation[:, bucket * piece_rows : (bucket + 1) * piece_rows]
        running_sum = running_sum + jnp.dot(
            act_piece, weight_piece, preferred_element_type=jnp.float32
        )
    partials = running_sum.astype(jnp.bfloat16).reshape(arrived.shape)
    returned = lax.all_to_all(partials, "exp", split_axis=0, concat_axis=0, tiled=True)
    summed = jnp.sum(returned.astype(jnp.float32).reshape(E_WIN, shards, CAP, width), axis=1)
    summed = summed.reshape(E_WIN * CAP, width)
    combined = jnp.dot(placing.astype(jnp.float32), summed, precision=lax.Precision.HIGHEST)
    result = (combined * route_weight[0][:, None]).astype(jnp.bfloat16)
    return result.reshape(1, row_count, width)


def swap(value, axis, bits):
    size = lax.axis_size(axis)
    return lax.ppermute(value, axis, [(i, i ^ bits) for i in range(size)])


NT = (((1,), (1,)), ((), ()))
VMEM = pl.BlockSpec(memory_space=pltpu.VMEM)
ANY = pl.BlockSpec(memory_space=pl.ANY)
HBM = pl.BlockSpec(memory_space=pltpu.HBM)
CODE = 128
MIB = 1 << 20


def held(*values):
    return [pltpu.with_memory_space_constraint(value, pltpu.VMEM) for value in values]


def in_hbm(*values):
    return [pltpu.with_memory_space_constraint(value, pltpu.HBM) for value in values]


def limit(mib):
    return pltpu.CompilerParams(vmem_limit_bytes=mib * MIB)


def prepare_body(shards, route_hbm, rows_hbm, gain_hbm, *refs):
    blocks, code_ref = refs[:E_WIN], refs[E_WIN]
    route_ref, rows_ref, gain_ref, sems = refs[E_WIN + 1 :]
    copies = [
        pltpu.make_async_copy(source, target, sems.at[index])
        for index, (source, target) in enumerate(
            ((rows_hbm, rows_ref), (gain_hbm, gain_ref), (route_hbm, route_ref))
        )
    ]
    for copy in copies:
        copy.start()
    for copy in copies:
        copy.wait()
    row_count, width = rows_ref.shape
    rows = rows_ref[...].astype(jnp.float32)
    scale = lax.rsqrt(jnp.sum(rows * rows, axis=1, keepdims=True) * (1.0 / width) + epsilon)
    normed = (rows * scale * gain_ref[...]).astype(jnp.bfloat16)
    named = [route_ref[0, row] for row in range(row_count)]
    at = lax.broadcasted_iota(jnp.int32, code_ref.shape, 1)
    code = jnp.full(code_ref.shape, -1, jnp.int32)
    for row in range(row_count):
        slot = jnp.int32(0)
        for before in range(row):
            slot = slot + jnp.where(named[before] == named[row], 1, 0)
        code = jnp.where(at == row, named[row] * row_count + slot, code)
    code_ref[...] = code.astype(jnp.float32)
    mine = lax.axis_index("exp") // shards
    height = E_WIN * row_count
    row = lax.broadcasted_iota(jnp.int32, (height, CODE), 0)
    wanted = (mine ^ (row // row_count)) * row_count + row % row_count
    placing = jnp.where(wanted == code[0:1], 1.0, 0.0).astype(jnp.bfloat16)[:, :row_count]
    packed = jnp.dot(placing, normed, preferred_element_type=jnp.float32)
    for expert in range(E_WIN):
        blocks[expert][...] = packed[expert * row_count : (expert + 1) * row_count].astype(
            jnp.bfloat16
        )


def flag_body(chips, row_count, owner, after, flags, placing, owner_ref, sems):
    owner_copy = pltpu.make_async_copy(owner, owner_ref, sems.at[0])
    owner_copy.start()
    shape = placing.shape[1:]
    row, column = (lax.broadcasted_iota(jnp.int32, shape, axis) for axis in (0, 1))
    block, used = 2 * CAP * chips, shape[0] // 2
    lower, home, spot = row // used, (row % used) // block, row % block
    slot, part, at = spot // (2 * chips), (spot % (2 * chips)) // chips, spot % chips
    matches = (part == lower) & (home == column // row_count) & (slot == column % row_count)
    for chip in range(chips):
        placing[chip] = jnp.where(matches & (at == chip), 1.0, 0.0).astype(jnp.bfloat16)
    owner_copy.wait()
    group = lax.axis_index("grp")
    row = lax.broadcasted_iota(jnp.int32, flags.shape, 0)
    values = jnp.zeros(flags.shape, jnp.float32)
    for which in range(PAIR):
        for bucket in range(BUCKETS):
            hit = jnp.where(owner_ref[0, bucket] == (group ^ which), 1.0, 0.0)
            values = jnp.where(row == which * BUCKETS + bucket, hit, values)
    flags[...] = values


def activate_body(devices, weights, code_ref, *refs):
    blocks, out, stacked = refs[:devices], refs[devices], refs[devices + 1]
    row_count = blocks[0].shape[0]
    for index in range(devices):
        stacked[index * row_count : (index + 1) * row_count, :] = blocks[index][...].astype(
            jnp.float32
        )
    rows = stacked[...].astype(jnp.bfloat16)
    width = rows.shape[1]
    step = width // 4 if width % 512 == 0 else width
    gate, up = 0.0, 0.0
    for start in range(0, width, step):
        part = rows[:, start : start + step]
        gate = gate + lax.dot_general(
            part, weights[0, :, start : start + step], NT, preferred_element_type=jnp.float32
        )
        up = up + lax.dot_general(
            part, weights[1, :, start : start + step], NT, preferred_element_type=jnp.float32
        )
    act = gate * jax.nn.sigmoid(gate) * up
    spare = lax.broadcasted_iota(jnp.int32, (act.shape[0], CODE), 0) == CAP
    out[:, :CODE] = jnp.where(spare, code_ref[0:1, :], act[:, :CODE]).astype(jnp.bfloat16)
    out[:, CODE:] = act[:, CODE:].astype(jnp.bfloat16)


def down_body(devices, chips, own, other, flags, placing, *refs):
    acts, partials = refs[:chips], refs[chips:]
    block, half = partials[0].shape
    used = devices * block
    rows, units = acts[0].shape
    piece = units // BUCKETS
    placed = [jnp.zeros((2 * used, piece), jnp.float32) for _ in range(PAIR)]
    for chip in range(chips):
        for which in range(PAIR):
            chosen = jnp.zeros((rows, piece), jnp.float32)
            for bucket in range(BUCKETS):
                flag = flags[which * BUCKETS + bucket : which * BUCKETS + bucket + 1, 0:piece]
                piece_of = acts[chip][:, bucket * piece : (bucket + 1) * piece].astype(jnp.float32)
                chosen = jnp.where(flag > 0.5, piece_of, chosen)
            placed[which] = placed[which] + jnp.dot(
                placing[chip], chosen.astype(jnp.bfloat16), preferred_element_type=jnp.float32
            )
    placed = [part.astype(jnp.bfloat16) for part in placed]
    step = half // 7 if half % (7 * 128) == 0 else half
    for start in range(0, half, step):
        out = 0.0
        for rows_at, column in ((0, start), (used, half + start)):
            for part, weights in zip(placed, (own, other)):
                out = out + jnp.dot(
                    part[rows_at : rows_at + used],
                    weights[:, column : column + step],
                    preferred_element_type=jnp.float32,
                )
        for index in range(devices):
            partials[index][:, start : start + step] = out[
                index * block : (index + 1) * block
            ].astype(jnp.bfloat16)


def place_body(chips, shards, row_count, block, *refs):
    acts, placing, codes = refs[:chips], refs[-2], refs[-1]
    mine = lax.axis_index("exp") // shards
    diagonal = lax.broadcasted_iota(jnp.int32, (row_count, CODE), 0) == lax.broadcasted_iota(
        jnp.int32, (row_count, CODE), 1
    )
    for chip in range(chips):
        line = acts[chip][:, :CODE].astype(jnp.float32)[CAP : CAP + 1, :]
        mark = jnp.sum(jnp.where(diagonal, line, 0.0), axis=1, keepdims=True)
        codes[chip * row_count : (chip + 1) * row_count, :] = jnp.broadcast_to(
            mark, (row_count, CODE)
        )
    code = codes[...]
    home = lax.broadcasted_iota(jnp.int32, code.shape, 0) // row_count
    at = lax.broadcasted_iota(jnp.int32, code.shape, 1)
    at_slot, at_part, at_chip = at // (2 * chips), (at % (2 * chips)) // chips, at % chips
    for expert in range(E_WIN):
        wanted = ((mine ^ expert) * row_count + at_slot).astype(jnp.float32)
        chosen = (wanted == code) & (at_chip == home) & (at < block)
        for part in range(2):
            placing[2 * expert + part] = jnp.where(chosen & (at_part == part), 1.0, 0.0).astype(
                jnp.bfloat16
            )


def combine_body(devices, chips, shards, placing, *refs):
    blocks, outs = refs[:devices], refs[devices:]
    block, half = blocks[0].shape
    row_count = outs[0].shape[0]
    for part in range(2):
        total = 0.0
        for index in range(devices):
            total = total + jnp.dot(
                placing[2 * (index // shards) + part][:, :block],
                blocks[index][...],
                preferred_element_type=jnp.float32,
            )
        for chip in range(chips):
            outs[chip][:, part * half : (part + 1) * half] = total[
                chip * row_count : (chip + 1) * row_count
            ].astype(outs[chip].dtype)


def exchange(values, axis, unit):
    moved = [values[0]]
    for bits in range(1, len(values)):
        moved.append(swap(values[bits], axis, bits * unit))
    return moved


def move_rows(hidden, norm_gain, route, route_weight, resident, sectioned, owner):
    rows, own_piece = hidden[0], sectioned[0]
    row_count, width = rows.shape
    devices = lax.axis_size("exp")
    chips = lax.axis_size("grp") // PAIR
    shards = devices // E_WIN
    half, block = width // 2, 2 * CAP * chips
    units = resident.shape[1]
    row_block = pltpu.VMEM((row_count, width), jnp.bfloat16)
    *packed, code = pl.pallas_call(
        functools.partial(prepare_body, shards),
        out_shape=[row_block] * E_WIN + [pltpu.VMEM((8, CODE), jnp.float32)],
        in_specs=[HBM] * 3,
        out_specs=[VMEM] * (E_WIN + 1),
        scratch_shapes=[
            pltpu.SMEM((1, row_count), jnp.int32),
            pltpu.VMEM((row_count, width), jnp.bfloat16),
            pltpu.VMEM((1, width), jnp.float32),
            pltpu.SemaphoreType.DMA((3,)),
        ],
        compiler_params=limit(4),
        cost_estimate=pl.CostEstimate(flops=10**10, transcendentals=0, bytes_accessed=2 * 10**7),
        name="prepare",
    )(*in_hbm(route.reshape(1, row_count), rows, norm_gain.reshape(1, width)))
    arrived = exchange([packed[bits // shards] for bits in range(devices)], "exp", 1)
    other_piece = swap(own_piece, "grp", 1)
    flags, spots = pl.pallas_call(
        functools.partial(flag_body, chips, row_count),
        out_shape=[
            pltpu.VMEM((8, CODE), jnp.float32),
            pltpu.VMEM((chips, 2 * devices * block, devices * row_count), jnp.bfloat16),
        ],
        in_specs=[HBM, ANY],
        out_specs=[VMEM] * 2,
        scratch_shapes=[pltpu.SMEM((1, owner.shape[0]), jnp.int32), pltpu.SemaphoreType.DMA((1,))],
        compiler_params=limit(2),
        name="flag",
    )(*in_hbm(owner.reshape(1, -1)), *held(code))
    act = pl.pallas_call(
        functools.partial(activate_body, devices),
        out_shape=pltpu.VMEM((devices * row_count, units), jnp.bfloat16),
        in_specs=[VMEM] * (2 + devices),
        out_specs=VMEM,
        scratch_shapes=[pltpu.VMEM((devices * row_count, width), jnp.float32)],
        compiler_params=limit(20),
        name="activate",
    )(resident, *held(code, *arrived))
    acts = exchange([act] * chips, "grp", PAIR)
    half_block = pltpu.VMEM((block, half), jnp.bfloat16)
    partials = pl.pallas_call(
        functools.partial(down_body, devices, chips),
        out_shape=[half_block] * devices,
        in_specs=[VMEM] * (4 + chips),
        out_specs=[VMEM] * devices,
        compiler_params=limit(12),
        name="down",
    )(*held(own_piece, other_piece, flags, spots, *acts))
    returned = exchange(partials, "exp", 1)
    placing = pl.pallas_call(
        functools.partial(place_body, chips, shards, row_count, block),
        out_shape=pltpu.VMEM((2 * E_WIN, chips * row_count, CODE), jnp.bfloat16),
        in_specs=[VMEM] * chips + [ANY],
        out_specs=VMEM,
        scratch_shapes=[pltpu.VMEM((chips * row_count, CODE), jnp.float32)],
        compiler_params=limit(2),
        name="place",
    )(*held(*acts, partials[0]))
    sums = pl.pallas_call(
        functools.partial(combine_body, devices, chips, shards),
        out_shape=[row_block] * chips,
        in_specs=[VMEM] * (1 + devices),
        out_specs=[VMEM] * chips,
        compiler_params=limit(8),
        name="combine",
    )(*held(placing, *returned))
    combined = 0.0
    for share in exchange(sums, "grp", PAIR):
        combined = combined + share.astype(jnp.float32)
    result = (combined * route_weight[0][:, None]).astype(jnp.bfloat16)
    return result.reshape(1, row_count, width)


def per_device(hidden, norm_gain, route, route_weight, resident, sectioned, owner):
    weight_rows = BUCKETS * sectioned.shape[1]
    partial_rows = lax.axis_size("exp") * lax.axis_size("grp") // PAIR * hidden.shape[1]
    plan = move_rows if partial_rows < weight_rows else move_weights
    return plan(hidden, norm_gain, route, route_weight, resident, sectioned, owner)


def solution(mesh):
    in_specs = (
        P("grp", "exp", None),
        P(),
        P("grp", "exp", None),
        P("grp", "exp"),
        P(None, "exp", None),
        P("grp", "exp", None),
        P(),
    )
    out_specs = P("grp", "exp", None)
    return jax.shard_map(
        per_device, mesh=mesh, in_specs=in_specs, out_specs=out_specs, check_vma=False
    )
```

```python
import functools

import jax
import jax.numpy as jnp
from jax import lax
from jax.experimental import pallas as pl
from jax.experimental.pallas import tpu as pltpu
from jax.sharding import PartitionSpec as P


E_WIN = 2
BUCKETS = 4
CAP = 3
PAIR = 2


epsilon = 1e-06


def from_root(value, axis, source):
    kept = jnp.where(lax.axis_index(axis) == source, value, 0).astype(value.dtype)
    return lax.psum(kept, axis)


def activate(slot_rows, gate_up):
    gate_part = lax.dot_general(
        slot_rows, gate_up[0], (((1,), (1,)), ((), ())), preferred_element_type=jnp.float32
    )
    up_part = lax.dot_general(
        slot_rows, gate_up[1], (((1,), (1,)), ((), ())), preferred_element_type=jnp.float32
    )
    return (jax.nn.silu(gate_part) * up_part).astype(jnp.bfloat16)


def normalize(rows, norm_gain):
    row_data = rows.astype(jnp.float32)
    scale = lax.rsqrt(jnp.mean(row_data * row_data, axis=1, keepdims=True) + epsilon)
    return (row_data * scale * norm_gain[None, :]).astype(jnp.bfloat16)


def move_weights(hidden, norm_gain, route, route_weight, resident, sectioned, owner):
    normed = normalize(hidden[0], norm_gain)
    row_count, width = normed.shape
    devices = lax.axis_size("exp")
    shards = devices // E_WIN
    expert_ids = route[0, :, 0]
    onehot = (expert_ids[:, None] == jnp.arange(E_WIN, dtype=jnp.int32)[None, :]).astype(jnp.int32)
    position = jnp.cumsum(onehot, axis=0) - onehot
    slot_index = jnp.sum(position * onehot, axis=1)
    placing = onehot[:, :, None] * (
        slot_index[:, None, None] == jnp.arange(CAP, dtype=jnp.int32)[None, None, :]
    ).astype(jnp.int32)
    placing = placing.reshape(row_count, E_WIN * CAP)
    packed = jnp.dot(
        placing.astype(jnp.bfloat16).T, normed, preferred_element_type=jnp.float32
    ).astype(jnp.bfloat16)
    packed = packed.reshape(E_WIN, 1, CAP, width)
    outgoing = jnp.broadcast_to(packed, (E_WIN, shards, CAP, width)).reshape(devices, CAP, width)
    piece_rows = sectioned.shape[1]
    arrived = lax.all_to_all(outgoing, "exp", split_axis=0, concat_axis=0, tiled=True)
    flat_slots = arrived.reshape(-1, width)
    activation = activate(flat_slots, resident)
    running_sum = jnp.zeros((flat_slots.shape[0], width), jnp.float32)
    for bucket in range(BUCKETS):
        weight_piece = from_root(sectioned[0], "grp", owner[bucket])
        act_piece = activation[:, bucket * piece_rows : (bucket + 1) * piece_rows]
        running_sum = running_sum + jnp.dot(
            act_piece, weight_piece, preferred_element_type=jnp.float32
        )
    partials = running_sum.astype(jnp.bfloat16).reshape(arrived.shape)
    returned = lax.all_to_all(partials, "exp", split_axis=0, concat_axis=0, tiled=True)
    summed = jnp.sum(returned.astype(jnp.float32).reshape(E_WIN, shards, CAP, width), axis=1)
    summed = summed.reshape(E_WIN * CAP, width)
    combined = jnp.dot(placing.astype(jnp.float32), summed, precision=lax.Precision.HIGHEST)
    result = (combined * route_weight[0][:, None]).astype(jnp.bfloat16)
    return result.reshape(1, row_count, width)


def swap(value, axis, bits):
    size = lax.axis_size(axis)
    return lax.ppermute(value, axis, [(i, i ^ bits) for i in range(size)])


NT = (((1,), (1,)), ((), ()))
VMEM = pl.BlockSpec(memory_space=pltpu.VMEM)
ANY = pl.BlockSpec(memory_space=pl.ANY)
HBM = pl.BlockSpec(memory_space=pltpu.HBM)
CODE = 128
MIB = 1 << 20


def held(*values):
    return [pltpu.with_memory_space_constraint(value, pltpu.VMEM) for value in values]


def in_hbm(*values):
    return [pltpu.with_memory_space_constraint(value, pltpu.HBM) for value in values]


def limit(mib):
    return pltpu.CompilerParams(vmem_limit_bytes=mib * MIB)


def prepare_body(shards, route_hbm, rows_hbm, gain_hbm, *refs):
    blocks, code_ref = refs[:E_WIN], refs[E_WIN]
    route_ref, rows_ref, gain_ref, sems = refs[E_WIN + 1 :]
    copies = [
        pltpu.make_async_copy(source, target, sems.at[index])
        for index, (source, target) in enumerate(
            ((rows_hbm, rows_ref), (gain_hbm, gain_ref), (route_hbm, route_ref))
        )
    ]
    for copy in copies:
        copy.start()
    for copy in copies:
        copy.wait()
    row_count, width = rows_ref.shape
    rows = rows_ref[...].astype(jnp.float32)
    scale = lax.rsqrt(jnp.sum(rows * rows, axis=1, keepdims=True) * (1.0 / width) + epsilon)
    normed = (rows * scale * gain_ref[...]).astype(jnp.bfloat16)
    named = [route_ref[0, row] for row in range(row_count)]
    at = lax.broadcasted_iota(jnp.int32, code_ref.shape, 1)
    code = jnp.full(code_ref.shape, -1, jnp.int32)
    for row in range(row_count):
        slot = jnp.int32(0)
        for before in range(row):
            slot = slot + jnp.where(named[before] == named[row], 1, 0)
        code = jnp.where(at == row, named[row] * row_count + slot, code)
    code_ref[...] = code.astype(jnp.float32)
    mine = lax.axis_index("exp") // shards
    height = E_WIN * row_count
    row = lax.broadcasted_iota(jnp.int32, (height, CODE), 0)
    wanted = (mine ^ (row // row_count)) * row_count + row % row_count
    placing = jnp.where(wanted == code[0:1], 1.0, 0.0).astype(jnp.bfloat16)[:, :row_count]
    packed = jnp.dot(placing, normed, preferred_element_type=jnp.float32)
    for expert in range(E_WIN):
        blocks[expert][...] = packed[expert * row_count : (expert + 1) * row_count].astype(
            jnp.bfloat16
        )


def flag_body(chips, row_count, owner, weight, after, flags, placing, column_ref, owner_ref, weight_ref, sems):
    owner_copy = pltpu.make_async_copy(owner, owner_ref, sems.at[0])
    owner_copy.start()
    weight_copy = pltpu.make_async_copy(weight, weight_ref, sems.at[1])
    weight_copy.start()
    shape = placing.shape[1:]
    row, column = (lax.broadcasted_iota(jnp.int32, shape, axis) for axis in (0, 1))
    block, used = 2 * CAP * chips, shape[0] // 2
    lower, home, spot = row // used, (row % used) // block, row % block
    slot, part, at = spot // (2 * chips), (spot % (2 * chips)) // chips, spot % chips
    matches = (part == lower) & (home == column // row_count) & (slot == column % row_count)
    for chip in range(chips):
        placing[chip] = jnp.where(matches & (at == chip), 1.0, 0.0).astype(jnp.bfloat16)
    owner_copy.wait()
    group = lax.axis_index("grp")
    row = lax.broadcasted_iota(jnp.int32, flags.shape, 0)
    values = jnp.zeros(flags.shape, jnp.float32)
    for which in range(PAIR):
        for bucket in range(BUCKETS):
            hit = jnp.where(owner_ref[0, bucket] == (group ^ which), 1.0, 0.0)
            values = jnp.where(row == which * BUCKETS + bucket, hit, values)
    flags[...] = values
    weight_copy.wait()
    square = (row_count, row_count)
    same = lax.broadcasted_iota(jnp.int32, square, 0) == lax.broadcasted_iota(jnp.int32, square, 1)
    picked = jnp.sum(jnp.where(same, weight_ref[...], 0.0), axis=1, keepdims=True)
    column_ref[...] = jnp.broadcast_to(picked, column_ref.shape)


def finish_body(column_ref, *refs):
    shares, out, staged, sems = refs[:-3], refs[-3], refs[-2], refs[-1]
    width = staged.shape[1]
    weight = column_ref[:, 0:1]
    half = width // 2
    copies = []
    for part in range(2):
        here = pl.ds(part * half, half)
        total = 0.0
        for share in shares:
            total = total + share[:, part * half : (part + 1) * half].astype(jnp.float32)
        staged[:, part * half : (part + 1) * half] = (total * weight).astype(jnp.bfloat16)
        copies.append(
            pltpu.make_async_copy(staged.at[:, here], out.at[:, here], sems.at[part])
        )
        copies[-1].start()
    for copy in copies:
        copy.wait()


def activate_body(devices, weights, code_ref, *refs):
    blocks, out, stacked = refs[:devices], refs[devices], refs[devices + 1]
    row_count = blocks[0].shape[0]
    for index in range(devices):
        stacked[index * row_count : (index + 1) * row_count, :] = blocks[index][...].astype(
            jnp.float32
        )
    rows = stacked[...].astype(jnp.bfloat16)
    width = rows.shape[1]
    step = width // 4 if width % 512 == 0 else width
    gate, up = 0.0, 0.0
    for start in range(0, width, step):
        part = rows[:, start : start + step]
        gate = gate + lax.dot_general(
            part, weights[0, :, start : start + step], NT, preferred_element_type=jnp.float32
        )
        up = up + lax.dot_general(
            part, weights[1, :, start : start + step], NT, preferred_element_type=jnp.float32
        )
    act = gate * jax.nn.sigmoid(gate) * up
    spare = lax.broadcasted_iota(jnp.int32, (act.shape[0], CODE), 0) == CAP
    out[:, :CODE] = jnp.where(spare, code_ref[0:1, :], act[:, :CODE]).astype(jnp.bfloat16)
    out[:, CODE:] = act[:, CODE:].astype(jnp.bfloat16)


def down_body(devices, chips, own, other, flags, placing, *refs):
    acts, partials = refs[:chips], refs[chips:]
    block, half = partials[0].shape
    used = devices * block
    rows, units = acts[0].shape
    piece = units // BUCKETS
    placed = [jnp.zeros((2 * used, piece), jnp.float32) for _ in range(PAIR)]
    for chip in range(chips):
        for which in range(PAIR):
            chosen = jnp.zeros((rows, piece), jnp.float32)
            for bucket in range(BUCKETS):
                flag = flags[which * BUCKETS + bucket : which * BUCKETS + bucket + 1, 0:piece]
                piece_of = acts[chip][:, bucket * piece : (bucket + 1) * piece].astype(jnp.float32)
                chosen = jnp.where(flag > 0.5, piece_of, chosen)
            placed[which] = placed[which] + jnp.dot(
                placing[chip], chosen.astype(jnp.bfloat16), preferred_element_type=jnp.float32
            )
    placed = [part.astype(jnp.bfloat16) for part in placed]
    step = half // 2 if half % 512 == 0 else half
    for start in range(0, half, step):
        out = 0.0
        for rows_at, column in ((0, start), (used, half + start)):
            for part, weights in zip(placed, (own, other)):
                out = out + jnp.dot(
                    part[rows_at : rows_at + used],
                    weights[:, column : column + step],
                    preferred_element_type=jnp.float32,
                )
        for index in range(devices):
            partials[index][:, start : start + step] = out[
                index * block : (index + 1) * block
            ].astype(jnp.bfloat16)


def place_body(chips, shards, row_count, block, *refs):
    acts, placing, codes = refs[:chips], refs[-2], refs[-1]
    mine = lax.axis_index("exp") // shards
    diagonal = lax.broadcasted_iota(jnp.int32, (row_count, CODE), 0) == lax.broadcasted_iota(
        jnp.int32, (row_count, CODE), 1
    )
    for chip in range(chips):
        line = acts[chip][:, :CODE].astype(jnp.float32)[CAP : CAP + 1, :]
        mark = jnp.sum(jnp.where(diagonal, line, 0.0), axis=1, keepdims=True)
        codes[chip * row_count : (chip + 1) * row_count, :] = jnp.broadcast_to(
            mark, (row_count, CODE)
        )
    code = codes[...]
    home = lax.broadcasted_iota(jnp.int32, code.shape, 0) // row_count
    at = lax.broadcasted_iota(jnp.int32, code.shape, 1)
    at_slot, at_part, at_chip = at // (2 * chips), (at % (2 * chips)) // chips, at % chips
    for expert in range(E_WIN):
        wanted = ((mine ^ expert) * row_count + at_slot).astype(jnp.float32)
        chosen = (wanted == code) & (at_chip == home) & (at < block)
        for part in range(2):
            placing[2 * expert + part] = jnp.where(chosen & (at_part == part), 1.0, 0.0).astype(
                jnp.bfloat16
            )


def combine_body(devices, chips, shards, placing, *refs):
    blocks, outs = refs[:devices], refs[devices:]
    block, half = blocks[0].shape
    row_count = outs[0].shape[0]
    for part in range(2):
        total = 0.0
        for index in range(devices):
            total = total + jnp.dot(
                placing[2 * (index // shards) + part][:, :block],
                blocks[index][...],
                preferred_element_type=jnp.float32,
            )
        for chip in range(chips):
            outs[chip][:, part * half : (part + 1) * half] = total[
                chip * row_count : (chip + 1) * row_count
            ].astype(outs[chip].dtype)


def exchange(values, axis, unit):
    moved = [values[0]]
    for bits in range(1, len(values)):
        moved.append(swap(values[bits], axis, bits * unit))
    return moved


def move_rows(hidden, norm_gain, route, route_weight, resident, sectioned, owner):
    rows, own_piece = hidden[0], sectioned[0]
    row_count, width = rows.shape
    devices = lax.axis_size("exp")
    chips = lax.axis_size("grp") // PAIR
    shards = devices // E_WIN
    half, block = width // 2, 2 * CAP * chips
    units = resident.shape[1]
    row_block = pltpu.VMEM((row_count, width), jnp.bfloat16)
    *packed, code = pl.pallas_call(
        functools.partial(prepare_body, shards),
        out_shape=[row_block] * E_WIN + [pltpu.VMEM((8, CODE), jnp.float32)],
        in_specs=[HBM] * 3,
        out_specs=[VMEM] * (E_WIN + 1),
        scratch_shapes=[
            pltpu.SMEM((1, row_count), jnp.int32),
            pltpu.VMEM((row_count, width), jnp.bfloat16),
            pltpu.VMEM((1, width), jnp.float32),
            pltpu.SemaphoreType.DMA((3,)),
        ],
        compiler_params=limit(4),
        cost_estimate=pl.CostEstimate(flops=10**10, transcendentals=0, bytes_accessed=2 * 10**7),
        name="prepare",
    )(*in_hbm(route.reshape(1, row_count), rows, norm_gain.reshape(1, width)))
    arrived = exchange([packed[bits // shards] for bits in range(devices)], "exp", 1)
    other_piece = swap(own_piece, "grp", 1)
    flags, spots, weight_column = pl.pallas_call(
        functools.partial(flag_body, chips, row_count),
        out_shape=[
            pltpu.VMEM((8, CODE), jnp.float32),
            pltpu.VMEM((chips, 2 * devices * block, devices * row_count), jnp.bfloat16),
            pltpu.VMEM((row_count, CODE), jnp.float32),
        ],
        in_specs=[HBM, HBM, ANY],
        out_specs=[VMEM] * 3,
        scratch_shapes=[
            pltpu.SMEM((1, owner.shape[0]), jnp.int32),
            pltpu.VMEM((1, row_count), jnp.float32),
            pltpu.SemaphoreType.DMA((2,)),
        ],
        compiler_params=limit(2),
        name="flag",
    )(*in_hbm(owner.reshape(1, -1), route_weight), *held(code))
    act = pl.pallas_call(
        functools.partial(activate_body, devices),
        out_shape=pltpu.VMEM((devices * row_count, units), jnp.bfloat16),
        in_specs=[VMEM] * (2 + devices),
        out_specs=VMEM,
        scratch_shapes=[pltpu.VMEM((devices * row_count, width), jnp.float32)],
        compiler_params=limit(20),
        name="activate",
    )(resident, *held(code, *arrived))
    acts = exchange([act] * chips, "grp", PAIR)
    half_block = pltpu.VMEM((block, half), jnp.bfloat16)
    partials = pl.pallas_call(
        functools.partial(down_body, devices, chips),
        out_shape=[half_block] * devices,
        in_specs=[VMEM] * (4 + chips),
        out_specs=[VMEM] * devices,
        compiler_params=limit(12),
        name="down",
    )(*held(own_piece, other_piece, flags, spots, *acts))
    returned = exchange(partials, "exp", 1)
    placing = pl.pallas_call(
        functools.partial(place_body, chips, shards, row_count, block),
        out_shape=pltpu.VMEM((2 * E_WIN, chips * row_count, CODE), jnp.bfloat16),
        in_specs=[VMEM] * chips + [ANY],
        out_specs=VMEM,
        scratch_shapes=[pltpu.VMEM((chips * row_count, CODE), jnp.float32)],
        compiler_params=limit(2),
        name="place",
    )(*held(*acts, partials[0]))
    sums = pl.pallas_call(
        functools.partial(combine_body, devices, chips, shards),
        out_shape=[row_block] * chips,
        in_specs=[VMEM] * (1 + devices),
        out_specs=[VMEM] * chips,
        compiler_params=limit(8),
        name="combine",
    )(*held(placing, *returned))
    result = pl.pallas_call(
        finish_body,
        out_shape=jax.ShapeDtypeStruct((row_count, width), jnp.bfloat16),
        in_specs=[VMEM] * (1 + chips),
        out_specs=HBM,
        scratch_shapes=[
            pltpu.VMEM((row_count, width), jnp.bfloat16),
            pltpu.SemaphoreType.DMA((2,)),
        ],
        compiler_params=limit(2),
        name="finish",
    )(*held(weight_column, *exchange(sums, "grp", PAIR)))
    return result.reshape(1, row_count, width)


def per_device(hidden, norm_gain, route, route_weight, resident, sectioned, owner):
    weight_rows = BUCKETS * sectioned.shape[1]
    partial_rows = lax.axis_size("exp") * lax.axis_size("grp") // PAIR * hidden.shape[1]
    plan = move_rows if partial_rows < weight_rows else move_weights
    return plan(hidden, norm_gain, route, route_weight, resident, sectioned, owner)


def solution(mesh):
    in_specs = (
        P("grp", "exp", None),
        P(),
        P("grp", "exp", None),
        P("grp", "exp"),
        P(None, "exp", None),
        P("grp", "exp", None),
        P(),
    )
    out_specs = P("grp", "exp", None)
    return jax.shard_map(
        per_device, mesh=mesh, in_specs=in_specs, out_specs=out_specs, check_vma=False
    )
```
